256 devices in a mesh: shot: 8 (over y_lo, x), mp: 32 (over z, y_hi, core).
Axes of the slice: x: 4, y: 4 (y_hi: 2, y_lo: 2; y = y_hi * 2 + y_lo), z: 8, core: 2. Of those that a mesh axis runs over, the one named last changes fastest.
Arguments:
- courant: float32 [2, 512, 64, 256], P(None, 'mp'), may hold values from 0.05 to 0.2
- aperture_first: int32 [8], P('shot'), may hold values from 0 to 32
- source_pos: int32 [8, 3], P('shot'), may hold values from 0 to 511, as said below
- wavelet: float32 [8, 4], P('shot'), may hold values from -6 to 6
- receiver_pos: int32 [8, 32, 3], P('shot'), may hold values from 0 to 511, as said below
- residual: float32 [8, 4, 32], P('shot'), may hold values from -6 to 6
- step_count: int32 [8], P('shot'), may hold values from 2 to 4
- forward_prev: float32 [8, 512, 64, 256], P('shot', 'mp'), may hold values from -1 to 1
- forward_now: float32 [8, 512, 64, 256], P('shot', 'mp'), may hold values from -1 to 1
- adjoint_prev: float32 [8, 512, 64, 256], P('shot', 'mp'), may hold values from -1 to 1
- adjoint_now: float32 [8, 512, 64, 256], P('shot', 'mp'), may hold values from -1 to 1
Outputs:
- gradient: float32 [2, 512, 64, 256], P(None, 'mp', 'shot')
The draws below stay inside these ranges and needn't reach their ends.
Inputs may be any that keep to these rules, and one draw needn't show every extreme that they name: `source_pos`: each component lies inside the aperture grid: first in 0..511, second in 0..63, third in 0..255. `receiver_pos`: each component lies inside the aperture grid (first in 0..511, second in 0..63, third in 0..255), within 12 cells of the shot's source along every dimension. The aperture covers model tiles aperture_first .. aperture_first + 31.
All inputs are finite; a program needn't handle non-finite values.
Results may differ from the reference program's by a relative error of at most 0.0003.
Values sent between devices are 32-bit elements; how exact they have to be, the bound alone decides.
No kernel may reach another device: no remote copies, remote signals or barrier semaphores. Data moves between devices by JAX's collectives and lax.ppermute only.
A program may use at most 128 MiB of HBM per device.

```python
import math
import jax
import jax.numpy as jnp
from jax import lax

TX = 16
NY = 64
NZ = 256
SHOT_DEV = 1
RECV = 32
NT = 4
HALF = 512
SHOTS = 8
N_SHOT = 8
N_MP = 32


CIRCLE = 6.283185307179586


def corner_shot(key):
    return jax.random.randint(jax.random.fold_in(key, 5), (), 0, SHOTS)


def source_layout(key):
    first = jax.random.randint(jax.random.fold_in(key, 1), (SHOTS, 1), 0, HALF)
    second = jax.random.randint(jax.random.fold_in(key, 2), (SHOTS, 1), 0, NY)
    third = jax.random.randint(jax.random.fold_in(key, 3), (SHOTS, 1), 0, NZ)
    layout = jnp.concatenate([first, second, third], axis=1).astype(jnp.int32)
    corner = jnp.array([HALF - 1, NY - 1, NZ - 1], jnp.int32)
    return layout.at[corner_shot(key)].set(corner).astype(jnp.int32)


def draw_source_pos(key, part):
    return source_layout(jax.random.fold_in(key, 11))


def draw_receiver_pos(key, part):
    base = jax.random.fold_in(key, 11)
    source = source_layout(base)
    offsets = jax.random.randint(jax.random.fold_in(key, 23), (SHOTS, RECV, 3), -12, 13)
    offsets = offsets.at[corner_shot(base), 0].set(jnp.array([12, 12, 12], jnp.int32))
    limits = jnp.array([HALF - 1, NY - 1, NZ - 1], jnp.int32)
    placed = jnp.clip(source[:, None, :] + offsets, 0, limits[None, None, :])
    return placed.astype(jnp.int32)


def draw_step_count(key, part):
    counts = jax.random.randint(jax.random.fold_in(key, 31), (SHOTS,), NT // 2, NT + 1)
    chosen = jax.random.randint(jax.random.fold_in(key, 37), (), 0, SHOTS)
    return counts.at[chosen].set(NT).astype(jnp.int32)


def state_field(key, salt):
    base_key = jax.random.fold_in(key, salt)
    x_frac = (jnp.arange(HALF, dtype=jnp.float32)[None, :, None, None] + 0.5) / HALF
    y_frac = jnp.arange(NY, dtype=jnp.float32)[None, None, :, None] / NY
    z_frac = jnp.arange(NZ, dtype=jnp.float32)[None, None, None, :] / NZ
    freq = jax.random.randint(jax.random.fold_in(base_key, 2), (SHOTS, 3), 1, 4).astype(jnp.float32)
    phase = jax.random.uniform(jax.random.fold_in(base_key, 3), (SHOTS, 3), jnp.float32, -3.14159, 3.14159)
    wave_x = jnp.cos(CIRCLE * freq[:, 0][:, None, None, None] * x_frac + phase[:, 0][:, None, None, None])
    wave_y = jnp.cos(CIRCLE * freq[:, 1][:, None, None, None] * y_frac + phase[:, 1][:, None, None, None])
    wave_z = jnp.cos(CIRCLE * freq[:, 2][:, None, None, None] * z_frac + phase[:, 2][:, None, None, None])
    smooth = 0.08 * wave_x * wave_y * wave_z
    rough = 0.08 * jnp.clip(jax.random.normal(jax.random.fold_in(base_key, 1), (SHOTS, HALF, NY, NZ), jnp.float32), -5.0, 5.0)
    return (rough + smooth).astype(jnp.float32)


def draw_forward_prev(key, part):
    return state_field(key, 101)


def draw_forward_now(key, part):
    return state_field(key, 103)


def draw_adjoint_prev(key, part):
    return state_field(key, 107)


def draw_adjoint_now(key, part):
    return state_field(key, 109)


def with_ends(drawn, rng, least, high):
    place = [jax.random.randint(jax.random.fold_in(rng, axis), (), 0, length) for axis, length in enumerate(drawn.shape)]
    longest = drawn.shape.index(max(drawn.shape))
    next_to = place[:longest] + [(place[longest] + 1) % drawn.shape[longest]] + place[longest + 1:]
    return drawn.at[tuple(place)].set(least).at[tuple(next_to)].set(high)


def level_of(key, dims, split, low, high):
    gain = 1.0
    for dim, parts in split:
        heights = jax.random.uniform(jax.random.fold_in(jax.random.fold_in(key, 6), dim), (parts,), jnp.float32, low / len(split), high / len(split))
        gain = gain * jnp.repeat(jnp.exp(heights), dims[dim] // parts).reshape((-1,) + (1,) * (len(dims) - 1 - dim))
    return gain


def gaussian(stream_key, extent, deviation, bound, shards=(), kind=jnp.bfloat16):
    factor_of = level_of(stream_key, extent, shards, -0.22, 0.18) if shards else 1.0
    values = jax.random.normal(stream_key, extent, jnp.float32) * deviation * factor_of
    return jnp.minimum(jnp.maximum(values, -bound), bound).astype(kind)


def setup_inputs(seed: int = 0) -> dict:
    key_of = jax.random.split(jax.random.key(seed), 12)
    courant = jnp.clip(jnp.exp(math.log(0.2) - 1.3862944 * jax.random.uniform(key_of[0], (2, HALF, NY, NZ), jnp.float32) ** level_of(key_of[0], (2, HALF, NY, NZ), ((1, 32),), -0.2, 0.2)), 0.05, 0.2)
    aperture_first = with_ends(jax.random.randint(key_of[1], (N_SHOT,), 0, N_MP + 1), jax.random.fold_in(key_of[1], 1), 0, N_MP).astype(jnp.int32)
    source_pos = draw_source_pos(jax.random.fold_in(key_of[11], 71), 0)
    wavelet = gaussian(key_of[3], (SHOTS, NT), 1.0, 6.0, ((0, 8),), jnp.float32)
    receiver_pos = draw_receiver_pos(jax.random.fold_in(key_of[11], 71), 0)
    residual = gaussian(key_of[5], (SHOTS, NT, RECV), 1.0, 6.0, ((0, 8),), jnp.float32)
    step_count = draw_step_count(jax.random.fold_in(key_of[11], 71), 0)
    forward_prev = draw_forward_prev(jax.random.fold_in(key_of[11], 71), 0)
    forward_now = draw_forward_now(jax.random.fold_in(key_of[11], 71), 0)
    adjoint_prev = draw_adjoint_prev(jax.random.fold_in(key_of[11], 71), 0)
    adjoint_now = draw_adjoint_now(jax.random.fold_in(key_of[11], 71), 0)
    return dict(courant=courant, aperture_first=aperture_first, source_pos=source_pos, wavelet=wavelet, receiver_pos=receiver_pos, residual=residual, step_count=step_count, forward_prev=forward_prev, forward_now=forward_now, adjoint_prev=adjoint_prev, adjoint_now=adjoint_now)


COEF = (-205.0 / 72.0, 1.6, -0.2, 8.0 / 315.0, -1.0 / 560.0)


def laplace(field):
    xs, ys, zs = field.shape
    padded = jnp.pad(field, 4)
    total = 3.0 * COEF[0] * field
    for k in range(1, 5):
        total = total + COEF[k] * (padded[4 + k:4 + k + xs, 4:4 + ys, 4:4 + zs] + padded[4 - k:4 - k + xs, 4:4 + ys, 4:4 + zs])
        total = total + COEF[k] * (padded[4:4 + xs, 4 + k:4 + k + ys, 4:4 + zs] + padded[4:4 + xs, 4 - k:4 - k + ys, 4:4 + zs])
        total = total + COEF[k] * (padded[4:4 + xs, 4:4 + ys, 4 + k:4 + k + zs] + padded[4:4 + xs, 4:4 + ys, 4 - k:4 - k + zs])
    return total


def reference(courant, aperture_first, source_pos, wavelet, receiver_pos, residual, step_count, forward_prev, forward_now, adjoint_prev, adjoint_now):
    model = courant.reshape(2 * HALF, NY, NZ)
    zeros = jnp.zeros((HALF, NY, NZ), jnp.float32)

    def one_shot(grad, shot_index):
        group = shot_index // SHOT_DEV
        start = (aperture_first[group] * TX).astype(jnp.int32)
        speed = lax.dynamic_slice_in_dim(model, start, HALF, 0)
        source = source_pos[shot_index]
        receivers = receiver_pos[shot_index]
        count = step_count[shot_index]
        u_prev, u_now = forward_prev[shot_index], forward_now[shot_index]
        stored = []
        for n in range(NT):
            force = zeros.at[source[0], source[1], source[2]].add(wavelet[shot_index, n])
            drive = laplace(u_now) + force
            u_next = 2.0 * u_now - u_prev + speed * drive
            active = n < count
            stored.append(jnp.where(active, drive, 0.0))
            u_prev, u_now = jnp.where(active, u_now, u_prev), jnp.where(active, u_next, u_now)
        w_prev, w_now = adjoint_prev[shot_index], adjoint_now[shot_index]
        image = zeros
        for k in range(NT):
            n = NT - 1 - k
            inject = zeros.at[receivers[:, 0], receivers[:, 1], receivers[:, 2]].add(residual[shot_index, n])
            w_next = 2.0 * w_now - w_prev + speed * (laplace(w_now) + inject)
            active = n < count
            image = image + jnp.where(active, w_next * stored[n], 0.0)
            w_prev, w_now = jnp.where(active, w_now, w_prev), jnp.where(active, w_next, w_now)
        window = lax.dynamic_slice_in_dim(grad, start, HALF, 0)
        grad = lax.dynamic_update_slice_in_dim(grad, window + image, start, 0)
        return grad, None

    grad, unused = lax.scan(one_shot, jnp.zeros((2 * HALF, NY, NZ), jnp.float32), jnp.arange(SHOTS, dtype=jnp.int32))
    return grad.reshape(2, HALF, NY, NZ)
```

```python
import jax
import jax.numpy as jnp
from jax import lax
from jax.sharding import Mesh, PartitionSpec as P

COEF = (-205.0 / 72.0, 1.6, -0.2, 8.0 / 315.0, -1.0 / 560.0)
QUAD = 4
MP = ("zz", "quad")
PLANE = ("shot", "quad")


def shifted(value, axes, steps, wrap=False):
    count = lax.axis_size(axes)
    pairs = [(i, (i + steps) % count) for i in range(count) if wrap or 0 <= i + steps < count]
    return lax.ppermute(value, axes, pairs)


def all_first(first):
    shots = lax.axis_size("shot")
    me = lax.axis_index("shot")
    known = jnp.where(jnp.arange(shots, dtype=jnp.int32) == me, first, 0)
    step = 1
    while step < shots:
        known = known + lax.ppermute(known, "shot", [(i, i ^ step) for i in range(shots)])
        step *= 2
    return known


def quad_exchange(parts, axis):
    return lax.all_to_all(parts, "quad", split_axis=axis, concat_axis=axis, tiled=True)


def fetch_model(courant, firsts):
    rows, tile_x, ny, nz = courant.shape
    shots = lax.axis_size("shot")
    zs = lax.axis_size("zz")
    slab = ny // shots
    planes = tile_x // QUAD
    me_shot = lax.axis_index("shot")
    me_z = lax.axis_index("zz")
    mine = lax.dynamic_slice_in_dim(courant, me_shot * slab, slab, 2)
    block = quad_exchange(mine, 1).reshape(rows, QUAD, planes, slab, nz)
    line = [block[0]]
    for j in range(1, zs):
        line.append(shifted(jnp.where(me_z >= j, block[0], block[1]), "zz", -j, wrap=True))
    line.append(block[1])
    line = jnp.concatenate(line, axis=0)
    sent = [lax.dynamic_slice_in_dim(line, firsts[s], QUAD, 0) for s in range(shots)]
    sent = jnp.concatenate(sent, axis=0)
    got = lax.all_to_all(sent, PLANE, split_axis=0, concat_axis=0, tiled=True)
    got = got.reshape(shots, QUAD * planes, slab, nz)
    return got.transpose(1, 0, 2, 3).reshape(tile_x, ny, nz)


def return_image(image, firsts):
    tile_x, ny, nz = image.shape
    shots = lax.axis_size("shot")
    zs = lax.axis_size("zz")
    slab = ny // shots
    planes = tile_x // QUAD
    me_z = lax.axis_index("zz")
    sent = image.reshape(QUAD, planes, shots, slab, nz).transpose(2, 0, 1, 3, 4)
    sent = sent.reshape(shots * QUAD, planes, slab, nz)
    got = lax.all_to_all(sent, PLANE, split_axis=0, concat_axis=0, tiled=True)
    got = got.reshape(shots, QUAD, planes, slab, nz)
    line = jnp.zeros(((zs + 1) * QUAD, planes, slab, nz), jnp.float32)
    for s in range(shots):
        old = lax.dynamic_slice_in_dim(line, firsts[s], QUAD, 0)
        line = lax.dynamic_update_slice_in_dim(line, old + got[s], firsts[s], 0)
    line = line.reshape(zs + 1, QUAD, planes, slab, nz)
    low, high = line[0], line[zs]
    for j in range(1, zs):
        came = shifted(line[j], "zz", j, wrap=True)
        low = low + jnp.where(me_z >= j, came, 0.0)
        high = high + jnp.where(me_z >= j, 0.0, came)
    both = jnp.stack([low, high]).reshape(2, tile_x, slab, nz)
    return quad_exchange(both, 1)


def laplace_core(padded, width):
    ys = padded.shape[1]
    zs = padded.shape[2]
    centre = padded[4 : 4 + width]
    side = jnp.pad(centre, ((0, 0), (4, 4), (4, 4)))
    total = 3.0 * COEF[0] * centre
    for k in range(1, 5):
        total = total + COEF[k] * (padded[4 + k : 4 + k + width] + padded[4 - k : 4 - k + width])
        total = total + COEF[k] * (
            side[:, 4 + k : 4 + k + ys, 4 : 4 + zs] + side[:, 4 - k : 4 - k + ys, 4 : 4 + zs]
        )
        total = total + COEF[k] * (
            side[:, 4 : 4 + ys, 4 + k : 4 + k + zs] + side[:, 4 : 4 + ys, 4 - k : 4 - k + zs]
        )
    return total


def body(
    courant,
    aperture_first,
    source_pos,
    wavelet,
    receiver_pos,
    residual,
    step_count,
    forward_prev,
    forward_now,
    adjoint_prev,
    adjoint_now,
):
    tile_x = courant.shape[1]
    ny_cells = courant.shape[2]
    nz_cells = courant.shape[3]
    me_index = lax.axis_index(MP)
    firsts = all_first(aperture_first[0])
    owned = fetch_model(courant, firsts)
    steps = wavelet.shape[1]
    count = step_count[0]
    u_prev, u_now = (forward_prev[0], forward_now[0])
    w_prev, w_now = (adjoint_prev[0], adjoint_now[0])
    x_cells = jnp.arange(tile_x, dtype=jnp.int32) + me_index * tile_x
    y_cells = jnp.arange(ny_cells, dtype=jnp.int32)
    z_cells = jnp.arange(nz_cells, dtype=jnp.int32)
    src_x = (x_cells == source_pos[0, 0]).astype(jnp.float32)
    src_y = (y_cells == source_pos[0, 1]).astype(jnp.float32)
    src_z = (z_cells == source_pos[0, 2]).astype(jnp.float32)
    src_field = src_x[:, None, None] * (src_y[:, None] * src_z[None, :])[None]
    rec = receiver_pos[0]
    rec_x = (x_cells[None, :] == rec[:, 0:1]).astype(jnp.float32)
    rec_y = (y_cells[None, :] == rec[:, 1:2]).astype(jnp.float32)
    rec_z = (z_cells[None, :] == rec[:, 2:3]).astype(jnp.float32)
    rec_plane = rec_y[:, :, None] * rec_z[:, None, :]
    drives = []
    image = jnp.zeros((tile_x, ny_cells, nz_cells), jnp.float32)
    adjoint = []
    for n in range(steps):
        k = steps - 1 - n
        before = shifted(jnp.concatenate([u_now[-4:], w_now[-4:]]), MP, 1)
        after = shifted(jnp.concatenate([u_now[:4], w_now[:4]]), MP, -1)
        lap_u = laplace_core(jnp.concatenate([before[:4], u_now, after[:4]]), tile_x)
        lap_w = laplace_core(jnp.concatenate([before[4:], w_now, after[4:]]), tile_x)
        drive = lap_u + wavelet[0, n] * src_field
        u_next = 2.0 * u_now - u_prev + owned * drive
        drives.append(jnp.where(n < count, drive, 0.0))
        u_prev, u_now = jnp.where(n < count, u_now, u_prev), jnp.where(n < count, u_next, u_now)
        weighted = rec_x * residual[0, k][:, None]
        inject = jnp.einsum("rx,ryz->xyz", weighted, rec_plane, precision=lax.Precision.HIGHEST)
        w_next = 2.0 * w_now - w_prev + owned * (lap_w + inject)
        adjoint.append(w_next)
        w_prev, w_now = jnp.where(k < count, w_now, w_prev), jnp.where(k < count, w_next, w_now)
    for k in range(steps):
        n = steps - 1 - k
        image = image + jnp.where(n < count, adjoint[k] * drives[n], 0.0)
    return return_image(image, firsts)


def solution(mesh):
    shots, mp = mesh.devices.shape
    fine = Mesh(mesh.devices.reshape(shots, mp // QUAD, QUAD), ("shot", "zz", "quad"))
    return jax.shard_map(
        body,
        mesh=fine,
        in_specs=(
            P(None, MP, None, None),
            P("shot"),
            P("shot", None),
            P("shot", None),
            P("shot", None, None),
            P("shot", None, None),
            P("shot"),
            P("shot", MP, None, None),
            P("shot", MP, None, None),
            P("shot", MP, None, None),
            P("shot", MP, None, None),
        ),
        out_specs=P(None, MP, "shot", None),
        check_vma=False,
    )
```

```python
import functools

import jax
import jax.numpy as jnp
from jax import lax
from jax.experimental import pallas as pl
from jax.experimental.pallas import tpu as pltpu
from jax.sharding import Mesh, PartitionSpec as P

COEF = (-205.0 / 72.0, 1.6, -0.2, 8.0 / 315.0, -1.0 / 560.0)
QUAD = 4
MP = ("zz", "quad")
PLANE = ("shot", "quad")
LANES = 128
SUB = 8
REACH = 4
COUNT, BASE, SOURCE, RECEIVERS = 0, 1, 2, 5
VMEM_LIMIT = 24 << 20


def shifted(value, axes, steps):
    count = lax.axis_size(axes)
    pairs = [(i, i + steps) for i in range(count) if 0 <= i + steps < count]
    return lax.ppermute(value, axes, pairs)


def all_first(first):
    shots = lax.axis_size("shot")
    me = lax.axis_index("shot")
    known = jnp.where(jnp.arange(shots, dtype=jnp.int32) == me, first, 0)
    step = 1
    while step < shots:
        known = known + lax.ppermute(known, "shot", [(i, i ^ step) for i in range(shots)])
        step *= 2
    return known


def f32(*shape):
    return jax.ShapeDtypeStruct(shape, jnp.float32)


def local_kernel(body, name, scalars, arrays, outs, scratch=()):
    vmem = pl.BlockSpec(memory_space=pltpu.VMEM)
    smem = pl.BlockSpec(memory_space=pltpu.SMEM)
    return pl.pallas_call(
        body,
        out_shape=outs,
        in_specs=[smem] * len(scalars) + [vmem] * len(arrays),
        out_specs=[vmem] * len(outs),
        scratch_shapes=list(scratch),
        compiler_params=pltpu.CompilerParams(vmem_limit_bytes=VMEM_LIMIT),
        name=name,
    )(*scalars, *arrays)


def band_matrix(nz):
    rows = lax.broadcasted_iota(jnp.int32, (nz, nz), 0)
    cols = lax.broadcasted_iota(jnp.int32, (nz, nz), 1)
    apart = jnp.abs(rows - cols)
    band = jnp.where(apart == 0, 3.0 * COEF[0], 0.0)
    for k in range(1, REACH + 1):
        band = jnp.where(apart == k, COEF[k], band)
    return band


def prepare(field, padded, along_z):
    xs, ys, nz = field.shape
    along_z[...] = jnp.dot(
        field[...].reshape(xs * ys, nz),
        band_matrix(nz),
        precision=lax.Precision.HIGHEST,
        preferred_element_type=jnp.float32,
    ).reshape(xs, ys, nz)
    edge = jnp.zeros((xs, SUB, LANES), jnp.float32)
    for h in range(nz // LANES):
        padded[h, :, 0:SUB, :] = edge
        padded[h, :, SUB + ys : SUB + ys + SUB, :] = edge
        padded[h, :, SUB : SUB + ys, :] = field[:, :, h * LANES : (h + 1) * LANES]


def add_point(target, x, y, z, amount):
    xs, _, nz = target.shape

    @pl.when((x >= 0) & (x < xs))
    def _():
        cells = lax.broadcasted_iota(jnp.int32, (1, 1, nz), 2)
        place = (pl.ds(x, 1), pl.ds(y, 1), slice(None))
        target[place] = target[place] + jnp.where(cells == z, amount, 0.0)


def add_source(target, ints, floats, n):
    x = ints[SOURCE] - ints[BASE]
    add_point(target, x, ints[SOURCE + 1], ints[SOURCE + 2], floats[n])


def add_receivers(target, ints, floats, steps, receivers, n):
    def one(j, carry):
        at = RECEIVERS + 3 * j
        amount = floats[steps + n * receivers + j]
        add_point(target, ints[at] - ints[BASE], ints[at + 1], ints[at + 2], amount)
        return carry

    lax.fori_loop(0, receivers, one, 0)


def laplacian(padded, along_z, before, after, plane, y0, h):
    xs = along_z.shape[0]
    rows = pl.ds(y0, SUB)
    lanes = slice(h * LANES, (h + 1) * LANES)
    column = [before[plane + j, rows, lanes] for j in range(REACH)]
    column += [padded[h, x, pl.ds(y0 + SUB, SUB), :] for x in range(xs)]
    column += [after[plane + j, rows, lanes] for j in range(REACH)]
    for x in range(xs):
        total = along_z[x, rows, lanes]
        for k in range(1, REACH + 1):
            pair = column[x + REACH + k] + column[x + REACH - k]
            pair = pair + (
                padded[h, x, pl.ds(y0 + SUB + k, SUB), :]
                + padded[h, x, pl.ds(y0 + SUB - k, SUB), :]
            )
            total = total + COEF[k] * pair
        yield x, column[x + REACH], total


def each_block(field, work):
    _, ys, nz = field.shape

    def step(i, carry):
        y0 = pl.multiple_of(i * SUB, SUB)
        for h in range(nz // LANES):
            work(i, y0, h, slice(h * LANES, (h + 1) * LANES))
        return carry

    lax.fori_loop(0, ys // SUB, step, 0)


def switch_on(ints, n):
    return jnp.where(ints[COUNT] > n, 1.0, 0.0).astype(jnp.float32)


def first_kernel(dims, ints, floats, u, w, before, after, d, e, pad_u, pad_w):
    steps, receivers = dims
    prepare(u, pad_u, d)
    prepare(w, pad_w, e)
    add_source(d, ints, floats, 0)
    add_receivers(e, ints, floats, steps, receivers, steps - 1)
    live = switch_on(ints, 0)

    def work(i, y0, h, lanes):
        rows = pl.ds(y0, SUB)
        for x, _, total in laplacian(pad_u, d, before, after, 0, y0, h):
            d[x, rows, lanes] = live * total
        for x, _, total in laplacian(pad_w, e, before, after, REACH, y0, h):
            e[x, rows, lanes] = total

    each_block(u, work)


def send_planes(low, high, plane, x, xs, rows, lanes, value):
    if x < REACH:
        low[plane + x, rows, lanes] = value
    if x >= xs - REACH:
        high[plane + x - (xs - REACH), rows, lanes] = value


def advance_kernel(dims, ints, u, ub, d, w, wb, e, p, u1, vu1, w1, vw1, low, high):
    steps, _ = dims
    xs = u.shape[0]
    live = switch_on(ints, steps - 1)

    def work(i, y0, h, lanes):
        rows = pl.ds(y0, SUB)
        for x in range(xs):
            speed = p[i, x, :, lanes]
            now = u[x, rows, lanes]
            gain = (now - ub[x, rows, lanes]) + speed * d[x, rows, lanes]
            vu1[x, rows, lanes] = gain
            now = now + gain
            u1[x, rows, lanes] = now
            send_planes(low, high, 0, x, xs, rows, lanes, now)
            now = w[x, rows, lanes]
            gain = (now - wb[x, rows, lanes]) + (live * speed) * e[x, rows, lanes]
            vw1[x, rows, lanes] = gain
            now = now + live * gain
            w1[x, rows, lanes] = now
            send_planes(low, high, REACH, x, xs, rows, lanes, now)

    each_block(u, work)


def round_kernel(dims, n, ints, floats, u, vu, w, vw, p, before, after, *rest):
    steps, receivers = dims
    last = n == steps - 1
    image_round = n == steps - 2
    if last:
        partial, d_first, w_first, image, pad_u, pad_w, z_u, z_w = rest
    elif image_round:
        d_before, d_out, u1, vu1, w1, vw1, low, high, pad_u, pad_w, z_u, z_w = rest
    else:
        d_out, u1, vu1, w1, vw1, low, high, pad_u, pad_w, z_u, z_w = rest
    xs = u.shape[0]
    back = steps - 1 - n
    prepare(u, pad_u, z_u)
    prepare(w, pad_w, z_w)
    add_source(z_u, ints, floats, n)
    add_receivers(z_w, ints, floats, steps, receivers, back)
    live = switch_on(ints, n)
    live_back = switch_on(ints, back)

    def work(i, y0, h, lanes):
        rows = pl.ds(y0, SUB)
        for x, now, total in laplacian(pad_u, z_u, before, after, 0, y0, h):
            drive = live * total
            if last:
                image[i, x, :, lanes] = partial[x, rows, lanes] + w_first[x, rows, lanes] * drive
                continue
            if image_round:
                d_out[x, rows, lanes] = drive * w[x, rows, lanes]
            else:
                d_out[x, rows, lanes] = drive
            gain = vu[x, rows, lanes] + p[i, x, :, lanes] * drive
            vu1[x, rows, lanes] = gain
            now = now + gain
            u1[x, rows, lanes] = now
            send_planes(low, high, 0, x, xs, rows, lanes, now)
        for x, now, total in laplacian(pad_w, z_w, before, after, REACH, y0, h):
            gain = vw[x, rows, lanes] + (live_back * p[i, x, :, lanes]) * total
            now = now + live_back * gain
            if last:
                image[i, x, :, lanes] = image[i, x, :, lanes] + now * d_first[x, rows, lanes]
                continue
            if image_round:
                d_out[x, rows, lanes] = d_out[x, rows, lanes] + now * d_before[x, rows, lanes]
            vw1[x, rows, lanes] = gain
            w1[x, rows, lanes] = now
            send_planes(low, high, REACH, x, xs, rows, lanes, now)

    each_block(u, work)


def gather_kernel(zs, firsts, line, extra, sent):
    me_z = firsts[sent.shape[0] // QUAD]

    def one(slot, carry):
        tile = firsts[slot // QUAD] + slot % QUAD
        place = ((me_z + tile // QUAD) % zs) * QUAD + tile % QUAD

        @pl.when(tile < zs * QUAD)
        def _():
            sent[slot] = line[place]

        @pl.when(tile >= zs * QUAD)
        def _():
            sent[slot] = extra[tile % QUAD]

        return carry

    lax.fori_loop(0, sent.shape[0], one, 0)


def scatter_kernel(zs, firsts, got, line, extra):
    me_z = firsts[got.shape[0] // QUAD]
    line[...] = jnp.zeros_like(line)
    extra[...] = jnp.zeros_like(extra)

    def one(slot, carry):
        tile = firsts[slot // QUAD] + slot % QUAD
        place = ((me_z + tile // QUAD) % zs) * QUAD + tile % QUAD

        @pl.when(tile < zs * QUAD)
        def _():
            line[place] = line[place] + got[slot]

        @pl.when(tile >= zs * QUAD)
        def _():
            extra[tile % QUAD] = extra[tile % QUAD] + got[slot]

        return carry

    lax.fori_loop(0, got.shape[0], one, 0)


def finish_kernel(zs, where, came, extra, out):
    planes = came.shape[1]
    me_z = where[0]
    for q in range(QUAD):
        low = came[q]
        high = extra[q]
        for z in range(1, zs):
            value = came[z * QUAD + q]
            low = low + jnp.where(z <= me_z, value, 0.0)
            high = high + jnp.where(z <= me_z, 0.0, value)
        out[0, q * planes : (q + 1) * planes] = low
        out[1, q * planes : (q + 1) * planes] = high


def exchange(parts, axes):
    return lax.all_to_all(parts, axes, split_axis=0, concat_axis=0, tiled=True)


def fetch_model(courant, table):
    _, tile_x, ny, nz = courant.shape
    shots = lax.axis_size("shot")
    zs = lax.axis_size("zz")
    slab = ny // shots
    planes = tile_x // QUAD
    me_z = lax.axis_index("zz")
    mine = lax.dynamic_slice_in_dim(courant, lax.axis_index("shot") * slab, slab, 2)
    near = (jnp.arange(zs) <= me_z)[:, None, None, None]
    parts = jnp.where(near, mine[0][None], mine[1][None])
    line = exchange(parts.reshape(zs * QUAD, planes, slab, nz), MP)
    extra = exchange(mine[1].reshape(QUAD, planes, slab, nz), "quad")
    (sent,) = local_kernel(
        functools.partial(gather_kernel, zs),
        "gather",
        [table],
        [line, extra],
        [f32(shots * QUAD, planes, slab, nz)],
    )
    return exchange(sent, PLANE).reshape(shots, tile_x, slab, nz)


def return_image(image, table, here):
    shots, tile_x, slab, nz = image.shape
    zs = lax.axis_size("zz")
    planes = tile_x // QUAD
    got = exchange(image.reshape(shots * QUAD, planes, slab, nz), PLANE)
    line, extra = local_kernel(
        functools.partial(scatter_kernel, zs),
        "scatter",
        [table],
        [got],
        [f32(zs * QUAD, planes, slab, nz), f32(QUAD, planes, slab, nz)],
    )
    came = exchange(line, MP)
    came_extra = exchange(extra, "quad")
    (out,) = local_kernel(
        functools.partial(finish_kernel, zs),
        "finish",
        [here],
        [came, came_extra],
        [f32(2, tile_x, slab, nz)],
    )
    return out


def body(
    courant,
    aperture_first,
    source_pos,
    wavelet,
    receiver_pos,
    residual,
    step_count,
    forward_prev,
    forward_now,
    adjoint_prev,
    adjoint_now,
):
    tile_x, ny, nz = forward_now.shape[1:]
    steps = wavelet.shape[1]
    receivers = receiver_pos.shape[1]
    dims = (steps, receivers)
    here = lax.axis_index("zz").reshape(1).astype(jnp.int32)
    table = jnp.concatenate([all_first(aperture_first[0]), here])
    base = (lax.axis_index(MP) * tile_x).reshape(1).astype(jnp.int32)
    ints = jnp.concatenate([step_count, base, source_pos[0], receiver_pos[0].reshape(-1)])
    floats = jnp.concatenate([wavelet[0], residual[0].reshape(-1)])
    u, w = forward_now[0], adjoint_now[0]
    low = jnp.concatenate([u[:REACH], w[:REACH]])
    high = jnp.concatenate([u[tile_x - REACH :], w[tile_x - REACH :]])
    before, after = shifted(high, MP, 1), shifted(low, MP, -1)
    field = f32(tile_x, ny, nz)
    edge = f32(2 * REACH, ny, nz)
    padded = pltpu.VMEM((nz // LANES, tile_x, ny + 2 * SUB, LANES), jnp.float32)
    work = pltpu.VMEM((tile_x, ny, nz), jnp.float32)
    drive, push = local_kernel(
        functools.partial(first_kernel, dims),
        "first",
        [ints, floats],
        [u, w, before, after],
        [field, field],
        [padded, padded],
    )
    owned = fetch_model(courant, table)
    d_first = drive
    u, vu, w, vw, low, high = local_kernel(
        functools.partial(advance_kernel, dims),
        "advance",
        [ints],
        [u, forward_prev[0], drive, w, adjoint_prev[0], push, owned],
        [field, field, field, field, edge, edge],
    )
    w_first = w
    d_before = None
    for n in range(1, steps):
        before, after = shifted(high, MP, 1), shifted(low, MP, -1)
        arrays = [u, vu, w, vw, owned, before, after]
        if n == steps - 1:
            (image,) = local_kernel(
                functools.partial(round_kernel, dims, n),
                "last",
                [ints, floats],
                arrays + [d_before, d_first, w_first],
                [f32(ny // SUB, tile_x, SUB, nz)],
                [padded, padded, work, work],
            )
            break
        if n == steps - 2:
            arrays = arrays + [d_before]
        d_before, u, vu, w, vw, low, high = local_kernel(
            functools.partial(round_kernel, dims, n),
            "round",
            [ints, floats],
            arrays,
            [field, field, field, field, field, edge, edge],
            [padded, padded, work, work],
        )
    return return_image(image, table, here)


def solution(mesh):
    shots, mp = mesh.devices.shape
    fine = Mesh(mesh.devices.reshape(shots, mp // QUAD, QUAD), ("shot", "zz", "quad"))
    return jax.shard_map(
        body,
        mesh=fine,
        in_specs=(
            P(None, MP, None, None),
            P("shot"),
            P("shot", None),
            P("shot", None),
            P("shot", None, None),
            P("shot", None, None),
            P("shot"),
            P("shot", MP, None, None),
            P("shot", MP, None, None),
            P("shot", MP, None, None),
            P("shot", MP, None, None),
        ),
        out_specs=P(None, MP, "shot", None),
        check_vma=False,
    )
```

```python
import functools

import jax
import jax.numpy as jnp
from jax import lax
from jax.experimental import pallas as pl
from jax.experimental.pallas import tpu as pltpu
from jax.sharding import Mesh, PartitionSpec as P

COEF = (-205.0 / 72.0, 1.6, -0.2, 8.0 / 315.0, -1.0 / 560.0)
QUAD = 4
MP = ("zz", "quad")
PLANE = ("shot", "quad")
LANES = 128
SUB = 8
REACH = 4
COUNT, BASE, SOURCE, RECEIVERS = 0, 1, 2, 5
VMEM_LIMIT = 16 << 20


def shifted(value, axes, steps):
    count = lax.axis_size(axes)
    pairs = [(i, i + steps) for i in range(count) if 0 <= i + steps < count]
    return lax.ppermute(value, axes, pairs)


def all_first(first):
    shots = lax.axis_size("shot")
    me = lax.axis_index("shot")
    known = jnp.where(jnp.arange(shots, dtype=jnp.int32) == me, first, 0)
    step = 1
    while step < shots:
        known = known + lax.ppermute(known, "shot", [(i, i ^ step) for i in range(shots)])
        step *= 2
    return known


def f32(*shape):
    return jax.ShapeDtypeStruct(shape, jnp.float32)


def local_kernel(body, name, scalars, arrays, outs, scratch=()):
    vmem = pl.BlockSpec(memory_space=pltpu.VMEM)
    smem = pl.BlockSpec(memory_space=pltpu.SMEM)
    return pl.pallas_call(
        body,
        out_shape=outs,
        in_specs=[smem] * len(scalars) + [vmem] * len(arrays),
        out_specs=[vmem] * len(outs),
        scratch_shapes=list(scratch),
        compiler_params=pltpu.CompilerParams(vmem_limit_bytes=VMEM_LIMIT),
        name=name,
    )(*scalars, *arrays)


def in_hbm(value):
    return pltpu.with_memory_space_constraint(value, pltpu.HBM)


def band_matrix(nz):
    rows = lax.broadcasted_iota(jnp.int32, (nz, nz), 0)
    cols = lax.broadcasted_iota(jnp.int32, (nz, nz), 1)
    apart = jnp.abs(rows - cols)
    band = jnp.where(apart == 0, 3.0 * COEF[0], 0.0)
    for k in range(1, REACH + 1):
        band = jnp.where(apart == k, COEF[k], band)
    return band


def prepare(field, padded, along_z):
    xs, ys, nz = field.shape
    along_z[...] = jnp.dot(
        field[...].reshape(xs * ys, nz),
        band_matrix(nz),
        precision=lax.Precision.HIGHEST,
        preferred_element_type=jnp.float32,
    ).reshape(xs, ys, nz)
    edge = jnp.zeros((xs, SUB, LANES), jnp.float32)
    for h in range(nz // LANES):
        padded[h, :, 0:SUB, :] = edge
        padded[h, :, SUB + ys : SUB + ys + SUB, :] = edge
        padded[h, :, SUB : SUB + ys, :] = field[:, :, h * LANES : (h + 1) * LANES]


def add_point(target, x, y, z, amount):
    xs, _, nz = target.shape

    @pl.when((x >= 0) & (x < xs))
    def _():
        cells = lax.broadcasted_iota(jnp.int32, (1, 1, nz), 2)
        place = (pl.ds(x, 1), pl.ds(y, 1), slice(None))
        target[place] = target[place] + jnp.where(cells == z, amount, 0.0)


def add_source(target, ints, floats, n):
    x = ints[SOURCE] - ints[BASE]
    add_point(target, x, ints[SOURCE + 1], ints[SOURCE + 2], floats[n])


def add_receivers(target, ints, floats, steps, receivers, n):
    def one(j, carry):
        at = RECEIVERS + 3 * j
        amount = floats[steps + n * receivers + j]
        add_point(target, ints[at] - ints[BASE], ints[at + 1], ints[at + 2], amount)
        return carry

    lax.fori_loop(0, receivers, one, 0)


def laplacian(padded, along_z, before, after, y0, h):
    xs = along_z.shape[0]
    rows = pl.ds(y0, SUB)
    lanes = slice(h * LANES, (h + 1) * LANES)
    column = [before[j, rows, lanes] for j in range(REACH)]
    column += [padded[h, x, pl.ds(y0 + SUB, SUB), :] for x in range(xs)]
    column += [after[j, rows, lanes] for j in range(REACH)]
    for x in range(xs):
        total = along_z[x, rows, lanes]
        for k in range(1, REACH + 1):
            pair = column[x + REACH + k] + column[x + REACH - k]
            pair = pair + (
                padded[h, x, pl.ds(y0 + SUB + k, SUB), :]
                + padded[h, x, pl.ds(y0 + SUB - k, SUB), :]
            )
            total = total + COEF[k] * pair
        yield x, column[x + REACH], total


def each_block(field, work):
    _, ys, nz = field.shape

    def step(i, carry):
        y0 = pl.multiple_of(i * SUB, SUB)
        for h in range(nz // LANES):
            work(i, y0, h, slice(h * LANES, (h + 1) * LANES))
        return carry

    lax.fori_loop(0, ys // SUB, step, 0)


def switch_on(ints, n):
    return jnp.where(ints[COUNT] > n, 1.0, 0.0).astype(jnp.float32)


def first_kernel(steps, receivers, kind, ints, floats, field, before, after, out, pad):
    prepare(field, pad, out)
    if kind == "forward":
        add_source(out, ints, floats, 0)
        live = switch_on(ints, 0)
    else:
        add_receivers(out, ints, floats, steps, receivers, steps - 1)
        live = switch_on(ints, steps - 1)

    def work(i, y0, h, lanes):
        rows = pl.ds(y0, SUB)
        for x, _, total in laplacian(pad, out, before, after, y0, h):
            out[x, rows, lanes] = live * total

    each_block(field, work)


def send_planes(low, high, x, xs, rows, lanes, value):
    if x < REACH:
        low[x, rows, lanes] = value
    if x >= xs - REACH:
        high[x - (xs - REACH), rows, lanes] = value


def advance_kernel(n, ints, now, back, drive, speed, new, gain, low, high):
    xs = now.shape[0]
    live = switch_on(ints, n)

    def work(i, y0, h, lanes):
        rows = pl.ds(y0, SUB)
        for x in range(xs):
            here = now[x, rows, lanes]
            more = (here - back[x, rows, lanes]) + speed[i, x, :, lanes] * drive[x, rows, lanes]
            gain[x, rows, lanes] = more
            here = here + live * more
            new[x, rows, lanes] = here
            send_planes(low, high, x, xs, rows, lanes, here)

    each_block(now, work)


def forward_kernel(n, last, ints, floats, u, vu, p, before, after, drive, *rest):
    if last:
        pad, along = rest
    else:
        new, gain, low, high, pad, along = rest
    xs = u.shape[0]
    prepare(u, pad, along)
    add_source(along, ints, floats, n)
    live = switch_on(ints, n)

    def work(i, y0, h, lanes):
        rows = pl.ds(y0, SUB)
        for x, here, total in laplacian(pad, along, before, after, y0, h):
            total = live * total
            drive[x, rows, lanes] = total
            if last:
                continue
            more = vu[x, rows, lanes] + p[i, x, :, lanes] * total
            gain[x, rows, lanes] = more
            here = here + more
            new[x, rows, lanes] = here
            send_planes(low, high, x, xs, rows, lanes, here)

    each_block(u, work)


def adjoint_kernel(steps, receivers, n, last, ints, floats, w, vw, p, before, after, *rest):
    if last:
        partial, drive, image, pad, along = rest
    else:
        new, gain, low, high, pad, along = rest
    xs = w.shape[0]
    prepare(w, pad, along)
    add_receivers(along, ints, floats, steps, receivers, n)
    live = switch_on(ints, n)

    def work(i, y0, h, lanes):
        rows = pl.ds(y0, SUB)
        for x, here, total in laplacian(pad, along, before, after, y0, h):
            more = vw[x, rows, lanes] + (live * p[i, x, :, lanes]) * total
            here = here + live * more
            if last:
                image[i, x, :, lanes] = partial[x, rows, lanes] + here * drive[x, rows, lanes]
                continue
            gain[x, rows, lanes] = more
            new[x, rows, lanes] = here
            send_planes(low, high, x, xs, rows, lanes, here)

    each_block(w, work)


def products_kernel(pairs, *refs):
    out = refs[-1]

    def work(i, y0, h, lanes):
        rows = pl.ds(y0, SUB)
        for x in range(out.shape[0]):
            total = refs[0][x, rows, lanes] * refs[1][x, rows, lanes]
            for j in range(1, pairs):
                total = total + refs[2 * j][x, rows, lanes] * refs[2 * j + 1][x, rows, lanes]
            out[x, rows, lanes] = total

    each_block(out, work)


def split_kernel(spot, courant, parts, *rest):
    extras, sems = rest[:QUAD], rest[QUAD]
    zs = parts.shape[0]
    _, planes, slab, _ = extras[0].shape
    me_shot, me_z, me_q = spot[0], spot[1], spot[2]
    rows = pl.ds(pl.multiple_of(me_shot * slab, SUB), slab)
    copies = []
    for z in range(zs):
        row = jnp.where(z <= me_z, 0, 1)
        copies.append(
            pltpu.make_async_copy(courant.at[row, :, rows, :], parts.at[z], sems.at[z])
        )
    for r in range(QUAD):
        to = ((me_q + r) % QUAD) * planes
        copies.append(
            pltpu.make_async_copy(
                courant.at[1, pl.ds(to, planes), rows, :], extras[r].at[0], sems.at[zs + r]
            )
        )
    for copy in copies:
        copy.start()
    for copy in copies:
        copy.wait()


def gather_kernel(zs, table, spot, line, *rest):
    extras, sent, sems = rest[:QUAD], rest[QUAD], rest[QUAD + 1]
    slots = sent.shape[0]
    me_z, me_q = spot[1], spot[2]
    for slot in range(slots):
        tile = table[slot // QUAD] + slot % QUAD
        place = ((me_z + tile // QUAD) % zs) * QUAD + tile % QUAD
        turn = (me_q + QUAD - tile % QUAD) % QUAD
        near = tile < zs * QUAD

        @pl.when(near)
        def _():
            pltpu.make_async_copy(line.at[place], sent.at[slot], sems.at[slot]).start()

        for r in range(QUAD):

            @pl.when(jnp.logical_not(near) & (turn == r))
            def _():
                pltpu.make_async_copy(extras[r].at[0], sent.at[slot], sems.at[slot]).start()

    for slot in range(slots):
        pltpu.make_async_copy(line.at[0], sent.at[slot], sems.at[slot]).wait()


def scatter_kernel(zs, table, spot, got, line, *rest):
    extras, held = rest[:QUAD], rest[QUAD]
    me_z, me_q = spot[1], spot[2]
    line[...] = jnp.zeros_like(line)
    held[...] = jnp.zeros_like(held)

    def one(slot, carry):
        tile = table[slot // QUAD] + slot % QUAD
        place = ((me_z + tile // QUAD) % zs) * QUAD + tile % QUAD
        turn = (tile % QUAD + QUAD - me_q) % QUAD

        @pl.when(tile < zs * QUAD)
        def _():
            line[place] = line[place] + got[slot]

        @pl.when(tile >= zs * QUAD)
        def _():
            held[turn] = held[turn] + got[slot]

        return carry

    lax.fori_loop(0, got.shape[0], one, 0)
    for r in range(QUAD):
        extras[r][0] = held[r]


def finish_kernel(zs, spot, came, *rest):
    extras, out = rest[:QUAD], rest[QUAD]
    planes = came.shape[1]
    me_z, me_q = spot[1], spot[2]
    for r in range(QUAD):
        q = (me_q + QUAD - r) % QUAD
        low = came[q]
        high = extras[r][0]
        for z in range(1, zs):
            value = came[z * QUAD + q]
            low = low + jnp.where(z <= me_z, value, 0.0)
            high = high + jnp.where(z <= me_z, 0.0, value)
        out[0, pl.ds(q * planes, planes)] = low
        out[1, pl.ds(q * planes, planes)] = high


def exchange(parts, axes):
    return lax.all_to_all(parts, axes, split_axis=0, concat_axis=0, tiled=True)


def quad_turn(extras):
    turned = [extras[0]]
    for r in range(1, QUAD):
        pairs = [(q, (q + r) % QUAD) for q in range(QUAD)]
        turned.append(lax.ppermute(extras[r], "quad", pairs))
    return turned


def model_line(courant, spot):
    _, tile_x, ny, nz = courant.shape
    zs = lax.axis_size("zz")
    slab = ny // lax.axis_size("shot")
    planes = tile_x // QUAD
    hbm = pl.BlockSpec(memory_space=pltpu.HBM)
    parts, *extras = pl.pallas_call(
        split_kernel,
        out_shape=[f32(zs, tile_x, slab, nz)] + [f32(1, planes, slab, nz)] * QUAD,
        in_specs=[pl.BlockSpec(memory_space=pltpu.SMEM), hbm],
        out_specs=[hbm] * (1 + QUAD),
        scratch_shapes=[pltpu.SemaphoreType.DMA((zs + QUAD,))],
        compiler_params=pltpu.CompilerParams(vmem_limit_bytes=1 << 20),
        name="split",
    )(spot, in_hbm(courant))
    line = exchange(parts.reshape(zs * QUAD, planes, slab, nz), MP)
    return line, quad_turn(extras)


def model_parts(line, extras, table, spot):
    slots = lax.axis_size("shot") * QUAD
    smem = pl.BlockSpec(memory_space=pltpu.SMEM)
    anywhere = pl.BlockSpec(memory_space=pl.ANY)
    return pl.pallas_call(
        functools.partial(gather_kernel, lax.axis_size("zz")),
        out_shape=f32(slots, *line.shape[1:]),
        in_specs=[smem, smem] + [anywhere] * (1 + QUAD),
        out_specs=pl.BlockSpec(memory_space=pltpu.HBM),
        scratch_shapes=[pltpu.SemaphoreType.DMA((slots,))],
        compiler_params=pltpu.CompilerParams(vmem_limit_bytes=1 << 20),
        name="gather",
    )(table, spot, line, *extras)


def return_image(image, table, spot):
    shots, tile_x, slab, nz = image.shape
    zs = lax.axis_size("zz")
    planes = tile_x // QUAD
    got = exchange(image.reshape(shots * QUAD, planes, slab, nz), PLANE)
    line, *extras = local_kernel(
        functools.partial(scatter_kernel, zs),
        "scatter",
        [table, spot],
        [got],
        [f32(zs * QUAD, planes, slab, nz)] + [f32(1, planes, slab, nz)] * QUAD,
        [pltpu.VMEM((QUAD, planes, slab, nz), jnp.float32)],
    )
    extras = quad_turn(extras)
    came = exchange(line, MP)
    (out,) = local_kernel(
        functools.partial(finish_kernel, zs),
        "finish",
        [spot],
        [came, *extras],
        [f32(2, tile_x, slab, nz)],
    )
    return out


def advance(n, name, ints, now, back, drive, speed):
    tile_x, ny, nz = now.shape
    rows = 2 * SUB
    block = pl.BlockSpec((tile_x, rows, nz), lambda i: (0, i, 0))
    side = pl.BlockSpec((REACH, rows, nz), lambda i: (0, i, 0))
    return pl.pallas_call(
        functools.partial(advance_kernel, n),
        grid=(ny // rows,),
        out_shape=[f32(tile_x, ny, nz)] * 2 + [f32(REACH, ny, nz)] * 2,
        in_specs=[
            pl.BlockSpec(memory_space=pltpu.SMEM),
            block,
            block,
            block,
            pl.BlockSpec((2, tile_x, SUB, nz), lambda i: (i, 0, 0, 0)),
        ],
        out_specs=[block, block, side, side],
        compiler_params=pltpu.CompilerParams(vmem_limit_bytes=VMEM_LIMIT),
        name=name,
    )(ints, in_hbm(now), in_hbm(back), in_hbm(drive), speed)


def halos(low, high):
    return shifted(high, MP, 1), shifted(low, MP, -1)


def body(
    courant,
    aperture_first,
    source_pos,
    wavelet,
    receiver_pos,
    residual,
    step_count,
    forward_prev,
    forward_now,
    adjoint_prev,
    adjoint_now,
):
    tile_x, ny, nz = forward_now.shape[1:]
    steps = wavelet.shape[1]
    receivers = receiver_pos.shape[1]
    spot = [lax.axis_index(name) for name in ("shot", "zz", "quad")]
    spot = jnp.stack(spot).astype(jnp.int32)
    line, extras = model_line(courant, spot)
    table = all_first(aperture_first[0])
    base = (lax.axis_index(MP) * tile_x).reshape(1).astype(jnp.int32)
    ints = jnp.concatenate([step_count, base, source_pos[0], receiver_pos[0].reshape(-1)])
    floats = jnp.concatenate([wavelet[0], residual[0].reshape(-1)])
    u, w = forward_now[0], adjoint_now[0]
    field = f32(tile_x, ny, nz)
    edge = f32(REACH, ny, nz)
    padded = pltpu.VMEM((nz // LANES, tile_x, ny + 2 * SUB, LANES), jnp.float32)
    along = pltpu.VMEM((tile_x, ny, nz), jnp.float32)
    scalars = [ints, floats]
    u_sides = halos(u[:REACH], u[tile_x - REACH :])
    w_sides = halos(w[:REACH], w[tile_x - REACH :])
    drives = []
    (drive,) = local_kernel(
        functools.partial(first_kernel, steps, receivers, "forward"),
        "first_forward",
        scalars,
        [u, *u_sides],
        [field],
        [padded],
    )
    (push,) = local_kernel(
        functools.partial(first_kernel, steps, receivers, "adjoint"),
        "first_adjoint",
        scalars,
        [w, *w_sides],
        [field],
        [padded],
    )
    sent = model_parts(line, extras, table, spot)
    sent, drive, push = lax.optimization_barrier((sent, drive, push))
    owned = exchange(sent, PLANE).reshape(-1, tile_x, SUB, nz)
    drives.append(drive)
    u, vu, low, high = advance(0, "advance_forward", ints, u, forward_prev[0], drive, owned)
    u_sides = halos(low, high)
    w, vw, low, high = advance(steps - 1, "advance_adjoint", ints, w, adjoint_prev[0], push, owned)
    w_sides = halos(low, high)
    backs = [w]
    for n in range(1, steps):
        last = n == steps - 1
        drive, *moved = local_kernel(
            functools.partial(forward_kernel, n, last),
            "forward",
            scalars,
            [u, vu, owned, *u_sides],
            [field] if last else [field, field, field, edge, edge],
            [padded, along],
        )
        drives.append(drive)
        if not last:
            u, vu, low, high = moved
            u_sides = halos(low, high)
        extra_in = []
        if last:
            pairs = []
            for k in range(steps - 1):
                pairs += [backs[k], drives[steps - 1 - k]]
            (partial,) = local_kernel(
                functools.partial(products_kernel, steps - 1), "products", [], pairs, [field]
            )
            extra_in = [partial, drives[0]]
        moved = local_kernel(
            functools.partial(adjoint_kernel, steps, receivers, steps - 1 - n, last),
            "adjoint",
            scalars,
            [w, vw, owned, *w_sides, *extra_in],
            [f32(ny // SUB, tile_x, SUB, nz)] if last else [field, field, edge, edge],
            [padded, along],
        )
        if not last:
            w, vw, low, high = moved
            w_sides = halos(low, high)
            backs.append(w)
    return return_image(moved[0], table, spot)


def solution(mesh):
    shots, mp = mesh.devices.shape
    fine = Mesh(mesh.devices.reshape(shots, mp // QUAD, QUAD), ("shot", "zz", "quad"))
    return jax.shard_map(
        body,
        mesh=fine,
        in_specs=(
            P(None, MP, None, None),
            P("shot"),
            P("shot", None),
            P("shot", None),
            P("shot", None, None),
            P("shot", None, None),
            P("shot"),
            P("shot", MP, None, None),
            P("shot", MP, None, None),
            P("shot", MP, None, None),
            P("shot", MP, None, None),
        ),
        out_specs=P(None, MP, "shot", None),
        check_vma=False,
    )
```

```python
import functools

import jax
import jax.numpy as jnp
from jax import lax
from jax.experimental import pallas as pl
from jax.experimental.pallas import tpu as pltpu
from jax.sharding import Mesh, PartitionSpec as P

COEF = (-205.0 / 72.0, 1.6, -0.2, 8.0 / 315.0, -1.0 / 560.0)
QUAD = 4
MP = ("zz", "quad")
PLANE = ("shot", "quad")
LANES = 128
SUB = 8
REACH = 4
COUNT, BASE, EVEN, SOURCE, RECEIVERS = 0, 1, 2, 3, 6
NEAR = 12
VMEM_LIMIT = 16 << 20


def all_first(first):
    return lax.all_gather(first, "shot", tiled=True)


def f32(*shape):
    return jax.ShapeDtypeStruct(shape, jnp.float32)


def local_kernel(body, name, scalars, arrays, outs, scratch=()):
    vmem = pl.BlockSpec(memory_space=pltpu.VMEM)
    smem = pl.BlockSpec(memory_space=pltpu.SMEM)
    return pl.pallas_call(
        body,
        out_shape=outs,
        in_specs=[smem] * len(scalars) + [vmem] * len(arrays),
        out_specs=[vmem] * len(outs),
        scratch_shapes=list(scratch),
        compiler_params=pltpu.CompilerParams(vmem_limit_bytes=VMEM_LIMIT),
        name=name,
    )(*scalars, *arrays)


def in_hbm(value):
    return pltpu.with_memory_space_constraint(value, pltpu.HBM)


def band_matrix(nz):
    rows = lax.broadcasted_iota(jnp.int32, (nz, nz), 0)
    cols = lax.broadcasted_iota(jnp.int32, (nz, nz), 1)
    apart = jnp.abs(rows - cols)
    band = jnp.where(apart == 0, 3.0 * COEF[0], 0.0)
    for k in range(1, REACH + 1):
        band = jnp.where(apart == k, COEF[k], band)
    return band


def prepare(field, padded, along_z):
    xs, ys, nz = field.shape
    along_z[...] = jnp.dot(
        field[...].reshape(xs * ys, nz),
        band_matrix(nz),
        precision=lax.Precision.HIGHEST,
        preferred_element_type=jnp.float32,
    ).reshape(xs, ys, nz)
    edge = jnp.zeros((xs, SUB, LANES), jnp.float32)
    for h in range(nz // LANES):
        padded[h, :, 0:SUB, :] = edge
        padded[h, :, SUB + ys : SUB + ys + SUB, :] = edge
        padded[h, :, SUB : SUB + ys, :] = field[:, :, h * LANES : (h + 1) * LANES]


def add_point(target, x, y, z, amount):
    xs, _, nz = target.shape

    @pl.when((x >= 0) & (x < xs))
    def _():
        cells = lax.broadcasted_iota(jnp.int32, (1, 1, nz), 2)
        place = (pl.ds(x, 1), pl.ds(y, 1), slice(None))
        target[place] = target[place] + jnp.where(cells == z, amount, 0.0)


def add_source(target, ints, floats, n):
    x = ints[SOURCE] - ints[BASE]
    add_point(target, x, ints[SOURCE + 1], ints[SOURCE + 2], floats[n])


def add_receivers(target, ints, floats, steps, receivers, n):
    xs = target.shape[0]
    away = ints[SOURCE] - ints[BASE]

    @pl.when((away + NEAR >= 0) & (away - NEAR < xs))
    def _():
        def one(j, carry):
            at = RECEIVERS + 3 * j
            amount = floats[steps + n * receivers + j]
            add_point(target, ints[at] - ints[BASE], ints[at + 1], ints[at + 2], amount)
            return carry

        lax.fori_loop(0, receivers, one, 0)


def laplacian(padded, along_z, even, inner, outer, y0, h, plane=0):
    xs = along_z.shape[0]
    rows = pl.ds(y0, SUB)
    lanes = slice(h * LANES, (h + 1) * LANES)
    near = [inner[plane + j, rows, lanes] for j in range(REACH)]
    far = [outer[plane + j, rows, lanes] for j in range(REACH)]
    column = [jnp.where(even, far[j], near[j]) for j in range(REACH)]
    column += [padded[h, x, pl.ds(y0 + SUB, SUB), :] for x in range(xs)]
    column += [jnp.where(even, near[j], far[j]) for j in range(REACH)]
    for x in range(xs):
        total = along_z[x, rows, lanes]
        for k in range(1, REACH + 1):
            pair = column[x + REACH + k] + column[x + REACH - k]
            pair = pair + (
                padded[h, x, pl.ds(y0 + SUB + k, SUB), :]
                + padded[h, x, pl.ds(y0 + SUB - k, SUB), :]
            )
            total = total + COEF[k] * pair
        yield x, column[x + REACH], total


def each_block(field, work):
    _, ys, nz = field.shape

    def step(i, carry):
        y0 = pl.multiple_of(i * SUB, SUB)
        for h in range(nz // LANES):
            work(i, y0, h, slice(h * LANES, (h + 1) * LANES))
        return carry

    lax.fori_loop(0, ys // SUB, step, 0)


def switch_on(ints, n):
    return jnp.where(ints[COUNT] > n, 1.0, 0.0).astype(jnp.float32)


def first_kernel(steps, receivers, ints, floats, u, w, inner, outer, d, e, pad_u, pad_w):
    prepare(u, pad_u, d)
    prepare(w, pad_w, e)
    add_source(d, ints, floats, 0)
    add_receivers(e, ints, floats, steps, receivers, steps - 1)
    live_u = switch_on(ints, 0)
    live_w = switch_on(ints, steps - 1)
    even = ints[EVEN] == 1

    def work(i, y0, h, lanes):
        rows = pl.ds(y0, SUB)
        for x, _, total in laplacian(pad_u, d, even, inner, outer, y0, h):
            d[x, rows, lanes] = live_u * total
        for x, _, total in laplacian(pad_w, e, even, inner, outer, y0, h, REACH):
            e[x, rows, lanes] = live_w * total

    each_block(u, work)


def edge_out(even, field, inner, outer):
    xs = field.shape[0]

    @pl.when(even)
    def _():
        inner[...] = field[xs - REACH :]
        outer[...] = field[:REACH]

    @pl.when(jnp.logical_not(even))
    def _():
        inner[...] = field[:REACH]
        outer[...] = field[xs - REACH :]


def edges_kernel(n, ints, now, back, drive, speed, inner, outer, held, sems):
    xs, ys, nz = now.shape
    live = switch_on(ints, n)
    even = ints[EVEN] == 1
    starts = (0, xs - REACH)
    copies = []
    for k, source in enumerate((now, back, drive)):
        for side, x0 in enumerate(starts):
            copies.append(
                pltpu.make_async_copy(
                    source.at[pl.ds(x0, REACH)], held.at[k, side], sems.at[k, side]
                )
            )
    for copy in copies:
        copy.start()
    for copy in copies:
        copy.wait()

    def step(i, carry):
        rows = pl.ds(pl.multiple_of(i * SUB, SUB), SUB)
        for side, x0 in enumerate(starts):
            for j in range(REACH):
                here = held[0, side, j, rows, :]
                more = (here - held[1, side, j, rows, :]) + speed[i, x0 + j] * held[2, side, j, rows, :]
                held[0, side, j, rows, :] = here + live * more
        return carry

    lax.fori_loop(0, ys // SUB, step, 0)

    @pl.when(even)
    def _():
        inner[...] = held[0, 1]
        outer[...] = held[0, 0]

    @pl.when(jnp.logical_not(even))
    def _():
        inner[...] = held[0, 0]
        outer[...] = held[0, 1]


def advance_kernel(n, ints, now, back, drive, speed, new, gain):
    live = switch_on(ints, n)

    def work(i, y0, h, lanes):
        rows = pl.ds(y0, SUB)
        for x in range(now.shape[0]):
            here = now[x, rows, lanes]
            more = (here - back[x, rows, lanes]) + speed[i, x, :, lanes] * drive[x, rows, lanes]
            gain[x, rows, lanes] = more
            new[x, rows, lanes] = here + live * more

    each_block(now, work)


def forward_kernel(n, last, ints, floats, u, vu, p, near, far, drive, *rest):
    if last:
        pad, along = rest
    else:
        new, gain, inner, outer, pad, along = rest
    prepare(u, pad, along)
    add_source(along, ints, floats, n)
    live = switch_on(ints, n)
    even = ints[EVEN] == 1

    def work(i, y0, h, lanes):
        rows = pl.ds(y0, SUB)
        for x, here, total in laplacian(pad, along, even, near, far, y0, h):
            total = live * total
            drive[x, rows, lanes] = total
            if last:
                continue
            more = vu[x, rows, lanes] + p[i, x, :, lanes] * total
            gain[x, rows, lanes] = more
            new[x, rows, lanes] = here + more

    each_block(u, work)
    if not last:
        edge_out(even, new, inner, outer)


def adjoint_kernel(steps, receivers, n, last, ints, floats, w, vw, p, near, far, *rest):
    if last:
        partial, drive, image, pad, along = rest
    else:
        new, gain, inner, outer, pad, along = rest
    prepare(w, pad, along)
    add_receivers(along, ints, floats, steps, receivers, n)
    live = switch_on(ints, n)
    even = ints[EVEN] == 1

    def work(i, y0, h, lanes):
        rows = pl.ds(y0, SUB)
        for x, here, total in laplacian(pad, along, even, near, far, y0, h):
            more = vw[x, rows, lanes] + (live * p[i, x, :, lanes]) * total
            here = here + live * more
            if last:
                image[i, x, :, lanes] = partial[x, rows, lanes] + here * drive[x, rows, lanes]
                continue
            gain[x, rows, lanes] = more
            new[x, rows, lanes] = here

    each_block(w, work)
    if not last:
        edge_out(even, new, inner, outer)


def products_kernel(pairs, *refs):
    out = refs[-1]

    def work(i, y0, h, lanes):
        rows = pl.ds(y0, SUB)
        for x in range(out.shape[0]):
            total = refs[0][x, rows, lanes] * refs[1][x, rows, lanes]
            for j in range(1, pairs):
                total = total + refs[2 * j][x, rows, lanes] * refs[2 * j + 1][x, rows, lanes]
            out[x, rows, lanes] = total

    each_block(out, work)


def split_kernel(spot, courant, parts, swap, keep, slab_in, sems):
    zs = parts.shape[0]
    _, tile_x, slab, _ = slab_in.shape
    planes = tile_x // QUAD
    me_shot, me_z, me_q = spot[0], spot[1], spot[2]
    rows = pl.ds(pl.multiple_of(me_shot * slab, SUB), slab)
    load = pltpu.make_async_copy(courant.at[:, :, rows, :], slab_in, sems.at[zs])
    load.start()
    load.wait()
    copies = []
    for z in range(zs):
        row = jnp.where(z <= me_z, 0, 1)
        copies.append(pltpu.make_async_copy(slab_in.at[row], parts.at[z], sems.at[z]))
    for copy in copies:
        copy.start()
    for k, turn in enumerate((0, 2)):
        keep[k] = slab_in[1, pl.ds((me_q ^ turn) * planes, planes)]
        swap[k] = slab_in[1, pl.ds((me_q ^ turn ^ 1) * planes, planes)]
    for copy in copies:
        copy.wait()


def relay_kernel(keep, swapped, out):
    out[0] = keep[1]
    out[1] = swapped[1]


def gather_kernel(zs, table, spot, line, keep, swapped, far, sent, held, sems):
    shots = sent.shape[0] // QUAD
    me_z, me_q = spot[1], spot[2]
    copies = []
    for s in range(shots):

        def one(j, carry):
            tile = table[s] + j
            place = ((me_z + tile // QUAD) % zs) * QUAD + tile % QUAD
            turn = me_q ^ (tile % QUAD)

            @pl.when(tile < zs * QUAD)
            def _():
                held[s, j] = line[place]

            @pl.when(tile >= zs * QUAD)
            def _():
                near = jnp.where(turn == 0, keep[0], swapped[0])
                other = jnp.where(turn == 2, far[0], far[1])
                held[s, j] = jnp.where(turn < 2, near, other)

            return carry

        lax.fori_loop(0, QUAD, one, 0)
        copy = pltpu.make_async_copy(held.at[s], sent.at[pl.ds(s * QUAD, QUAD)], sems.at[s])
        copy.start()
        copies.append(copy)
    for copy in copies:
        copy.wait()


def scatter_kernel(zs, table, spot, got, line, keep, swap, held, sems):
    me_z, me_q = spot[1], spot[2]
    planes = held.shape[1]
    held[...] = jnp.zeros_like(held)
    keep[...] = jnp.zeros_like(keep)
    swap[...] = jnp.zeros_like(swap)

    def one(slot, carry):
        tile = table[slot // QUAD] + slot % QUAD
        place = ((me_z + tile // QUAD) % zs) * QUAD + tile % QUAD
        turn = me_q ^ (tile % QUAD)

        @pl.when(tile < zs * QUAD)
        def _():
            held[place] = held[place] + got[slot]

        @pl.when((tile >= zs * QUAD) & (turn % 2 == 0))
        def _():
            keep[turn // 2] = keep[turn // 2] + got[slot]

        @pl.when((tile >= zs * QUAD) & (turn % 2 == 1))
        def _():
            swap[turn // 2] = swap[turn // 2] + got[slot]

        return carry

    lax.fori_loop(0, got.shape[0], one, 0)
    copy = pltpu.make_async_copy(held, line, sems.at[0])
    copy.start()
    copy.wait()


def finish_kernel(zs, spot, came, keep, swapped, far, out):
    planes = came.shape[1]
    me_z, me_q = spot[1], spot[2]
    extras = (keep[0], swapped[0], far[0], far[1])
    for turn in range(QUAD):
        q = me_q ^ turn
        low = came[q]
        high = extras[turn]
        for z in range(1, zs):
            value = came[z * QUAD + q]
            low = low + jnp.where(z <= me_z, value, 0.0)
            high = high + jnp.where(z <= me_z, 0.0, value)
        out[0, pl.ds(q * planes, planes)] = low
        out[1, pl.ds(q * planes, planes)] = high


def exchange(parts, axes):
    return lax.all_to_all(parts, axes, split_axis=0, concat_axis=0, tiled=True)


def swap_quads(value, turn):
    return lax.ppermute(value, "quad", [(q, q ^ turn) for q in range(QUAD)])


def quad_relay(keep, swap):
    swapped = swap_quads(swap, 1)
    (far,) = local_kernel(relay_kernel, "relay", [], [keep, swapped], [f32(*keep.shape)])
    return keep, swapped, swap_quads(far, 2)


def model_line(courant, spot):
    rows, tile_x, ny, nz = courant.shape
    zs = lax.axis_size("zz")
    slab = ny // lax.axis_size("shot")
    planes = tile_x // QUAD
    hbm = pl.BlockSpec(memory_space=pltpu.HBM)
    vmem = pl.BlockSpec(memory_space=pltpu.VMEM)
    parts, swap, keep = pl.pallas_call(
        split_kernel,
        out_shape=[f32(zs, tile_x, slab, nz)] + [f32(2, planes, slab, nz)] * 2,
        in_specs=[pl.BlockSpec(memory_space=pltpu.SMEM), hbm],
        out_specs=[hbm, vmem, vmem],
        scratch_shapes=[
            pltpu.VMEM((rows, tile_x, slab, nz), jnp.float32),
            pltpu.SemaphoreType.DMA((zs + 1,)),
        ],
        compiler_params=pltpu.CompilerParams(vmem_limit_bytes=VMEM_LIMIT),
        name="split",
    )(spot, in_hbm(courant))
    line = exchange(parts.reshape(zs * QUAD, planes, slab, nz), MP)
    return line, quad_relay(keep, swap)


def model_parts(line, extras, table, spot):
    shots = lax.axis_size("shot")
    smem = pl.BlockSpec(memory_space=pltpu.SMEM)
    vmem = pl.BlockSpec(memory_space=pltpu.VMEM)
    shape = line.shape[1:]
    return pl.pallas_call(
        functools.partial(gather_kernel, lax.axis_size("zz")),
        out_shape=f32(shots * QUAD, *shape),
        in_specs=[smem, smem] + [vmem] * 4,
        out_specs=pl.BlockSpec(memory_space=pltpu.HBM),
        scratch_shapes=[
            pltpu.VMEM((shots, QUAD, *shape), jnp.float32),
            pltpu.SemaphoreType.DMA((shots,)),
        ],
        compiler_params=pltpu.CompilerParams(vmem_limit_bytes=VMEM_LIMIT),
        name="gather",
    )(table, spot, line, *extras)


def return_image(image, table, spot):
    shots, tile_x, slab, nz = image.shape
    zs = lax.axis_size("zz")
    planes = tile_x // QUAD
    got = exchange(image.reshape(shots * QUAD, planes, slab, nz), PLANE)
    smem = pl.BlockSpec(memory_space=pltpu.SMEM)
    vmem = pl.BlockSpec(memory_space=pltpu.VMEM)
    line, keep, swap = pl.pallas_call(
        functools.partial(scatter_kernel, zs),
        out_shape=[f32(zs * QUAD, planes, slab, nz)] + [f32(2, planes, slab, nz)] * 2,
        in_specs=[smem, smem, vmem],
        out_specs=[pl.BlockSpec(memory_space=pltpu.HBM), vmem, vmem],
        scratch_shapes=[
            pltpu.VMEM((zs * QUAD, planes, slab, nz), jnp.float32),
            pltpu.SemaphoreType.DMA((1,)),
        ],
        compiler_params=pltpu.CompilerParams(vmem_limit_bytes=VMEM_LIMIT),
        name="scatter",
    )(table, spot, got)
    came = exchange(line, MP)
    extras = quad_relay(keep, swap)
    (out,) = local_kernel(
        functools.partial(finish_kernel, zs),
        "finish",
        [spot],
        [came, *extras],
        [f32(2, tile_x, slab, nz)],
    )
    return out


def edges(n, name, ints, now, back, drive, speed):
    _, ny, nz = now.shape
    hbm = pl.BlockSpec(memory_space=pltpu.HBM)
    vmem = pl.BlockSpec(memory_space=pltpu.VMEM)
    return pl.pallas_call(
        functools.partial(edges_kernel, n),
        out_shape=[f32(REACH, ny, nz)] * 2,
        in_specs=[pl.BlockSpec(memory_space=pltpu.SMEM), hbm, hbm, hbm, vmem],
        out_specs=[vmem, vmem],
        scratch_shapes=[
            pltpu.VMEM((3, 2, REACH, ny, nz), jnp.float32),
            pltpu.SemaphoreType.DMA((3, 2)),
        ],
        compiler_params=pltpu.CompilerParams(vmem_limit_bytes=VMEM_LIMIT),
        name=name,
    )(ints, in_hbm(now), in_hbm(back), in_hbm(drive), speed)


def advance(n, name, ints, now, back, drive, speed):
    tile_x, ny, nz = now.shape
    rows = 2 * SUB
    block = pl.BlockSpec((tile_x, rows, nz), lambda i: (0, i, 0))
    return pl.pallas_call(
        functools.partial(advance_kernel, n),
        grid=(ny // rows,),
        out_shape=[f32(tile_x, ny, nz)] * 2,
        in_specs=[
            pl.BlockSpec(memory_space=pltpu.SMEM),
            block,
            block,
            block,
            pl.BlockSpec((2, tile_x, SUB, nz), lambda i: (i, 0, 0, 0)),
        ],
        out_specs=[block, block],
        compiler_params=pltpu.CompilerParams(vmem_limit_bytes=VMEM_LIMIT),
        name=name,
    )(ints, in_hbm(now), in_hbm(back), in_hbm(drive), speed)


def halos(inner, outer):
    count = lax.axis_size(MP)
    across = [(i, i + 1) for i in range(1, count - 1, 2)]
    return (
        lax.ppermute(inner, MP, [(i, i ^ 1) for i in range(count)]),
        lax.ppermute(outer, MP, across + [(j, i) for i, j in across]),
    )


def body(
    courant,
    aperture_first,
    source_pos,
    wavelet,
    receiver_pos,
    residual,
    step_count,
    forward_prev,
    forward_now,
    adjoint_prev,
    adjoint_now,
):
    tile_x, ny, nz = forward_now.shape[1:]
    steps = wavelet.shape[1]
    receivers = receiver_pos.shape[1]
    spot = [lax.axis_index(name) for name in ("shot", "zz", "quad")]
    spot = jnp.stack(spot).astype(jnp.int32)
    line, extras = model_line(courant, spot)
    table = all_first(aperture_first)
    me_index = lax.axis_index(MP)
    even = me_index % 2 == 0
    base = (me_index * tile_x).reshape(1).astype(jnp.int32)
    ints = jnp.concatenate(
        [
            step_count,
            base,
            even.reshape(1).astype(jnp.int32),
            source_pos[0],
            receiver_pos[0].reshape(-1),
        ]
    )
    floats = jnp.concatenate([wavelet[0], residual[0].reshape(-1)])
    u, w = forward_now[0], adjoint_now[0]
    field = f32(tile_x, ny, nz)
    edge = f32(REACH, ny, nz)
    padded = pltpu.VMEM((nz // LANES, tile_x, ny + 2 * SUB, LANES), jnp.float32)
    along = pltpu.VMEM((tile_x, ny, nz), jnp.float32)
    scalars = [ints, floats]
    low = jnp.concatenate([u[:REACH], w[:REACH]])
    high = jnp.concatenate([u[tile_x - REACH :], w[tile_x - REACH :]])
    sides = halos(jnp.where(even, high, low), jnp.where(even, low, high))
    drives = []
    drive, push = local_kernel(
        functools.partial(first_kernel, steps, receivers),
        "first",
        scalars,
        [u, w, *sides],
        [field, field],
        [padded, padded],
    )
    sent = model_parts(line, extras, table, spot)
    sent, drive, push = lax.optimization_barrier((sent, drive, push))
    owned = exchange(sent, PLANE).reshape(-1, tile_x, SUB, nz)
    drives.append(drive)
    before_u = (0, ints, u, forward_prev[0], drive, owned)
    before_w = (steps - 1, ints, w, adjoint_prev[0], push, owned)
    u_sides = halos(*edges(before_u[0], "edges_forward", *before_u[1:]))
    w_sides = halos(*edges(before_w[0], "edges_adjoint", *before_w[1:]))
    u, vu = advance(before_u[0], "advance_forward", *before_u[1:])
    w, vw = advance(before_w[0], "advance_adjoint", *before_w[1:])
    backs = [w]
    for n in range(1, steps):
        last = n == steps - 1
        drive, *moved = local_kernel(
            functools.partial(forward_kernel, n, last),
            "forward",
            scalars,
            [u, vu, owned, *u_sides],
            [field] if last else [field, field, field, edge, edge],
            [padded, along],
        )
        drives.append(drive)
        if not last:
            u, vu, inner, outer = moved
            u_sides = halos(inner, outer)
        extra_in = []
        if last:
            pairs = []
            for k in range(steps - 1):
                pairs += [backs[k], drives[steps - 1 - k]]
            (partial,) = local_kernel(
                functools.partial(products_kernel, steps - 1), "products", [], pairs, [field]
            )
            extra_in = [partial, drives[0]]
        moved = local_kernel(
            functools.partial(adjoint_kernel, steps, receivers, steps - 1 - n, last),
            "adjoint",
            scalars,
            [w, vw, owned, *w_sides, *extra_in],
            [f32(ny // SUB, tile_x, SUB, nz)] if last else [field, field, edge, edge],
            [padded, along],
        )
        if not last:
            w, vw, inner, outer = moved
            w_sides = halos(inner, outer)
            backs.append(w)
    return return_image(moved[0], table, spot)


def solution(mesh):
    shots, mp = mesh.devices.shape
    fine = Mesh(mesh.devices.reshape(shots, mp // QUAD, QUAD), ("shot", "zz", "quad"))
    return jax.shard_map(
        body,
        mesh=fine,
        in_specs=(
            P(None, MP, None, None),
            P("shot"),
            P("shot", None),
            P("shot", None),
            P("shot", None, None),
            P("shot", None, None),
            P("shot"),
            P("shot", MP, None, None),
            P("shot", MP, None, None),
            P("shot", MP, None, None),
            P("shot", MP, None, None),
        ),
        out_specs=P(None, MP, "shot", None),
        check_vma=False,
    )
```

```python
import functools

import jax
import jax.numpy as jnp
from jax import lax
from jax.experimental import pallas as pl
from jax.experimental.pallas import tpu as pltpu
from jax.sharding import Mesh, PartitionSpec as P


COEF = (-205.0 / 72.0, 1.6, -0.2, 8.0 / 315.0, -1.0 / 560.0)
QUAD = 4
MP = ("zz", "quad")
PLANE = ("shot", "quad")
LANES = 128
SUB = 8
REACH = 4
COUNT, BASE, EVEN, SOURCE, RECEIVERS = 0, 1, 2, 3, 6
NEAR = 12
VMEM_LIMIT = 16 << 20


def all_first(first):
    shots = lax.axis_size("shot")
    me = lax.axis_index("shot")
    known = jnp.where(jnp.arange(shots, dtype=jnp.int32) == me, first, 0)
    step = 1
    while step < shots:
        known = known + lax.ppermute(known, "shot", [(i, i ^ step) for i in range(shots)])
        step *= 2
    return known


def f32(*shape):
    return jax.ShapeDtypeStruct(shape, jnp.float32)


def hbm32(*shape):
    return pltpu.HBM(shape, jnp.float32)


def local_kernel(body, scalars, arrays, outs, scratch=()):
    vmem = pl.BlockSpec(memory_space=pltpu.VMEM)
    smem = pl.BlockSpec(memory_space=pltpu.SMEM)
    return pl.pallas_call(
        body,
        out_shape=outs,
        in_specs=[smem] * len(scalars) + [vmem] * len(arrays),
        out_specs=[vmem] * len(outs),
        scratch_shapes=list(scratch),
        compiler_params=pltpu.CompilerParams(vmem_limit_bytes=VMEM_LIMIT),
    )(*scalars, *arrays)


def in_hbm(value):
    return pltpu.with_memory_space_constraint(value, pltpu.HBM)


def band_matrix(nz):
    rows = lax.broadcasted_iota(jnp.int32, (nz, nz), 0)
    cols = lax.broadcasted_iota(jnp.int32, (nz, nz), 1)
    apart = jnp.abs(rows - cols)
    band = jnp.where(apart == 0, 3.0 * COEF[0], 0.0)
    for k in range(1, REACH + 1):
        band = jnp.where(apart == k, COEF[k], band)
    return band


def prepare(field, padded, along_z):
    xs, ys, nz = field.shape
    along_z[...] = jnp.dot(
        field[...].reshape(xs * ys, nz),
        band_matrix(nz),
        precision=lax.Precision.HIGHEST,
        preferred_element_type=jnp.float32,
    ).reshape(xs, ys, nz)
    edge = jnp.zeros((xs, SUB, LANES), jnp.float32)
    for h in range(nz // LANES):
        padded[h, :, 0:SUB, :] = edge
        padded[h, :, SUB + ys : SUB + ys + SUB, :] = edge
        padded[h, :, SUB : SUB + ys, :] = field[:, :, h * LANES : (h + 1) * LANES]


def add_point(target, x, y, z, amount):
    xs, _, nz = target.shape

    @pl.when((x >= 0) & (x < xs))
    def _():
        cells = lax.broadcasted_iota(jnp.int32, (1, 1, nz), 2)
        place = (pl.ds(x, 1), pl.ds(y, 1), slice(None))
        target[place] = target[place] + jnp.where(cells == z, amount, 0.0)


def add_source(target, ints, floats, n):
    x = ints[SOURCE] - ints[BASE]
    add_point(target, x, ints[SOURCE + 1], ints[SOURCE + 2], floats[n])


def add_receivers(target, ints, floats, steps, receivers, n):
    xs = target.shape[0]
    away = ints[SOURCE] - ints[BASE]

    @pl.when((away + NEAR >= 0) & (away - NEAR < xs))
    def _():
        def one(j, carry):
            at = RECEIVERS + 3 * j
            amount = floats[steps + n * receivers + j]
            add_point(target, ints[at] - ints[BASE], ints[at + 1], ints[at + 2], amount)
            return carry

        lax.fori_loop(0, receivers, one, 0)


def laplacian(padded, along_z, even, inner, outer, y0, h, plane=0):
    xs = along_z.shape[0]
    rows = pl.ds(y0, SUB)
    lanes = slice(h * LANES, (h + 1) * LANES)
    near = [inner[plane + j, rows, lanes] for j in range(REACH)]
    far = [outer[plane + j, rows, lanes] for j in range(REACH)]
    column = [jnp.where(even, far[j], near[j]) for j in range(REACH)]
    column += [padded[h, x, pl.ds(y0 + SUB, SUB), :] for x in range(xs)]
    column += [jnp.where(even, near[j], far[j]) for j in range(REACH)]
    for x in range(xs):
        total = along_z[x, rows, lanes]
        for k in range(1, REACH + 1):
            pair = column[x + REACH + k] + column[x + REACH - k]
            pair = pair + (
                padded[h, x, pl.ds(y0 + SUB + k, SUB), :]
                + padded[h, x, pl.ds(y0 + SUB - k, SUB), :]
            )
            total = total + COEF[k] * pair
        yield x, column[x + REACH], total


def each_block(field, work):
    _, ys, nz = field.shape

    def step(i, carry):
        y0 = pl.multiple_of(i * SUB, SUB)
        for h in range(nz // LANES):
            work(i, y0, h, slice(h * LANES, (h + 1) * LANES))
        return carry

    lax.fori_loop(0, ys // SUB, step, 0)


def switch_on(ints, n):
    return jnp.where(ints[COUNT] > n, 1.0, 0.0).astype(jnp.float32)


def first_kernel(steps, receivers, ints, floats, u, w, near, far, d, e, along_u, along_w, pad, sems):
    even = ints[EVEN] == 1
    copies = []
    for k, (field, along, out) in enumerate(((u, along_u, d), (w, along_w, e))):
        prepare(field, pad, along)
        if k == 0:
            add_source(along, ints, floats, 0)
            live = switch_on(ints, 0)
        else:
            add_receivers(along, ints, floats, steps, receivers, steps - 1)
            live = switch_on(ints, steps - 1)

        def work(i, y0, h, lanes):
            rows = pl.ds(y0, SUB)
            for x, _, total in laplacian(pad, along, even, near, far, y0, h, k * REACH):
                along[x, rows, lanes] = live * total

        each_block(field, work)
        copy = pltpu.make_async_copy(along, out, sems.at[k])
        copy.start()
        copies.append(copy)
    for copy in copies:
        copy.wait()


def edge_out(even, field, inner, outer):
    xs = field.shape[0]

    @pl.when(even)
    def _():
        inner[...] = field[xs - REACH :]
        outer[...] = field[:REACH]

    @pl.when(jnp.logical_not(even))
    def _():
        inner[...] = field[:REACH]
        outer[...] = field[xs - REACH :]


def edges_kernel(n, ints, now, back, drive, speed, inner, outer, held, sems):
    xs, ys, _ = now.shape
    live = switch_on(ints, n)
    even = ints[EVEN] == 1
    starts = (0, xs - REACH)
    copies = []
    for k, source in enumerate((now, back, drive)):
        for side, x0 in enumerate(starts):
            copies.append(
                pltpu.make_async_copy(
                    source.at[pl.ds(x0, REACH)], held.at[k, side], sems.at[k, side]
                )
            )
    for copy in copies:
        copy.start()
    for copy in copies:
        copy.wait()

    def step(i, carry):
        rows = pl.ds(pl.multiple_of(i * SUB, SUB), SUB)
        for side, x0 in enumerate(starts):
            for j in range(REACH):
                here = held[0, side, j, rows, :]
                more = (here - held[1, side, j, rows, :]) + speed[i, x0 + j] * held[2, side, j, rows, :]
                held[0, side, j, rows, :] = here + live * more
        return carry

    lax.fori_loop(0, ys // SUB, step, 0)

    @pl.when(even)
    def _():
        inner[...] = held[0, 1]
        outer[...] = held[0, 0]

    @pl.when(jnp.logical_not(even))
    def _():
        inner[...] = held[0, 0]
        outer[...] = held[0, 1]


def opening(ints, n, now, back, drive, speed, new, gain):
    live = switch_on(ints, n)

    def work(i, y0, h, lanes):
        rows = pl.ds(y0, SUB)
        for x in range(now.shape[0]):
            here = now[x, rows, lanes]
            more = (here - back[x, rows, lanes]) + speed[i, x, :, lanes] * drive[x, rows, lanes]
            gain[x, rows, lanes] = more
            new[x, rows, lanes] = here + live * more

    each_block(now, work)


def forward_kernel(n, last, ints, floats, *refs):
    if n == 1:
        u0, back, drive0, p, near, far, drive, new, gain, inner, outer, pad, along = refs
        opening(ints, 0, u0, back, drive0, p, new, gain)
        u, vu = new, gain
    elif last:
        u, vu, p, near, far, drive, pad, along = refs
    else:
        u, vu, p, near, far, drive, new, gain, inner, outer, pad, along = refs
    prepare(u, pad, along)
    add_source(along, ints, floats, n)
    live = switch_on(ints, n)
    even = ints[EVEN] == 1

    def work(i, y0, h, lanes):
        rows = pl.ds(y0, SUB)
        for x, here, total in laplacian(pad, along, even, near, far, y0, h):
            total = live * total
            drive[x, rows, lanes] = total
            if last:
                continue
            more = vu[x, rows, lanes] + p[i, x, :, lanes] * total
            gain[x, rows, lanes] = more
            new[x, rows, lanes] = here + more

    each_block(u, work)
    if not last:
        edge_out(even, new, inner, outer)


def adjoint_kernel(steps, receivers, n, last, ints, floats, *refs):
    if n == steps - 2:
        w0, back, push, p, near, far, w, new, gain, inner, outer, pad, along = refs
        opening(ints, steps - 1, w0, back, push, p, w, gain)
        vw = gain
    elif last:
        w, vw, p, near, far, partial, drive, image, pad, along = refs
    else:
        w, vw, p, near, far, new, gain, inner, outer, pad, along = refs
    prepare(w, pad, along)
    add_receivers(along, ints, floats, steps, receivers, n)
    live = switch_on(ints, n)
    even = ints[EVEN] == 1

    def work(i, y0, h, lanes):
        rows = pl.ds(y0, SUB)
        for x, here, total in laplacian(pad, along, even, near, far, y0, h):
            more = vw[x, rows, lanes] + (live * p[i, x, :, lanes]) * total
            here = here + live * more
            if last:
                image[i, x, :, lanes] = partial[x, rows, lanes] + here * drive[x, rows, lanes]
                continue
            gain[x, rows, lanes] = more
            new[x, rows, lanes] = here

    each_block(w, work)
    if not last:
        edge_out(even, new, inner, outer)


def products_kernel(pairs, *refs):
    out = refs[-1]

    def work(i, y0, h, lanes):
        rows = pl.ds(y0, SUB)
        for x in range(out.shape[0]):
            total = refs[0][x, rows, lanes] * refs[1][x, rows, lanes]
            for j in range(1, pairs):
                total = total + refs[2 * j][x, rows, lanes] * refs[2 * j + 1][x, rows, lanes]
            out[x, rows, lanes] = total

    each_block(out, work)


def split_kernel(spot, courant, u, w, parts, inner, outer, swap, keep, slab_in, sems):
    zs = parts.shape[0]
    _, tile_x, slab, _ = slab_in.shape
    planes = tile_x // QUAD
    me_shot, me_z, me_q = spot[0], spot[1], spot[2]
    rows = pl.ds(pl.multiple_of(me_shot * slab, SUB), slab)
    load = pltpu.make_async_copy(courant.at[:, :, rows, :], slab_in, sems.at[zs])
    load.start()
    copies = []
    first = jnp.where(me_q % 2 == 0, tile_x - REACH, 0)
    for k, field in enumerate((u, w)):
        for side, out in enumerate((inner, outer)):
            x0 = first if side == 0 else tile_x - REACH - first
            copies.append(
                pltpu.make_async_copy(
                    field.at[pl.ds(x0, REACH)],
                    out.at[pl.ds(k * REACH, REACH)],
                    sems.at[zs + 1 + 2 * k + side],
                )
            )
    for copy in copies:
        copy.start()
    load.wait()
    for z in range(zs):
        row = jnp.where(z <= me_z, 0, 1)
        copy = pltpu.make_async_copy(slab_in.at[row], parts.at[z], sems.at[z])
        copy.start()
        copies.append(copy)
    for k, turn in enumerate((0, 2)):
        keep[k] = slab_in[1, pl.ds((me_q ^ turn) * planes, planes)]
        swap[k] = slab_in[1, pl.ds((me_q ^ turn ^ 1) * planes, planes)]
    for copy in copies:
        copy.wait()


def relay_kernel(keep, swapped, out):
    out[0] = keep[1]
    out[1] = swapped[1]


def gather_kernel(zs, table, spot, line, keep, swapped, far, sent, sems):
    slots = sent.shape[0]
    me_z, me_q = spot[1], spot[2]

    def one(slot, carry):
        tile = table[slot // QUAD] + slot % QUAD
        place = ((me_z + tile // QUAD) % zs) * QUAD + tile % QUAD
        turn = me_q ^ (tile % QUAD)

        def send(source):
            pltpu.make_async_copy(source, sent.at[slot], sems.at[slot]).start()

        @pl.when(tile < zs * QUAD)
        def _():
            send(line.at[place])

        @pl.when(tile >= zs * QUAD)
        def _():
            @pl.when(turn == 0)
            def _():
                send(keep.at[0])

            @pl.when(turn == 1)
            def _():
                send(swapped.at[0])

            @pl.when(turn > 1)
            def _():
                send(far.at[turn - 2])

        return carry

    lax.fori_loop(0, slots, one, 0)

    def done(slot, carry):
        pltpu.make_async_copy(line.at[0], sent.at[slot], sems.at[slot]).wait()
        return carry

    lax.fori_loop(0, slots, done, 0)


def scatter_kernel(zs, table, spot, got, line, keep, swap, held, sems):
    me_z, me_q = spot[1], spot[2]
    held[...] = jnp.zeros_like(held)
    keep[...] = jnp.zeros_like(keep)
    swap[...] = jnp.zeros_like(swap)

    def one(slot, carry):
        tile = table[slot // QUAD] + slot % QUAD
        place = ((me_z + tile // QUAD) % zs) * QUAD + tile % QUAD
        turn = me_q ^ (tile % QUAD)

        @pl.when(tile < zs * QUAD)
        def _():
            held[place] = held[place] + got[slot]

        @pl.when((tile >= zs * QUAD) & (turn % 2 == 0))
        def _():
            keep[turn // 2] = keep[turn // 2] + got[slot]

        @pl.when((tile >= zs * QUAD) & (turn % 2 == 1))
        def _():
            swap[turn // 2] = swap[turn // 2] + got[slot]

        return carry

    lax.fori_loop(0, got.shape[0], one, 0)
    copy = pltpu.make_async_copy(held, line, sems.at[0])
    copy.start()
    copy.wait()


def finish_kernel(zs, spot, came, keep, swapped, far, out):
    planes = came.shape[1]
    me_z, me_q = spot[1], spot[2]
    extras = (keep[0], swapped[0], far[0], far[1])
    for turn in range(QUAD):
        q = me_q ^ turn
        low = came[q]
        high = extras[turn]
        for z in range(1, zs):
            value = came[z * QUAD + q]
            low = low + jnp.where(z <= me_z, value, 0.0)
            high = high + jnp.where(z <= me_z, 0.0, value)
        out[0, pl.ds(q * planes, planes)] = low
        out[1, pl.ds(q * planes, planes)] = high


def exchange(parts, axes):
    return lax.all_to_all(parts, axes, split_axis=0, concat_axis=0, tiled=True)


def swap_quads(value, turn):
    return lax.ppermute(value, "quad", [(q, q ^ turn) for q in range(QUAD)])


def quad_relay(keep, swap):
    swapped = swap_quads(swap, 1)
    (far,) = local_kernel(relay_kernel, [], [keep, swapped], [f32(*keep.shape)])
    return keep, swapped, swap_quads(far, 2)


def open_moves(courant, u, w, spot):
    rows, tile_x, ny, nz = courant.shape
    zs = lax.axis_size("zz")
    slab = ny // lax.axis_size("shot")
    planes = tile_x // QUAD
    hbm = pl.BlockSpec(memory_space=pltpu.HBM)
    vmem = pl.BlockSpec(memory_space=pltpu.VMEM)
    parts, inner, outer, swap, keep = pl.pallas_call(
        split_kernel,
        out_shape=[hbm32(zs, tile_x, slab, nz)]
        + [hbm32(2 * REACH, ny, nz)] * 2
        + [f32(2, planes, slab, nz)] * 2,
        in_specs=[pl.BlockSpec(memory_space=pltpu.SMEM), hbm, hbm, hbm],
        out_specs=[hbm, hbm, hbm, vmem, vmem],
        scratch_shapes=[
            pltpu.VMEM((rows, tile_x, slab, nz), jnp.float32),
            pltpu.SemaphoreType.DMA((zs + 5,)),
        ],
        compiler_params=pltpu.CompilerParams(vmem_limit_bytes=VMEM_LIMIT),
        name="split",
    )(spot, in_hbm(courant), in_hbm(u), in_hbm(w))
    return parts.reshape(zs * QUAD, planes, slab, nz), inner, outer, keep, swap


def model_parts(line, extras, table, spot):
    slots = lax.axis_size("shot") * QUAD
    smem = pl.BlockSpec(memory_space=pltpu.SMEM)
    anywhere = pl.BlockSpec(memory_space=pl.ANY)
    return pl.pallas_call(
        functools.partial(gather_kernel, lax.axis_size("zz")),
        out_shape=hbm32(slots, *line.shape[1:]),
        in_specs=[smem, smem] + [anywhere] * 4,
        out_specs=pl.BlockSpec(memory_space=pltpu.HBM),
        scratch_shapes=[pltpu.SemaphoreType.DMA((slots,))],
        compiler_params=pltpu.CompilerParams(vmem_limit_bytes=1 << 20),
        name="gather",
    )(table, spot, line, *extras)


def return_image(image, table, spot):
    shots, tile_x, slab, nz = image.shape
    zs = lax.axis_size("zz")
    planes = tile_x // QUAD
    got = exchange(image.reshape(shots * QUAD, planes, slab, nz), PLANE)
    smem = pl.BlockSpec(memory_space=pltpu.SMEM)
    vmem = pl.BlockSpec(memory_space=pltpu.VMEM)
    line, keep, swap = pl.pallas_call(
        functools.partial(scatter_kernel, zs),
        out_shape=[hbm32(zs * QUAD, planes, slab, nz)] + [f32(2, planes, slab, nz)] * 2,
        in_specs=[smem, smem, vmem],
        out_specs=[pl.BlockSpec(memory_space=pltpu.HBM), vmem, vmem],
        scratch_shapes=[
            pltpu.VMEM((zs * QUAD, planes, slab, nz), jnp.float32),
            pltpu.SemaphoreType.DMA((1,)),
        ],
        compiler_params=pltpu.CompilerParams(vmem_limit_bytes=VMEM_LIMIT),
        name="scatter",
    )(table, spot, got)
    came = exchange(line, MP)
    extras = quad_relay(keep, swap)
    (out,) = local_kernel(
        functools.partial(finish_kernel, zs),
        [spot],
        [came, *extras],
        [f32(2, tile_x, slab, nz)],
    )
    return out


def edges(n, ints, now, back, drive, speed):
    _, ny, nz = now.shape
    hbm = pl.BlockSpec(memory_space=pltpu.HBM)
    vmem = pl.BlockSpec(memory_space=pltpu.VMEM)
    return pl.pallas_call(
        functools.partial(edges_kernel, n),
        out_shape=[f32(REACH, ny, nz)] * 2,
        in_specs=[pl.BlockSpec(memory_space=pltpu.SMEM), hbm, hbm, hbm, vmem],
        out_specs=[vmem, vmem],
        scratch_shapes=[
            pltpu.VMEM((3, 2, REACH, ny, nz), jnp.float32),
            pltpu.SemaphoreType.DMA((3, 2)),
        ],
        compiler_params=pltpu.CompilerParams(vmem_limit_bytes=VMEM_LIMIT),
    )(ints, in_hbm(now), in_hbm(back), in_hbm(drive), speed)


def halos(inner, outer):
    count = lax.axis_size(MP)
    across = [(i, i + 1) for i in range(1, count - 1, 2)]
    return (
        lax.ppermute(inner, MP, [(i, i ^ 1) for i in range(count)]),
        lax.ppermute(outer, MP, across + [(j, i) for i, j in across]),
    )


def window(
    courant,
    aperture_first,
    source_pos,
    wavelet,
    receiver_pos,
    residual,
    step_count,
    forward_prev,
    forward_now,
    adjoint_prev,
    adjoint_now,
):
    tile_x, ny, nz = forward_now.shape[1:]
    steps = wavelet.shape[1]
    receivers = receiver_pos.shape[1]
    spot = [lax.axis_index(name) for name in ("shot", "zz", "quad")]
    spot = jnp.stack(spot).astype(jnp.int32)
    u, w = forward_now[0], adjoint_now[0]
    parts, inner, outer, keep, swap = open_moves(courant, u, w, spot)
    sides = halos(inner, outer)
    line = exchange(parts, MP)
    extras = quad_relay(keep, swap)
    table = all_first(aperture_first[0])
    me_index = lax.axis_index(MP)
    even = me_index % 2 == 0
    base = (me_index * tile_x).reshape(1).astype(jnp.int32)
    ints = jnp.concatenate(
        [
            step_count,
            base,
            even.reshape(1).astype(jnp.int32),
            source_pos[0],
            receiver_pos[0].reshape(-1),
        ]
    )
    floats = jnp.concatenate([wavelet[0], residual[0].reshape(-1)])
    field = f32(tile_x, ny, nz)
    edge = f32(REACH, ny, nz)
    padded = pltpu.VMEM((nz // LANES, tile_x, ny + 2 * SUB, LANES), jnp.float32)
    along = pltpu.VMEM((tile_x, ny, nz), jnp.float32)
    scalars = [ints, floats]
    drives = []
    hbm = pl.BlockSpec(memory_space=pltpu.HBM)
    vmem = pl.BlockSpec(memory_space=pltpu.VMEM)
    smem = pl.BlockSpec(memory_space=pltpu.SMEM)
    drive, push = pl.pallas_call(
        functools.partial(first_kernel, steps, receivers),
        out_shape=[hbm32(tile_x, ny, nz)] * 2,
        in_specs=[smem, smem] + [vmem] * 4,
        out_specs=[hbm, hbm],
        scratch_shapes=[along, along, padded, pltpu.SemaphoreType.DMA((2,))],
        compiler_params=pltpu.CompilerParams(vmem_limit_bytes=VMEM_LIMIT),
        name="first",
    )(*scalars, u, w, *sides)
    sent = model_parts(line, extras, table, spot)
    sent, drive, push = lax.optimization_barrier((sent, drive, push))
    owned = exchange(sent, PLANE).reshape(-1, tile_x, SUB, nz)
    drives.append(drive)
    before_u = (0, ints, u, forward_prev[0], drive, owned)
    before_w = (steps - 1, ints, w, adjoint_prev[0], push, owned)
    u_sides = halos(*edges(before_u[0], *before_u[1:]))
    w_sides = halos(*edges(before_w[0], *before_w[1:]))
    backs = []
    for n in range(1, steps):
        last = n == steps - 1
        state = [u, forward_prev[0], drive] if n == 1 else [u, vu]
        drive, *moved = local_kernel(
            functools.partial(forward_kernel, n, last),
            scalars,
            [*state, owned, *u_sides],
            [field] if last else [field, field, field, edge, edge],
            [padded, along],
        )
        drives.append(drive)
        if not last:
            u, vu, inner, outer = moved
            u_sides = halos(inner, outer)
        extra_in = []
        if last:
            pairs = []
            for k in range(steps - 1):
                pairs += [backs[k], drives[steps - 1 - k]]
            (partial,) = local_kernel(
                functools.partial(products_kernel, steps - 1), [], pairs, [field]
            )
            extra_in = [partial, drives[0]]
        state = [w, adjoint_prev[0], push] if n == 1 else [w, vw]
        outs = [field, field, edge, edge]
        if n == 1:
            outs = [field] + outs
        moved = local_kernel(
            functools.partial(adjoint_kernel, steps, receivers, steps - 1 - n, last),
            scalars,
            [*state, owned, *w_sides, *extra_in],
            [f32(ny // SUB, tile_x, SUB, nz)] if last else outs,
            [padded, along],
        )
        if not last:
            *opened, w, vw, inner, outer = moved
            w_sides = halos(inner, outer)
            backs += [*opened, w]
    return return_image(moved[0], table, spot)


def solution(mesh):
    shots, mp = mesh.devices.shape
    fine = Mesh(mesh.devices.reshape(shots, mp // QUAD, QUAD), ("shot", "zz", "quad"))
    return jax.shard_map(
        window,
        mesh=fine,
        in_specs=(
            P(None, MP, None, None),
            P("shot"),
            P("shot", None),
            P("shot", None),
            P("shot", None, None),
            P("shot", None, None),
            P("shot"),
            P("shot", MP, None, None),
            P("shot", MP, None, None),
            P("shot", MP, None, None),
            P("shot", MP, None, None),
        ),
        out_specs=P(None, MP, "shot", None),
        check_vma=False,
    )
```

```python
import functools

import jax
import jax.numpy as jnp
from jax import lax
from jax.experimental import pallas as pl
from jax.experimental.pallas import tpu as pltpu
from jax.sharding import Mesh, PartitionSpec as P


COEF = (-205.0 / 72.0, 1.6, -0.2, 8.0 / 315.0, -1.0 / 560.0)
QUAD = 4
MP = ("zz", "quad")
PLANE = ("shot", "quad")
LANES = 128
SUB = 8
REACH = 4
COUNT, BASE, EVEN, SOURCE, RECEIVERS = 0, 1, 2, 3, 6
NEAR = 12
VMEM_LIMIT = 16 << 20


def all_first(first):
    shots = lax.axis_size("shot")
    me = lax.axis_index("shot")
    known = jnp.where(jnp.arange(shots, dtype=jnp.int32) == me, first, 0)
    step = 1
    while step < shots:
        known = known + lax.ppermute(known, "shot", [(i, i ^ step) for i in range(shots)])
        step *= 2
    return known


def f32(*shape):
    return jax.ShapeDtypeStruct(shape, jnp.float32)


def hbm32(*shape):
    return pltpu.HBM(shape, jnp.float32)


def local_kernel(body, scalars, arrays, outs, scratch=(), aliases=None):
    vmem = pl.BlockSpec(memory_space=pltpu.VMEM)
    smem = pl.BlockSpec(memory_space=pltpu.SMEM)
    return pl.pallas_call(
        body,
        out_shape=outs,
        in_specs=[smem] * len(scalars) + [vmem] * len(arrays),
        out_specs=[vmem] * len(outs),
        scratch_shapes=list(scratch),
        input_output_aliases=aliases or {},
        compiler_params=pltpu.CompilerParams(vmem_limit_bytes=VMEM_LIMIT),
    )(*scalars, *arrays)


def in_hbm(value):
    return pltpu.with_memory_space_constraint(value, pltpu.HBM)


def band_matrix(nz):
    rows = lax.broadcasted_iota(jnp.int32, (nz, nz), 0)
    cols = lax.broadcasted_iota(jnp.int32, (nz, nz), 1)
    apart = jnp.abs(rows - cols)
    band = jnp.where(apart == 0, 3.0 * COEF[0], 0.0)
    for k in range(1, REACH + 1):
        band = jnp.where(apart == k, COEF[k], band)
    return band


def prepare(field, padded, along_z):
    xs, ys, nz = field.shape
    along_z[...] = jnp.dot(
        field[...].reshape(xs * ys, nz),
        band_matrix(nz),
        precision=lax.Precision.HIGHEST,
        preferred_element_type=jnp.float32,
    ).reshape(xs, ys, nz)
    edge = jnp.zeros((xs, SUB, LANES), jnp.float32)
    for h in range(nz // LANES):
        padded[h, :, 0:SUB, :] = edge
        padded[h, :, SUB + ys : SUB + ys + SUB, :] = edge
        padded[h, :, SUB : SUB + ys, :] = field[:, :, h * LANES : (h + 1) * LANES]


def add_point(target, x, y, z, amount):
    xs, _, nz = target.shape

    @pl.when((x >= 0) & (x < xs))
    def _():
        cells = lax.broadcasted_iota(jnp.int32, (1, 1, nz), 2)
        place = (pl.ds(x, 1), pl.ds(y, 1), slice(None))
        target[place] = target[place] + jnp.where(cells == z, amount, 0.0)


def add_source(target, ints, floats, n):
    x = ints[SOURCE] - ints[BASE]
    add_point(target, x, ints[SOURCE + 1], ints[SOURCE + 2], floats[n])


def add_receivers(target, ints, floats, steps, receivers, n):
    xs = target.shape[0]
    away = ints[SOURCE] - ints[BASE]

    @pl.when((away + NEAR >= 0) & (away - NEAR < xs))
    def _():
        def one(j, carry):
            at = RECEIVERS + 3 * j
            amount = floats[steps + n * receivers + j]
            add_point(target, ints[at] - ints[BASE], ints[at + 1], ints[at + 2], amount)
            return carry

        lax.fori_loop(0, receivers, one, 0)


def laplacian(padded, along_z, even, inner, outer, y0, h, plane=0):
    xs = along_z.shape[0]
    rows = pl.ds(y0, SUB)
    lanes = slice(h * LANES, (h + 1) * LANES)
    if inner is None:
        before = after = [None] * REACH
    else:
        near = [inner[plane + j, rows, lanes] for j in range(REACH)]
        far = [outer[plane + j, rows, lanes] for j in range(REACH)]
        before = [jnp.where(even, far[j], near[j]) for j in range(REACH)]
        after = [jnp.where(even, near[j], far[j]) for j in range(REACH)]
    column = before + [padded[h, x, pl.ds(y0 + SUB, SUB), :] for x in range(xs)] + after
    for x in range(xs):
        total = along_z[x, rows, lanes]
        for k in range(1, REACH + 1):
            pair = (
                padded[h, x, pl.ds(y0 + SUB + k, SUB), :]
                + padded[h, x, pl.ds(y0 + SUB - k, SUB), :]
            )
            for other in (column[x + REACH + k], column[x + REACH - k]):
                if other is not None:
                    pair = pair + other
            total = total + COEF[k] * pair
        yield x, column[x + REACH], total


def each_block(field, work):
    _, ys, nz = field.shape

    def step(i, carry):
        y0 = pl.multiple_of(i * SUB, SUB)
        for h in range(nz // LANES):
            work(i, y0, h, slice(h * LANES, (h + 1) * LANES))
        return carry

    lax.fori_loop(0, ys // SUB, step, 0)


def switch_on(ints, n):
    return jnp.where(ints[COUNT] > n, 1.0, 0.0).astype(jnp.float32)


def first_kernel(steps, receivers, ints, floats, u, w, near, far, d, e, along_u, along_w, pad, sems):
    even = ints[EVEN] == 1
    copies = []
    for k, (field, along, out) in enumerate(((u, along_u, d), (w, along_w, e))):
        prepare(field, pad, along)
        if k == 0:
            add_source(along, ints, floats, 0)
            live = switch_on(ints, 0)
        else:
            add_receivers(along, ints, floats, steps, receivers, steps - 1)
            live = switch_on(ints, steps - 1)

        def work(i, y0, h, lanes):
            rows = pl.ds(y0, SUB)
            for x, _, total in laplacian(pad, along, even, near, far, y0, h, k * REACH):
                along[x, rows, lanes] = live * total

        each_block(field, work)
        copy = pltpu.make_async_copy(along, out, sems.at[k])
        copy.start()
        copies.append(copy)
    for copy in copies:
        copy.wait()


def edge_out(even, field, inner, outer):
    xs = field.shape[0]

    @pl.when(even)
    def _():
        inner[...] = field[xs - REACH :]
        outer[...] = field[:REACH]

    @pl.when(jnp.logical_not(even))
    def _():
        inner[...] = field[:REACH]
        outer[...] = field[xs - REACH :]


def edges_kernel(steps, ints, *refs):
    fields, speed = (refs[0:3], refs[3:6]), refs[6]
    outs, held, sems = (refs[7:9], refs[9:11]), refs[11], refs[12]
    xs, ys, _ = refs[0].shape
    even = ints[EVEN] == 1
    starts = (0, xs - REACH)
    copies = [
        pltpu.make_async_copy(
            source.at[pl.ds(x0, REACH)], held.at[f, k, side], sems.at[f, k, side]
        )
        for f in range(2)
        for k, source in enumerate(fields[f])
        for side, x0 in enumerate(starts)
    ]
    for copy in copies:
        copy.start()
    for f in range(2):
        live = switch_on(ints, 0 if f == 0 else steps - 1)
        for copy in copies[6 * f : 6 * f + 6]:
            copy.wait()

        def step(i, carry):
            rows = pl.ds(pl.multiple_of(i * SUB, SUB), SUB)
            for side, x0 in enumerate(starts):
                for j in range(REACH):
                    here = held[f, 0, side, j, rows, :]
                    more = (here - held[f, 1, side, j, rows, :]) + speed[i, x0 + j] * held[
                        f, 2, side, j, rows, :
                    ]
                    held[f, 0, side, j, rows, :] = here + live * more
            return carry

        lax.fori_loop(0, ys // SUB, step, 0)
        inner, outer = outs[f]

        @pl.when(even)
        def _():
            inner[...] = held[f, 0, 1]
            outer[...] = held[f, 0, 0]

        @pl.when(jnp.logical_not(even))
        def _():
            inner[...] = held[f, 0, 0]
            outer[...] = held[f, 0, 1]


def opening(ints, n, now, back, drive, speed, new, gain):
    live = switch_on(ints, n)

    def work(i, y0, h, lanes):
        rows = pl.ds(y0, SUB)
        for x in range(now.shape[0]):
            here = now[x, rows, lanes]
            more = (here - back[x, rows, lanes]) + speed[i, x, :, lanes] * drive[x, rows, lanes]
            gain[x, rows, lanes] = more
            new[x, rows, lanes] = here + live * more

    each_block(now, work)


def forward_kernel(n, last, ints, floats, *refs):
    if n == 1:
        u0, back, drive0, p, near, far, drive, new, gain, inner, outer, pad, along = refs
        opening(ints, 0, u0, back, drive0, p, new, gain)
        u, vu = new, gain
    elif last:
        u, vu, p, near, far, drive, pad, along = refs
    else:
        u, vu, p, near, far, drive, new, gain, inner, outer, pad, along = refs
    prepare(u, pad, along)
    add_source(along, ints, floats, n)
    live = switch_on(ints, n)
    even = ints[EVEN] == 1

    def work(i, y0, h, lanes):
        rows = pl.ds(y0, SUB)
        for x, here, total in laplacian(pad, along, even, near, far, y0, h):
            total = live * total
            drive[x, rows, lanes] = total
            if last:
                continue
            more = vu[x, rows, lanes] + p[i, x, :, lanes] * total
            gain[x, rows, lanes] = more
            new[x, rows, lanes] = here + more

    each_block(u, work)
    if not last:
        edge_out(even, new, inner, outer)


def adjoint_kernel(steps, receivers, n, ints, floats, *refs):
    if n == steps - 2:
        w0, back, push, p, near, far, w, new, gain, inner, outer, pad, along = refs
        opening(ints, steps - 1, w0, back, push, p, w, gain)
        vw = gain
    else:
        w, vw, p, near, far, new, gain, inner, outer, pad, along = refs
    prepare(w, pad, along)
    add_receivers(along, ints, floats, steps, receivers, n)
    live = switch_on(ints, n)
    even = ints[EVEN] == 1

    def work(i, y0, h, lanes):
        rows = pl.ds(y0, SUB)
        for x, here, total in laplacian(pad, along, even, near, far, y0, h):
            more = vw[x, rows, lanes] + (live * p[i, x, :, lanes]) * total
            gain[x, rows, lanes] = more
            new[x, rows, lanes] = here + live * more

    each_block(w, work)
    edge_out(even, new, inner, outer)


def last_inner_kernel(steps, receivers, ints, floats, w, vw, p, partial, drive, image, open_sum, pad, along):
    xs = w.shape[0]
    prepare(w, pad, along)
    add_receivers(along, ints, floats, steps, receivers, 0)
    live = switch_on(ints, 0)

    def work(i, y0, h, lanes):
        rows = pl.ds(y0, SUB)
        for x, here, total in laplacian(pad, along, None, None, None, y0, h):
            if x < REACH or x >= xs - REACH:
                open_sum[x if x < REACH else x + 2 * REACH - xs, rows, lanes] = total
                continue
            more = vw[x, rows, lanes] + (live * p[i, x, :, lanes]) * total
            here = here + live * more
            image[i, x, :, lanes] = partial[x, rows, lanes] + here * drive[x, rows, lanes]

    each_block(w, work)


def last_outer_kernel(ints, w, vw, p, partial, drive, open_sum, near, far, inside, image):
    del inside
    xs = w.shape[0]
    live = switch_on(ints, 0)
    even = ints[EVEN] == 1

    def work(i, y0, h, lanes):
        rows = pl.ds(y0, SUB)
        a = [near[j, rows, lanes] for j in range(REACH)]
        b = [far[j, rows, lanes] for j in range(REACH)]
        before = [jnp.where(even, b[j], a[j]) for j in range(REACH)]
        after = [jnp.where(even, a[j], b[j]) for j in range(REACH)]
        for side in range(2 * REACH):
            x = side if side < REACH else side + xs - 2 * REACH
            total = open_sum[side, rows, lanes]
            for k in range(1, REACH + 1):
                if x - k < 0:
                    total = total + COEF[k] * before[REACH + x - k]
                if x + k >= xs:
                    total = total + COEF[k] * after[x + k - xs]
            more = vw[x, rows, lanes] + (live * p[i, x, :, lanes]) * total
            here = w[x, rows, lanes] + live * more
            image[i, x, :, lanes] = partial[x, rows, lanes] + here * drive[x, rows, lanes]

    each_block(w, work)


def products_kernel(pairs, *refs):
    out = refs[-1]

    def work(i, y0, h, lanes):
        rows = pl.ds(y0, SUB)
        for x in range(out.shape[0]):
            total = refs[0][x, rows, lanes] * refs[1][x, rows, lanes]
            for j in range(1, pairs):
                total = total + refs[2 * j][x, rows, lanes] * refs[2 * j + 1][x, rows, lanes]
            out[x, rows, lanes] = total

    each_block(out, work)


def split_kernel(spot, courant, u, w, parts, inner, outer, swap, keep, slab_in, sides, sems):
    zs = parts.shape[0]
    _, tile_x, slab, _ = slab_in.shape
    planes = tile_x // QUAD
    me_shot, me_z, me_q = spot[0], spot[1], spot[2]
    rows = pl.ds(pl.multiple_of(me_shot * slab, SUB), slab)
    first = jnp.where(me_q % 2 == 0, tile_x - REACH, 0)
    loads = []
    for side in range(2):
        x0 = first if side == 0 else tile_x - REACH - first
        for k, field in enumerate((u, w)):
            loads.append(
                pltpu.make_async_copy(
                    field.at[pl.ds(x0, REACH)],
                    sides.at[side, pl.ds(k * REACH, REACH)],
                    sems.at[2 * side + k],
                )
            )
    loads.append(pltpu.make_async_copy(courant.at[:, :, rows, :], slab_in, sems.at[4]))
    for load in loads:
        load.start()
    stores = []
    for side, out in enumerate((inner, outer)):
        loads[2 * side].wait()
        loads[2 * side + 1].wait()
        stores.append(pltpu.make_async_copy(sides.at[side], out, sems.at[5 + side]))
        stores[-1].start()
    loads[4].wait()
    for z in range(zs):
        row = jnp.where(z <= me_z, 0, 1)
        stores.append(pltpu.make_async_copy(slab_in.at[row], parts.at[z], sems.at[7 + z]))
        stores[-1].start()
    for k, turn in enumerate((0, 2)):
        keep[k] = slab_in[1, pl.ds((me_q ^ turn) * planes, planes)]
        swap[k] = slab_in[1, pl.ds((me_q ^ turn ^ 1) * planes, planes)]
    for store in stores:
        store.wait()


def relay_kernel(keep, swapped, out):
    out[0] = keep[1]
    out[1] = swapped[1]


def gather_kernel(zs, table, spot, line, keep, swapped, far, sent, sems):
    slots = sent.shape[0]
    me_z, me_q = spot[1], spot[2]

    def one(slot, carry):
        tile = table[slot // QUAD] + slot % QUAD
        place = ((me_z + tile // QUAD) % zs) * QUAD + tile % QUAD
        turn = me_q ^ (tile % QUAD)

        def send(source):
            pltpu.make_async_copy(source, sent.at[slot], sems.at[slot]).start()

        @pl.when(tile < zs * QUAD)
        def _():
            send(line.at[place])

        @pl.when(tile >= zs * QUAD)
        def _():
            @pl.when(turn == 0)
            def _():
                send(keep.at[0])

            @pl.when(turn == 1)
            def _():
                send(swapped.at[0])

            @pl.when(turn > 1)
            def _():
                send(far.at[turn - 2])

        return carry

    lax.fori_loop(0, slots, one, 0)

    def done(slot, carry):
        pltpu.make_async_copy(line.at[0], sent.at[slot], sems.at[slot]).wait()
        return carry

    lax.fori_loop(0, slots, done, 0)


def scatter_kernel(zs, table, spot, got, line, keep, swap, held, sems):
    me_z, me_q = spot[1], spot[2]
    held[...] = jnp.zeros_like(held)

    def one(s, carry):
        place = pl.ds(table[s], QUAD)
        held[place] = held[place] + got[pl.ds(s * QUAD, QUAD)]
        return carry

    lax.fori_loop(0, got.shape[0] // QUAD, one, 0)
    copies = []
    for j in range(zs):
        to = ((me_z + j) % zs) * QUAD
        copies.append(
            pltpu.make_async_copy(
                held.at[pl.ds(j * QUAD, QUAD)], line.at[pl.ds(to, QUAD)], sems.at[j]
            )
        )
        copies[-1].start()
    for k, turn in enumerate((0, 2)):
        keep[k] = held[zs * QUAD + (me_q ^ turn)]
        swap[k] = held[zs * QUAD + (me_q ^ turn ^ 1)]
    for copy in copies:
        copy.wait()


def finish_kernel(zs, spot, came, keep, swapped, far, out):
    planes = came.shape[1]
    me_z, me_q = spot[1], spot[2]
    extras = (keep[0], swapped[0], far[0], far[1])
    for turn in range(QUAD):
        q = me_q ^ turn
        low = came[q]
        high = extras[turn]
        for z in range(1, zs):
            value = came[z * QUAD + q]
            low = low + jnp.where(z <= me_z, value, 0.0)
            high = high + jnp.where(z <= me_z, 0.0, value)
        out[0, pl.ds(q * planes, planes)] = low
        out[1, pl.ds(q * planes, planes)] = high


def exchange(parts, axes):
    return lax.all_to_all(parts, axes, split_axis=0, concat_axis=0, tiled=True)


def swap_quads(value, turn):
    return lax.ppermute(value, "quad", [(q, q ^ turn) for q in range(QUAD)])


def quad_relay(keep, swap):
    swapped = swap_quads(swap, 1)
    (far,) = local_kernel(relay_kernel, [], [keep, swapped], [f32(*keep.shape)])
    return keep, swapped, swap_quads(far, 2)


def open_moves(courant, u, w, spot):
    rows, tile_x, ny, nz = courant.shape
    zs = lax.axis_size("zz")
    slab = ny // lax.axis_size("shot")
    planes = tile_x // QUAD
    hbm = pl.BlockSpec(memory_space=pltpu.HBM)
    vmem = pl.BlockSpec(memory_space=pltpu.VMEM)
    parts, inner, outer, swap, keep = pl.pallas_call(
        split_kernel,
        out_shape=[hbm32(zs, tile_x, slab, nz)]
        + [hbm32(2 * REACH, ny, nz)] * 2
        + [f32(2, planes, slab, nz)] * 2,
        in_specs=[pl.BlockSpec(memory_space=pltpu.SMEM), hbm, hbm, hbm],
        out_specs=[hbm, hbm, hbm, vmem, vmem],
        scratch_shapes=[
            pltpu.VMEM((rows, tile_x, slab, nz), jnp.float32),
            pltpu.VMEM((2, 2 * REACH, ny, nz), jnp.float32),
            pltpu.SemaphoreType.DMA((zs + 7,)),
        ],
        compiler_params=pltpu.CompilerParams(vmem_limit_bytes=VMEM_LIMIT),
        name="split",
    )(spot, in_hbm(courant), in_hbm(u), in_hbm(w))
    return parts.reshape(zs * QUAD, planes, slab, nz), inner, outer, keep, swap


def model_parts(line, extras, table, spot):
    slots = lax.axis_size("shot") * QUAD
    smem = pl.BlockSpec(memory_space=pltpu.SMEM)
    anywhere = pl.BlockSpec(memory_space=pl.ANY)
    return pl.pallas_call(
        functools.partial(gather_kernel, lax.axis_size("zz")),
        out_shape=hbm32(slots, *line.shape[1:]),
        in_specs=[smem, smem] + [anywhere] * 4,
        out_specs=pl.BlockSpec(memory_space=pltpu.HBM),
        scratch_shapes=[pltpu.SemaphoreType.DMA((slots,))],
        compiler_params=pltpu.CompilerParams(vmem_limit_bytes=1 << 20),
        name="gather",
    )(table, spot, line, *extras)


def return_image(image, table, spot):
    shots, tile_x, slab, nz = image.shape
    zs = lax.axis_size("zz")
    planes = tile_x // QUAD
    got = exchange(image.reshape(shots * QUAD, planes, slab, nz), PLANE)
    smem = pl.BlockSpec(memory_space=pltpu.SMEM)
    vmem = pl.BlockSpec(memory_space=pltpu.VMEM)
    line, keep, swap = pl.pallas_call(
        functools.partial(scatter_kernel, zs),
        out_shape=[hbm32(zs * QUAD, planes, slab, nz)] + [f32(2, planes, slab, nz)] * 2,
        in_specs=[smem, smem, vmem],
        out_specs=[pl.BlockSpec(memory_space=pltpu.HBM), vmem, vmem],
        scratch_shapes=[
            pltpu.VMEM(((zs + 1) * QUAD, planes, slab, nz), jnp.float32),
            pltpu.SemaphoreType.DMA((zs,)),
        ],
        compiler_params=pltpu.CompilerParams(vmem_limit_bytes=VMEM_LIMIT),
        name="scatter",
    )(table, spot, got)
    came = exchange(line, MP)
    extras = quad_relay(keep, swap)
    (out,) = local_kernel(
        functools.partial(finish_kernel, zs), [spot], [came, *extras], [f32(2, tile_x, slab, nz)]
    )
    return out


def edges(steps, ints, forward, adjoint, speed):
    _, ny, nz = forward[0].shape
    hbm = pl.BlockSpec(memory_space=pltpu.HBM)
    vmem = pl.BlockSpec(memory_space=pltpu.VMEM)
    return pl.pallas_call(
        functools.partial(edges_kernel, steps),
        out_shape=[f32(REACH, ny, nz)] * 4,
        in_specs=[pl.BlockSpec(memory_space=pltpu.SMEM)] + [hbm] * 6 + [vmem],
        out_specs=[vmem] * 4,
        scratch_shapes=[
            pltpu.VMEM((2, 3, 2, REACH, ny, nz), jnp.float32),
            pltpu.SemaphoreType.DMA((2, 3, 2)),
        ],
        compiler_params=pltpu.CompilerParams(vmem_limit_bytes=VMEM_LIMIT),
        name="edges",
    )(ints, *map(in_hbm, forward), *map(in_hbm, adjoint), speed)


def halos(inner, outer):
    count = lax.axis_size(MP)
    across = [(i, i + 1) for i in range(1, count - 1, 2)]
    return (
        lax.ppermute(inner, MP, [(i, i ^ 1) for i in range(count)]),
        lax.ppermute(outer, MP, across + [(j, i) for i, j in across]),
    )


def window(
    courant,
    aperture_first,
    source_pos,
    wavelet,
    receiver_pos,
    residual,
    step_count,
    forward_prev,
    forward_now,
    adjoint_prev,
    adjoint_now,
):
    tile_x, ny, nz = forward_now.shape[1:]
    steps = wavelet.shape[1]
    receivers = receiver_pos.shape[1]
    spot = [lax.axis_index(name) for name in ("shot", "zz", "quad")]
    spot = jnp.stack(spot).astype(jnp.int32)
    u, w = forward_now[0], adjoint_now[0]
    parts, inner, outer, keep, swap = open_moves(courant, u, w, spot)
    sides = halos(inner, outer)
    line = exchange(parts, MP)
    extras = quad_relay(keep, swap)
    table = all_first(aperture_first[0])
    me_index = lax.axis_index(MP)
    even = me_index % 2 == 0
    base = (me_index * tile_x).reshape(1).astype(jnp.int32)
    ints = jnp.concatenate(
        [
            step_count,
            base,
            even.reshape(1).astype(jnp.int32),
            source_pos[0],
            receiver_pos[0].reshape(-1),
        ]
    )
    floats = jnp.concatenate([wavelet[0], residual[0].reshape(-1)])
    field = f32(tile_x, ny, nz)
    edge = f32(REACH, ny, nz)
    padded = pltpu.VMEM((nz // LANES, tile_x, ny + 2 * SUB, LANES), jnp.float32)
    along = pltpu.VMEM((tile_x, ny, nz), jnp.float32)
    scalars = [ints, floats]
    drives = []
    hbm = pl.BlockSpec(memory_space=pltpu.HBM)
    vmem = pl.BlockSpec(memory_space=pltpu.VMEM)
    smem = pl.BlockSpec(memory_space=pltpu.SMEM)
    drive, push = pl.pallas_call(
        functools.partial(first_kernel, steps, receivers),
        out_shape=[hbm32(tile_x, ny, nz)] * 2,
        in_specs=[smem, smem] + [vmem] * 4,
        out_specs=[hbm, hbm],
        scratch_shapes=[along, along, padded, pltpu.SemaphoreType.DMA((2,))],
        compiler_params=pltpu.CompilerParams(vmem_limit_bytes=VMEM_LIMIT),
        name="first",
    )(*scalars, u, w, *sides)
    sent = model_parts(line, extras, table, spot)
    sent, drive, push = lax.optimization_barrier((sent, drive, push))
    owned = exchange(sent, PLANE).reshape(-1, tile_x, SUB, nz)
    drives.append(drive)
    openings = edges(
        steps, ints, (u, forward_prev[0], drive), (w, adjoint_prev[0], push), owned
    )
    u_sides = halos(*openings[:2])
    w_sides = halos(*openings[2:])
    backs = []
    for n in range(1, steps):
        last = n == steps - 1
        state = [u, forward_prev[0], drive] if n == 1 else [u, vu]
        drive, *moved = local_kernel(
            functools.partial(forward_kernel, n, last),
            scalars,
            [*state, owned, *u_sides],
            [field] if last else [field, field, field, edge, edge],
            [padded, along],
        )
        drives.append(drive)
        if not last:
            u, vu, inner, outer = moved
            u_sides = halos(inner, outer)
        if last:
            break
        state = [w, adjoint_prev[0], push] if n == 1 else [w, vw]
        outs = [field, field, edge, edge]
        if n == 1:
            outs = [field] + outs
        *opened, w, vw, inner, outer = local_kernel(
            functools.partial(adjoint_kernel, steps, receivers, steps - 1 - n),
            scalars,
            [*state, owned, *w_sides],
            outs,
            [padded, along],
        )
        w_sides = halos(inner, outer)
        backs += [*opened, w]
    pairs = []
    for k in range(steps - 1):
        pairs += [backs[k], drives[steps - 1 - k]]
    (partial,) = local_kernel(functools.partial(products_kernel, steps - 1), [], pairs, [field])
    state = [w, vw, owned, partial, drives[0]]
    whole = f32(ny // SUB, tile_x, SUB, nz)
    image, open_sum = local_kernel(
        functools.partial(last_inner_kernel, steps, receivers),
        scalars,
        state,
        [whole, f32(2 * REACH, ny, nz)],
        [padded, along],
    )
    (image,) = local_kernel(
        last_outer_kernel, [ints], [*state, open_sum, *w_sides, image], [whole], aliases={9: 0}
    )
    return return_image(image, table, spot)


def solution(mesh):
    shots, mp = mesh.devices.shape
    fine = Mesh(mesh.devices.reshape(shots, mp // QUAD, QUAD), ("shot", "zz", "quad"))
    return jax.shard_map(
        window,
        mesh=fine,
        in_specs=(
            P(None, MP, None, None),
            P("shot"),
            P("shot", None),
            P("shot", None),
            P("shot", None, None),
            P("shot", None, None),
            P("shot"),
            P("shot", MP, None, None),
            P("shot", MP, None, None),
            P("shot", MP, None, None),
            P("shot", MP, None, None),
        ),
        out_specs=P(None, MP, "shot", None),
        check_vma=False,
    )
```

```python
import functools

import jax
import jax.numpy as jnp
from jax import lax
from jax.experimental import pallas as pl
from jax.experimental.pallas import tpu as pltpu
from jax.sharding import Mesh, PartitionSpec as P


COEF = (-205.0 / 72.0, 1.6, -0.2, 8.0 / 315.0, -1.0 / 560.0)
WHOLE = (8064.0, -1008.0, 128.0, -9.0)
SCALE = 5040.0
QUAD = 4
MP = ("zz", "quad")
PLANE = ("shot", "quad")
LANES = 128
SUB = 8
REACH = 4
COUNT, BASE, EVEN, SOURCE, RECEIVERS = 0, 1, 2, 3, 6
NEAR = 12
VMEM_LIMIT = 16 << 20


def all_first(first):
    shots = lax.axis_size("shot")
    me = lax.axis_index("shot")
    known = jnp.where(jnp.arange(shots, dtype=jnp.int32) == me, first, 0)
    step = 1
    while step < shots:
        known = known + lax.ppermute(known, "shot", [(i, i ^ step) for i in range(shots)])
        step *= 2
    return known


def f32(*shape):
    return jax.ShapeDtypeStruct(shape, jnp.float32)


def hbm32(*shape):
    return pltpu.HBM(shape, jnp.float32)


def local_kernel(body, scalars, arrays, outs, scratch=(), aliases=None):
    vmem = pl.BlockSpec(memory_space=pltpu.VMEM)
    smem = pl.BlockSpec(memory_space=pltpu.SMEM)
    return pl.pallas_call(
        body,
        out_shape=outs,
        in_specs=[smem] * len(scalars) + [vmem] * len(arrays),
        out_specs=[vmem] * len(outs),
        scratch_shapes=list(scratch),
        input_output_aliases=aliases or {},
        compiler_params=pltpu.CompilerParams(vmem_limit_bytes=VMEM_LIMIT),
    )(*scalars, *arrays)


def in_hbm(value):
    return pltpu.with_memory_space_constraint(value, pltpu.HBM)


def band_matrix(nz):
    rows = lax.broadcasted_iota(jnp.int32, (nz, nz), 0)
    cols = lax.broadcasted_iota(jnp.int32, (nz, nz), 1)
    apart = jnp.abs(rows - cols)
    band = jnp.zeros((nz, nz), jnp.float32)
    for k in range(1, REACH + 1):
        band = jnp.where(apart == k, WHOLE[k - 1], band)
    return band.astype(jnp.bfloat16)


def prepare(field, padded, along_z):
    xs, ys, nz = field.shape
    band = band_matrix(nz)

    def times_band(part):
        return jnp.dot(part, band, preferred_element_type=jnp.float32)

    for x in range(0, xs, REACH):
        value = field[x : x + REACH].reshape(REACH * ys, nz)
        high = value.astype(jnp.bfloat16)
        rest = value - high.astype(jnp.float32)
        middle = rest.astype(jnp.bfloat16)
        low = (rest - middle.astype(jnp.float32)).astype(jnp.bfloat16)
        total = (times_band(low) + times_band(middle)) + times_band(high)
        total = total * (1.0 / SCALE) + (3.0 * COEF[0]) * value
        along_z[x : x + REACH] = total.reshape(REACH, ys, nz)
    edge = jnp.zeros((xs, SUB, LANES), jnp.float32)
    for h in range(nz // LANES):
        padded[h, :, 0:SUB, :] = edge
        padded[h, :, SUB + ys : SUB + ys + SUB, :] = edge
        padded[h, :, SUB : SUB + ys, :] = field[:, :, h * LANES : (h + 1) * LANES]


def add_point(target, x, y, z, amount):
    xs, _, nz = target.shape

    @pl.when((x >= 0) & (x < xs))
    def _():
        cells = lax.broadcasted_iota(jnp.int32, (1, 1, nz), 2)
        place = (pl.ds(x, 1), pl.ds(y, 1), slice(None))
        target[place] = target[place] + jnp.where(cells == z, amount, 0.0)


def whole(scalars, at):
    return scalars[at].astype(jnp.int32)


def is_even(scalars):
    return scalars[EVEN] > 0.5


def add_source(target, receivers, scalars, n):
    x = whole(scalars, SOURCE) - whole(scalars, BASE)
    amount = scalars[RECEIVERS + 3 * receivers + n]
    add_point(target, x, whole(scalars, SOURCE + 1), whole(scalars, SOURCE + 2), amount)


def add_receivers(target, scalars, steps, receivers, n):
    xs = target.shape[0]
    base = whole(scalars, BASE)
    away = whole(scalars, SOURCE) - base
    amounts = RECEIVERS + 3 * receivers + steps + n * receivers

    @pl.when((away + NEAR >= 0) & (away - NEAR < xs))
    def _():
        def one(j, carry):
            at = RECEIVERS + 3 * j
            x = whole(scalars, at) - base
            y, z = whole(scalars, at + 1), whole(scalars, at + 2)
            add_point(target, x, y, z, scalars[amounts + j])
            return carry

        lax.fori_loop(0, receivers, one, 0)


def laplacian(padded, along_z, even, inner, outer, y0, h, plane=0):
    xs = along_z.shape[0]
    rows = pl.ds(y0, SUB)
    lanes = slice(h * LANES, (h + 1) * LANES)
    if inner is None:
        before = after = [None] * REACH
    else:
        near = [inner[plane + j, rows, lanes] for j in range(REACH)]
        far = [outer[plane + j, rows, lanes] for j in range(REACH)]
        before = [jnp.where(even, far[j], near[j]) for j in range(REACH)]
        after = [jnp.where(even, near[j], far[j]) for j in range(REACH)]
    column = before + [padded[h, x, pl.ds(y0 + SUB, SUB), :] for x in range(xs)] + after
    for x in range(xs):
        total = along_z[x, rows, lanes]
        for k in range(1, REACH + 1):
            pair = (
                padded[h, x, pl.ds(y0 + SUB + k, SUB), :]
                + padded[h, x, pl.ds(y0 + SUB - k, SUB), :]
            )
            for other in (column[x + REACH + k], column[x + REACH - k]):
                if other is not None:
                    pair = pair + other
            total = total + COEF[k] * pair
        yield x, column[x + REACH], total


def each_block(field, work):
    _, ys, nz = field.shape

    def step(i, carry):
        y0 = pl.multiple_of(i * SUB, SUB)
        for h in range(nz // LANES):
            work(i, y0, h, slice(h * LANES, (h + 1) * LANES))
        return carry

    lax.fori_loop(0, ys // SUB, step, 0)


def switch_on(scalars, n):
    return jnp.where(scalars[COUNT] > n + 0.5, 1.0, 0.0).astype(jnp.float32)


def first_kernel(steps, receivers, scalars, u, w, near, far, d, e, along_u, along_w, pad, sems):
    even = is_even(scalars)
    copies = []
    for k, (field, along, out) in enumerate(((u, along_u, d), (w, along_w, e))):
        prepare(field, pad, along)
        if k == 0:
            add_source(along, receivers, scalars, 0)
            live = switch_on(scalars, 0)
        else:
            add_receivers(along, scalars, steps, receivers, steps - 1)
            live = switch_on(scalars, steps - 1)

        def work(i, y0, h, lanes):
            rows = pl.ds(y0, SUB)
            for x, _, total in laplacian(pad, along, even, near, far, y0, h, k * REACH):
                along[x, rows, lanes] = live * total

        each_block(field, work)
        copy = pltpu.make_async_copy(along, out, sems.at[k])
        copy.start()
        copies.append(copy)
    for copy in copies:
        copy.wait()


def edge_out(even, field, inner, outer):
    xs = field.shape[0]

    @pl.when(even)
    def _():
        inner[...] = field[xs - REACH :]
        outer[...] = field[:REACH]

    @pl.when(jnp.logical_not(even))
    def _():
        inner[...] = field[:REACH]
        outer[...] = field[xs - REACH :]


def edges_kernel(steps, scalars, *refs):
    fields, speed = (refs[0:3], refs[3:6]), refs[6]
    outs, held, sems = (refs[7:9], refs[9:11]), refs[11], refs[12]
    xs, ys, _ = refs[0].shape
    even = is_even(scalars)
    starts = (0, xs - REACH)
    copies = [
        pltpu.make_async_copy(
            source.at[pl.ds(x0, REACH)], held.at[f, k, side], sems.at[f, k, side]
        )
        for f in range(2)
        for k, source in enumerate(fields[f])
        for side, x0 in enumerate(starts)
    ]
    for copy in copies:
        copy.start()
    for f in range(2):
        live = switch_on(scalars, 0 if f == 0 else steps - 1)
        for copy in copies[6 * f : 6 * f + 6]:
            copy.wait()

        def step(i, carry):
            rows = pl.ds(pl.multiple_of(i * SUB, SUB), SUB)
            for side, x0 in enumerate(starts):
                for j in range(REACH):
                    here = held[f, 0, side, j, rows, :]
                    more = (here - held[f, 1, side, j, rows, :]) + speed[i, x0 + j] * held[
                        f, 2, side, j, rows, :
                    ]
                    held[f, 0, side, j, rows, :] = here + live * more
            return carry

        lax.fori_loop(0, ys // SUB, step, 0)
        inner, outer = outs[f]

        @pl.when(even)
        def _():
            inner[...] = held[f, 0, 1]
            outer[...] = held[f, 0, 0]

        @pl.when(jnp.logical_not(even))
        def _():
            inner[...] = held[f, 0, 0]
            outer[...] = held[f, 0, 1]


def opening(scalars, n, now, back, drive, speed, new, gain):
    live = switch_on(scalars, n)

    def work(i, y0, h, lanes):
        rows = pl.ds(y0, SUB)
        for x in range(now.shape[0]):
            here = now[x, rows, lanes]
            more = (here - back[x, rows, lanes]) + speed[i, x, :, lanes] * drive[x, rows, lanes]
            gain[x, rows, lanes] = more
            new[x, rows, lanes] = here + live * more

    each_block(now, work)


def forward_kernel(receivers, n, last, scalars, *refs):
    if n == 1:
        u0, back, drive0, p, near, far, drive, new, gain, inner, outer, pad, along = refs
        opening(scalars, 0, u0, back, drive0, p, new, gain)
        u, vu = new, gain
    elif last:
        u, vu, p, near, far, drive, pad, along = refs
    else:
        u, vu, p, near, far, drive, new, gain, inner, outer, pad, along = refs
    prepare(u, pad, along)
    add_source(along, receivers, scalars, n)
    live = switch_on(scalars, n)
    even = is_even(scalars)

    def work(i, y0, h, lanes):
        rows = pl.ds(y0, SUB)
        for x, here, total in laplacian(pad, along, even, near, far, y0, h):
            total = live * total
            drive[x, rows, lanes] = total
            if last:
                continue
            more = vu[x, rows, lanes] + p[i, x, :, lanes] * total
            gain[x, rows, lanes] = more
            new[x, rows, lanes] = here + more

    each_block(u, work)
    if not last:
        edge_out(even, new, inner, outer)


def adjoint_kernel(steps, receivers, n, scalars, *refs):
    if n == steps - 2:
        w0, back, push, p, near, far, w, new, gain, inner, outer, pad, along = refs
        opening(scalars, steps - 1, w0, back, push, p, w, gain)
        vw = gain
    else:
        w, vw, p, near, far, new, gain, inner, outer, pad, along = refs
    prepare(w, pad, along)
    add_receivers(along, scalars, steps, receivers, n)
    live = switch_on(scalars, n)
    even = is_even(scalars)

    def work(i, y0, h, lanes):
        rows = pl.ds(y0, SUB)
        for x, here, total in laplacian(pad, along, even, near, far, y0, h):
            more = vw[x, rows, lanes] + (live * p[i, x, :, lanes]) * total
            gain[x, rows, lanes] = more
            new[x, rows, lanes] = here + live * more

    each_block(w, work)
    edge_out(even, new, inner, outer)


def last_inner_kernel(steps, receivers, scalars, w, vw, p, partial, drive, image, open_sum, pad, along):
    xs = w.shape[0]
    prepare(w, pad, along)
    add_receivers(along, scalars, steps, receivers, 0)
    live = switch_on(scalars, 0)

    def work(i, y0, h, lanes):
        rows = pl.ds(y0, SUB)
        for x, here, total in laplacian(pad, along, None, None, None, y0, h):
            if x < REACH or x >= xs - REACH:
                open_sum[x if x < REACH else x + 2 * REACH - xs, rows, lanes] = total
                continue
            more = vw[x, rows, lanes] + (live * p[i, x, :, lanes]) * total
            here = here + live * more
            image[i, x, :, lanes] = partial[x, rows, lanes] + here * drive[x, rows, lanes]

    each_block(w, work)


def last_outer_kernel(scalars, w, vw, p, partial, drive, open_sum, near, far, inside, image):
    del inside
    xs = w.shape[0]
    live = switch_on(scalars, 0)
    even = is_even(scalars)

    def work(i, y0, h, lanes):
        rows = pl.ds(y0, SUB)
        a = [near[j, rows, lanes] for j in range(REACH)]
        b = [far[j, rows, lanes] for j in range(REACH)]
        before = [jnp.where(even, b[j], a[j]) for j in range(REACH)]
        after = [jnp.where(even, a[j], b[j]) for j in range(REACH)]
        for side in range(2 * REACH):
            x = side if side < REACH else side + xs - 2 * REACH
            total = open_sum[side, rows, lanes]
            for k in range(1, REACH + 1):
                if x - k < 0:
                    total = total + COEF[k] * before[REACH + x - k]
                if x + k >= xs:
                    total = total + COEF[k] * after[x + k - xs]
            more = vw[x, rows, lanes] + (live * p[i, x, :, lanes]) * total
            here = w[x, rows, lanes] + live * more
            image[i, x, :, lanes] = partial[x, rows, lanes] + here * drive[x, rows, lanes]

    each_block(w, work)


def products_kernel(pairs, *refs):
    out = refs[-1]

    def work(i, y0, h, lanes):
        rows = pl.ds(y0, SUB)
        for x in range(out.shape[0]):
            total = refs[0][x, rows, lanes] * refs[1][x, rows, lanes]
            for j in range(1, pairs):
                total = total + refs[2 * j][x, rows, lanes] * refs[2 * j + 1][x, rows, lanes]
            out[x, rows, lanes] = total

    each_block(out, work)


def split_kernel(spot, courant, u, w, parts, inner, outer, swap, keep, slab_in, sides, sems):
    zs = parts.shape[0]
    _, tile_x, slab, _ = slab_in.shape
    planes = tile_x // QUAD
    me_shot, me_z, me_q = spot[0], spot[1], spot[2]
    rows = pl.ds(pl.multiple_of(me_shot * slab, SUB), slab)
    first = jnp.where(me_q % 2 == 0, tile_x - REACH, 0)
    loads = []
    for side in range(2):
        x0 = first if side == 0 else tile_x - REACH - first
        for k, field in enumerate((u, w)):
            loads.append(
                pltpu.make_async_copy(
                    field.at[pl.ds(x0, REACH)],
                    sides.at[side, pl.ds(k * REACH, REACH)],
                    sems.at[2 * side + k],
                )
            )
    loads.append(pltpu.make_async_copy(courant.at[:, :, rows, :], slab_in, sems.at[4]))
    for load in loads:
        load.start()
    stores = []
    for side, out in enumerate((inner, outer)):
        loads[2 * side].wait()
        loads[2 * side + 1].wait()
        stores.append(pltpu.make_async_copy(sides.at[side], out, sems.at[5 + side]))
        stores[-1].start()
    loads[4].wait()
    for z in range(zs):
        row = jnp.where(z <= me_z, 0, 1)
        stores.append(pltpu.make_async_copy(slab_in.at[row], parts.at[z], sems.at[7 + z]))
        stores[-1].start()
    for k, turn in enumerate((0, 2)):
        keep[k] = slab_in[1, pl.ds((me_q ^ turn) * planes, planes)]
        swap[k] = slab_in[1, pl.ds((me_q ^ turn ^ 1) * planes, planes)]
    for store in stores:
        store.wait()


def relay_kernel(keep, swapped, out):
    out[0] = keep[1]
    out[1] = swapped[1]


def gather_kernel(zs, table, line, keep, swapped, far, sent, sems):
    slots = sent.shape[0]
    me_z, me_q = table[table.shape[0] - 2], table[table.shape[0] - 1]

    def one(slot, carry):
        tile = table[slot // QUAD] + slot % QUAD
        place = ((me_z + tile // QUAD) % zs) * QUAD + tile % QUAD
        turn = me_q ^ (tile % QUAD)

        def send(source):
            pltpu.make_async_copy(source, sent.at[slot], sems.at[slot]).start()

        @pl.when(tile < zs * QUAD)
        def _():
            send(line.at[place])

        @pl.when(tile >= zs * QUAD)
        def _():
            @pl.when(turn == 0)
            def _():
                send(keep.at[0])

            @pl.when(turn == 1)
            def _():
                send(swapped.at[0])

            @pl.when(turn > 1)
            def _():
                send(far.at[turn - 2])

        return carry

    lax.fori_loop(0, slots, one, 0)

    def done(slot, carry):
        pltpu.make_async_copy(line.at[0], sent.at[slot], sems.at[slot]).wait()
        return carry

    lax.fori_loop(0, slots, done, 0)


def scatter_kernel(zs, table, got, line, keep, swap, held, sems):
    me_z, me_q = table[table.shape[0] - 2], table[table.shape[0] - 1]
    held[...] = jnp.zeros_like(held)

    def one(s, carry):
        place = pl.ds(table[s], QUAD)
        held[place] = held[place] + got[pl.ds(s * QUAD, QUAD)]
        return carry

    lax.fori_loop(0, got.shape[0] // QUAD, one, 0)
    copies = []
    for j in range(zs):
        to = ((me_z + j) % zs) * QUAD
        copies.append(
            pltpu.make_async_copy(
                held.at[pl.ds(j * QUAD, QUAD)], line.at[pl.ds(to, QUAD)], sems.at[j]
            )
        )
        copies[-1].start()
    for k, turn in enumerate((0, 2)):
        keep[k] = held[zs * QUAD + (me_q ^ turn)]
        swap[k] = held[zs * QUAD + (me_q ^ turn ^ 1)]
    for copy in copies:
        copy.wait()


def finish_kernel(zs, table, came, keep, swapped, far, out):
    planes = came.shape[1]
    me_z, me_q = table[table.shape[0] - 2], table[table.shape[0] - 1]
    extras = (keep[0], swapped[0], far[0], far[1])
    for turn in range(QUAD):
        q = me_q ^ turn
        low = came[q]
        high = extras[turn]
        for z in range(1, zs):
            value = came[z * QUAD + q]
            low = low + jnp.where(z <= me_z, value, 0.0)
            high = high + jnp.where(z <= me_z, 0.0, value)
        out[0, pl.ds(q * planes, planes)] = low
        out[1, pl.ds(q * planes, planes)] = high


def exchange(parts, axes):
    return lax.all_to_all(parts, axes, split_axis=0, concat_axis=0, tiled=True)


def swap_quads(value, turn):
    return lax.ppermute(value, "quad", [(q, q ^ turn) for q in range(QUAD)])


def quad_relay(keep, swap):
    swapped = swap_quads(swap, 1)
    (far,) = local_kernel(relay_kernel, [], [keep, swapped], [f32(*keep.shape)])
    return keep, swapped, swap_quads(far, 2)


def open_moves(courant, u, w, spot):
    rows, tile_x, ny, nz = courant.shape
    zs = lax.axis_size("zz")
    slab = ny // lax.axis_size("shot")
    planes = tile_x // QUAD
    hbm = pl.BlockSpec(memory_space=pltpu.HBM)
    vmem = pl.BlockSpec(memory_space=pltpu.VMEM)
    parts, inner, outer, swap, keep = pl.pallas_call(
        split_kernel,
        out_shape=[hbm32(zs, tile_x, slab, nz)]
        + [hbm32(2 * REACH, ny, nz)] * 2
        + [f32(2, planes, slab, nz)] * 2,
        in_specs=[pl.BlockSpec(memory_space=pltpu.SMEM), hbm, hbm, hbm],
        out_specs=[hbm, hbm, hbm, vmem, vmem],
        scratch_shapes=[
            pltpu.VMEM((rows, tile_x, slab, nz), jnp.float32),
            pltpu.VMEM((2, 2 * REACH, ny, nz), jnp.float32),
            pltpu.SemaphoreType.DMA((zs + 7,)),
        ],
        compiler_params=pltpu.CompilerParams(vmem_limit_bytes=VMEM_LIMIT),
        name="split",
    )(spot, in_hbm(courant), in_hbm(u), in_hbm(w))
    return parts.reshape(zs * QUAD, planes, slab, nz), inner, outer, keep, swap


def model_parts(line, extras, table):
    slots = lax.axis_size("shot") * QUAD
    smem = pl.BlockSpec(memory_space=pltpu.SMEM)
    anywhere = pl.BlockSpec(memory_space=pl.ANY)
    return pl.pallas_call(
        functools.partial(gather_kernel, lax.axis_size("zz")),
        out_shape=hbm32(slots, *line.shape[1:]),
        in_specs=[smem] + [anywhere] * 4,
        out_specs=pl.BlockSpec(memory_space=pltpu.HBM),
        scratch_shapes=[pltpu.SemaphoreType.DMA((slots,))],
        compiler_params=pltpu.CompilerParams(vmem_limit_bytes=1 << 20),
        name="gather",
    )(table, line, *extras)


def return_image(image, table):
    shots, tile_x, slab, nz = image.shape
    zs = lax.axis_size("zz")
    planes = tile_x // QUAD
    got = exchange(image.reshape(shots * QUAD, planes, slab, nz), PLANE)
    smem = pl.BlockSpec(memory_space=pltpu.SMEM)
    vmem = pl.BlockSpec(memory_space=pltpu.VMEM)
    line, keep, swap = pl.pallas_call(
        functools.partial(scatter_kernel, zs),
        out_shape=[hbm32(zs * QUAD, planes, slab, nz)] + [f32(2, planes, slab, nz)] * 2,
        in_specs=[smem, vmem],
        out_specs=[pl.BlockSpec(memory_space=pltpu.HBM), vmem, vmem],
        scratch_shapes=[
            pltpu.VMEM(((zs + 1) * QUAD, planes, slab, nz), jnp.float32),
            pltpu.SemaphoreType.DMA((zs,)),
        ],
        compiler_params=pltpu.CompilerParams(vmem_limit_bytes=VMEM_LIMIT),
        name="scatter",
    )(table, got)
    came = exchange(line, MP)
    extras = quad_relay(keep, swap)
    (out,) = local_kernel(
        functools.partial(finish_kernel, zs), [table], [came, *extras], [f32(2, tile_x, slab, nz)]
    )
    return out


def edges(steps, scalars, forward, adjoint, speed):
    _, ny, nz = forward[0].shape
    hbm = pl.BlockSpec(memory_space=pltpu.HBM)
    vmem = pl.BlockSpec(memory_space=pltpu.VMEM)
    return pl.pallas_call(
        functools.partial(edges_kernel, steps),
        out_shape=[f32(REACH, ny, nz)] * 4,
        in_specs=[pl.BlockSpec(memory_space=pltpu.SMEM)] + [hbm] * 6 + [vmem],
        out_specs=[vmem] * 4,
        scratch_shapes=[
            pltpu.VMEM((2, 3, 2, REACH, ny, nz), jnp.float32),
            pltpu.SemaphoreType.DMA((2, 3, 2)),
        ],
        compiler_params=pltpu.CompilerParams(vmem_limit_bytes=VMEM_LIMIT),
        name="edges",
    )(scalars, *map(in_hbm, forward), *map(in_hbm, adjoint), speed)


def halos(inner, outer):
    count = lax.axis_size(MP)
    across = [(i, i + 1) for i in range(1, count - 1, 2)]
    return (
        lax.ppermute(inner, MP, [(i, i ^ 1) for i in range(count)]),
        lax.ppermute(outer, MP, across + [(j, i) for i, j in across]),
    )


def window(
    courant,
    aperture_first,
    source_pos,
    wavelet,
    receiver_pos,
    residual,
    step_count,
    forward_prev,
    forward_now,
    adjoint_prev,
    adjoint_now,
):
    tile_x, ny, nz = forward_now.shape[1:]
    steps = wavelet.shape[1]
    receivers = receiver_pos.shape[1]
    spot = [lax.axis_index(name) for name in ("shot", "zz", "quad")]
    spot = jnp.stack(spot).astype(jnp.int32)
    u, w = forward_now[0], adjoint_now[0]
    parts, inner, outer, keep, swap = open_moves(courant, u, w, spot)
    sides = halos(inner, outer)
    line = exchange(parts, MP)
    extras = quad_relay(keep, swap)
    table = jnp.concatenate([all_first(aperture_first[0]), spot])
    me_index = lax.axis_index(MP)
    even = me_index % 2 == 0
    base = (me_index * tile_x).reshape(1).astype(jnp.int32)
    scalars = jnp.concatenate(
        [
            step_count.astype(jnp.float32),
            base.astype(jnp.float32),
            even.reshape(1).astype(jnp.float32),
            source_pos[0].astype(jnp.float32),
            receiver_pos[0].reshape(-1).astype(jnp.float32),
            wavelet[0],
            residual[0].reshape(-1),
        ]
    )
    field = f32(tile_x, ny, nz)
    edge = f32(REACH, ny, nz)
    padded = pltpu.VMEM((nz // LANES, tile_x, ny + 2 * SUB, LANES), jnp.float32)
    along = pltpu.VMEM((tile_x, ny, nz), jnp.float32)
    drives = []
    hbm = pl.BlockSpec(memory_space=pltpu.HBM)
    vmem = pl.BlockSpec(memory_space=pltpu.VMEM)
    smem = pl.BlockSpec(memory_space=pltpu.SMEM)
    drive, push = pl.pallas_call(
        functools.partial(first_kernel, steps, receivers),
        out_shape=[hbm32(tile_x, ny, nz)] * 2,
        in_specs=[smem] + [vmem] * 4,
        out_specs=[hbm, hbm],
        scratch_shapes=[along, along, padded, pltpu.SemaphoreType.DMA((2,))],
        compiler_params=pltpu.CompilerParams(vmem_limit_bytes=VMEM_LIMIT),
        name="first",
    )(scalars, u, w, *sides)
    sent = model_parts(line, extras, table)
    sent, drive, push = lax.optimization_barrier((sent, drive, push))
    owned = exchange(sent, PLANE).reshape(-1, tile_x, SUB, nz)
    drives.append(drive)
    openings = edges(
        steps, scalars, (u, forward_prev[0], drive), (w, adjoint_prev[0], push), owned
    )
    u_sides = halos(*openings[:2])
    w_sides = halos(*openings[2:])
    backs = []
    for n in range(1, steps):
        last = n == steps - 1
        state = [u, forward_prev[0], drive] if n == 1 else [u, vu]
        drive, *moved = local_kernel(
            functools.partial(forward_kernel, receivers, n, last),
            [scalars],
            [*state, owned, *u_sides],
            [field] if last else [field, field, field, edge, edge],
            [padded, along],
        )
        drives.append(drive)
        if not last:
            u, vu, inner, outer = moved
            u_sides = halos(inner, outer)
        if last:
            break
        state = [w, adjoint_prev[0], push] if n == 1 else [w, vw]
        outs = [field, field, edge, edge]
        if n == 1:
            outs = [field] + outs
        *opened, w, vw, inner, outer = local_kernel(
            functools.partial(adjoint_kernel, steps, receivers, steps - 1 - n),
            [scalars],
            [*state, owned, *w_sides],
            outs,
            [padded, along],
        )
        w_sides = halos(inner, outer)
        backs += [*opened, w]
    pairs = []
    for k in range(steps - 1):
        pairs += [backs[k], drives[steps - 1 - k]]
    (partial,) = local_kernel(functools.partial(products_kernel, steps - 1), [], pairs, [field])
    state = [w, vw, owned, partial, drives[0]]
    whole = f32(ny // SUB, tile_x, SUB, nz)
    image, open_sum = local_kernel(
        functools.partial(last_inner_kernel, steps, receivers),
        [scalars],
        state,
        [whole, f32(2 * REACH, ny, nz)],
        [padded, along],
    )
    (image,) = local_kernel(
        last_outer_kernel, [scalars], [*state, open_sum, *w_sides, image], [whole], aliases={9: 0}
    )
    return return_image(image, table)


def solution(mesh):
    shots, mp = mesh.devices.shape
    fine = Mesh(mesh.devices.reshape(shots, mp // QUAD, QUAD), ("shot", "zz", "quad"))
    return jax.shard_map(
        window,
        mesh=fine,
        in_specs=(
            P(None, MP, None, None),
            P("shot"),
            P("shot", None),
            P("shot", None),
            P("shot", None, None),
            P("shot", None, None),
            P("shot"),
            P("shot", MP, None, None),
            P("shot", MP, None, None),
            P("shot", MP, None, None),
            P("shot", MP, None, None),
        ),
        out_specs=P(None, MP, "shot", None),
        check_vma=False,
    )
```

```python
import functools

import jax
import jax.numpy as jnp
from jax import lax
from jax.experimental import pallas as pl
from jax.experimental.pallas import tpu as pltpu
from jax.sharding import Mesh, PartitionSpec as P


COEF = (-205.0 / 72.0, 1.6, -0.2, 8.0 / 315.0, -1.0 / 560.0)
WHOLE = (8064.0, -1008.0, 128.0, -9.0)
SCALE = 5040.0
QUAD = 4
MP = ("zz", "quad")
PLANE = ("shot", "quad")
LANES = 128
SUB = 8
REACH = 4
COUNT, BASE, EVEN, SOURCE, RECEIVERS = 0, 1, 2, 3, 6
NEAR = 12
VMEM_LIMIT = 16 << 20


def all_first(first):
    shots = lax.axis_size("shot")
    me = lax.axis_index("shot")
    known = jnp.where(jnp.arange(shots, dtype=jnp.int32) == me, first, 0)
    step = 1
    while step < shots:
        known = known + lax.ppermute(known, "shot", [(i, i ^ step) for i in range(shots)])
        step *= 2
    return known


def f32(*shape):
    return jax.ShapeDtypeStruct(shape, jnp.float32)


def hbm32(*shape):
    return pltpu.HBM(shape, jnp.float32)


def local_kernel(body, scalars, arrays, outs, scratch=(), aliases=None):
    vmem = pl.BlockSpec(memory_space=pltpu.VMEM)
    smem = pl.BlockSpec(memory_space=pltpu.SMEM)
    return pl.pallas_call(
        body,
        out_shape=outs,
        in_specs=[smem] * len(scalars) + [vmem] * len(arrays),
        out_specs=[vmem] * len(outs),
        scratch_shapes=list(scratch),
        input_output_aliases=aliases or {},
        compiler_params=pltpu.CompilerParams(vmem_limit_bytes=VMEM_LIMIT),
    )(*scalars, *arrays)


def in_hbm(value):
    return pltpu.with_memory_space_constraint(value, pltpu.HBM)


def band_matrix(nz):
    rows = lax.broadcasted_iota(jnp.int32, (nz, nz), 0)
    cols = lax.broadcasted_iota(jnp.int32, (nz, nz), 1)
    apart = jnp.abs(rows - cols)
    band = jnp.zeros((nz, nz), jnp.float32)
    for k in range(1, REACH + 1):
        band = jnp.where(apart == k, WHOLE[k - 1], band)
    return band.astype(jnp.bfloat16)


def prepare(field, padded, along_z):
    xs, ys, nz = field.shape
    band = band_matrix(nz)

    def times_band(part):
        return jnp.dot(part, band, preferred_element_type=jnp.float32)

    for x in range(0, xs, REACH):
        value = field[x : x + REACH].reshape(REACH * ys, nz)
        high = value.astype(jnp.bfloat16)
        rest = value - high.astype(jnp.float32)
        middle = rest.astype(jnp.bfloat16)
        low = (rest - middle.astype(jnp.float32)).astype(jnp.bfloat16)
        total = (times_band(low) + times_band(middle)) + times_band(high)
        total = total * (1.0 / SCALE) + (3.0 * COEF[0]) * value
        along_z[x : x + REACH] = total.reshape(REACH, ys, nz)
    edge = jnp.zeros((xs, SUB, LANES), jnp.float32)
    for h in range(nz // LANES):
        padded[h, :, 0:SUB, :] = edge
        padded[h, :, SUB + ys : SUB + ys + SUB, :] = edge
        padded[h, :, SUB : SUB + ys, :] = field[:, :, h * LANES : (h + 1) * LANES]


def add_point(target, x, y, z, amount):
    xs, _, nz = target.shape

    @pl.when((x >= 0) & (x < xs))
    def _():
        cells = lax.broadcasted_iota(jnp.int32, (1, 1, nz), 2)
        place = (pl.ds(x, 1), pl.ds(y, 1), slice(None))
        target[place] = target[place] + jnp.where(cells == z, amount, 0.0)


def whole(scalars, at):
    return scalars[at].astype(jnp.int32)


def is_even(scalars):
    return scalars[EVEN] > 0.5


def add_source(target, receivers, scalars, n):
    x = whole(scalars, SOURCE) - whole(scalars, BASE)
    amount = scalars[RECEIVERS + receivers + n]
    add_point(target, x, whole(scalars, SOURCE + 1), whole(scalars, SOURCE + 2), amount)


def add_receivers(target, scalars, steps, receivers, n):
    xs, ys, nz = target.shape
    base = whole(scalars, BASE)
    away = whole(scalars, SOURCE) - base
    amounts = RECEIVERS + receivers + steps + n * receivers
    z_bits = nz.bit_length() - 1
    x_bits = z_bits + ys.bit_length() - 1

    @pl.when((away + NEAR >= 0) & (away - NEAR < xs))
    def _():
        def one(j, carry):
            cell = whole(scalars, RECEIVERS + j)
            x, y = (cell >> x_bits) - base, (cell >> z_bits) & (ys - 1)
            add_point(target, x, y, cell & (nz - 1), scalars[amounts + j])
            return carry

        lax.fori_loop(0, receivers, one, 0)


def laplacian(padded, along_z, even, inner, outer, y0, h, plane=0):
    xs = along_z.shape[0]
    rows = pl.ds(y0, SUB)
    lanes = slice(h * LANES, (h + 1) * LANES)
    if inner is None:
        before = after = [None] * REACH
    else:
        near = [inner[plane + j, rows, lanes] for j in range(REACH)]
        far = [outer[plane + j, rows, lanes] for j in range(REACH)]
        before = [jnp.where(even, far[j], near[j]) for j in range(REACH)]
        after = [jnp.where(even, near[j], far[j]) for j in range(REACH)]
    column = before + [padded[h, x, pl.ds(y0 + SUB, SUB), :] for x in range(xs)] + after
    for x in range(xs):
        total = along_z[x, rows, lanes]
        for k in range(1, REACH + 1):
            pair = (
                padded[h, x, pl.ds(y0 + SUB + k, SUB), :]
                + padded[h, x, pl.ds(y0 + SUB - k, SUB), :]
            )
            for other in (column[x + REACH + k], column[x + REACH - k]):
                if other is not None:
                    pair = pair + other
            total = total + COEF[k] * pair
        yield x, column[x + REACH], total


def each_block(field, work):
    _, ys, nz = field.shape

    def step(i, carry):
        y0 = pl.multiple_of(i * SUB, SUB)
        for h in range(nz // LANES):
            work(i, y0, h, slice(h * LANES, (h + 1) * LANES))
        return carry

    lax.fori_loop(0, ys // SUB, step, 0)


def switch_on(scalars, n):
    return jnp.where(scalars[COUNT] > n + 0.5, 1.0, 0.0).astype(jnp.float32)


def first_kernel(steps, receivers, scalars, u, w, near, far, d, e, along_u, along_w, pad, sems):
    even = is_even(scalars)
    copies = []
    for k, (field, along, out) in enumerate(((u, along_u, d), (w, along_w, e))):
        prepare(field, pad, along)
        if k == 0:
            add_source(along, receivers, scalars, 0)
            live = switch_on(scalars, 0)
        else:
            add_receivers(along, scalars, steps, receivers, steps - 1)
            live = switch_on(scalars, steps - 1)

        def work(i, y0, h, lanes):
            rows = pl.ds(y0, SUB)
            for x, _, total in laplacian(pad, along, even, near, far, y0, h, k * REACH):
                along[x, rows, lanes] = live * total

        each_block(field, work)
        copy = pltpu.make_async_copy(along, out, sems.at[k])
        copy.start()
        copies.append(copy)
    for copy in copies:
        copy.wait()


def edge_out(even, field, inner, outer):
    xs = field.shape[0]

    @pl.when(even)
    def _():
        inner[...] = field[xs - REACH :]
        outer[...] = field[:REACH]

    @pl.when(jnp.logical_not(even))
    def _():
        inner[...] = field[:REACH]
        outer[...] = field[xs - REACH :]


def edges_kernel(n, scalars, now, back, drive, speed, inner, outer, held, sems):
    xs, ys, _ = now.shape
    even = is_even(scalars)
    live = switch_on(scalars, n)
    starts = (0, xs - REACH)
    copies = [
        pltpu.make_async_copy(source.at[pl.ds(x0, REACH)], held.at[k, side], sems.at[k, side])
        for side, x0 in enumerate(starts)
        for k, source in enumerate((now, back, drive))
    ]
    for copy in copies:
        copy.start()
    for side, x0 in enumerate(starts):
        for copy in copies[3 * side : 3 * side + 3]:
            copy.wait()
        ahead = even if side == 1 else jnp.logical_not(even)

        def update(out):
            def step(i, carry):
                rows = pl.ds(pl.multiple_of(i * SUB, SUB), SUB)
                for j in range(REACH):
                    here = held[0, side, j, rows, :]
                    more = (here - held[1, side, j, rows, :]) + speed[i, x0 + j] * held[
                        2, side, j, rows, :
                    ]
                    out[j, rows, :] = here + live * more
                return carry

            lax.fori_loop(0, ys // SUB, step, 0)

        @pl.when(ahead)
        def _():
            update(inner)

        @pl.when(jnp.logical_not(ahead))
        def _():
            update(outer)


def opening(scalars, n, now, back, drive, speed, new, gain):
    live = switch_on(scalars, n)

    def work(i, y0, h, lanes):
        rows = pl.ds(y0, SUB)
        for x in range(now.shape[0]):
            here = now[x, rows, lanes]
            more = (here - back[x, rows, lanes]) + speed[i, x, :, lanes] * drive[x, rows, lanes]
            gain[x, rows, lanes] = more
            new[x, rows, lanes] = here + live * more

    each_block(now, work)


def forward_kernel(receivers, n, last, scalars, *refs):
    if n == 1:
        u0, back, drive0, p, near, far, drive, new, gain, inner, outer, pad, along = refs
        opening(scalars, 0, u0, back, drive0, p, new, gain)
        u, vu = new, gain
    elif last:
        u, vu, p, near, far, drive, pad, along = refs
    else:
        u, vu, p, near, far, drive, new, gain, inner, outer, pad, along = refs
    prepare(u, pad, along)
    add_source(along, receivers, scalars, n)
    live = switch_on(scalars, n)
    even = is_even(scalars)

    def work(i, y0, h, lanes):
        rows = pl.ds(y0, SUB)
        for x, here, total in laplacian(pad, along, even, near, far, y0, h):
            total = live * total
            drive[x, rows, lanes] = total
            if last:
                continue
            more = vu[x, rows, lanes] + p[i, x, :, lanes] * total
            gain[x, rows, lanes] = more
            new[x, rows, lanes] = here + more

    each_block(u, work)
    if not last:
        edge_out(even, new, inner, outer)


def adjoint_kernel(steps, receivers, n, scalars, *refs):
    if n == steps - 2:
        w0, back, push, p, near, far, w, new, gain, inner, outer, pad, along = refs
        opening(scalars, steps - 1, w0, back, push, p, w, gain)
        vw = gain
    else:
        w, vw, p, near, far, new, gain, inner, outer, pad, along = refs
    prepare(w, pad, along)
    add_receivers(along, scalars, steps, receivers, n)
    live = switch_on(scalars, n)
    even = is_even(scalars)

    def work(i, y0, h, lanes):
        rows = pl.ds(y0, SUB)
        for x, here, total in laplacian(pad, along, even, near, far, y0, h):
            more = vw[x, rows, lanes] + (live * p[i, x, :, lanes]) * total
            gain[x, rows, lanes] = more
            new[x, rows, lanes] = here + live * more

    each_block(w, work)
    edge_out(even, new, inner, outer)


def last_inner_kernel(steps, receivers, scalars, w, vw, p, partial, drive, image, open_sum, pad, along):
    xs = w.shape[0]
    prepare(w, pad, along)
    add_receivers(along, scalars, steps, receivers, 0)
    live = switch_on(scalars, 0)

    def work(i, y0, h, lanes):
        rows = pl.ds(y0, SUB)
        for x, here, total in laplacian(pad, along, None, None, None, y0, h):
            if x < REACH or x >= xs - REACH:
                open_sum[x if x < REACH else x + 2 * REACH - xs, rows, lanes] = total
                continue
            more = vw[x, rows, lanes] + (live * p[i, x, :, lanes]) * total
            here = here + live * more
            image[i, x, :, lanes] = partial[x, rows, lanes] + here * drive[x, rows, lanes]

    each_block(w, work)


def last_outer_kernel(scalars, w, vw, p, partial, drive, open_sum, near, far, inside, image):
    del inside
    xs = w.shape[0]
    live = switch_on(scalars, 0)
    even = is_even(scalars)

    def work(i, y0, h, lanes):
        rows = pl.ds(y0, SUB)
        a = [near[j, rows, lanes] for j in range(REACH)]
        b = [far[j, rows, lanes] for j in range(REACH)]
        before = [jnp.where(even, b[j], a[j]) for j in range(REACH)]
        after = [jnp.where(even, a[j], b[j]) for j in range(REACH)]
        for side in range(2 * REACH):
            x = side if side < REACH else side + xs - 2 * REACH
            total = open_sum[side, rows, lanes]
            for k in range(1, REACH + 1):
                if x - k < 0:
                    total = total + COEF[k] * before[REACH + x - k]
                if x + k >= xs:
                    total = total + COEF[k] * after[x + k - xs]
            more = vw[x, rows, lanes] + (live * p[i, x, :, lanes]) * total
            here = w[x, rows, lanes] + live * more
            image[i, x, :, lanes] = partial[x, rows, lanes] + here * drive[x, rows, lanes]

    each_block(w, work)


def products_kernel(pairs, *refs):
    out = refs[-1]

    def work(i, y0, h, lanes):
        rows = pl.ds(y0, SUB)
        for x in range(out.shape[0]):
            total = refs[0][x, rows, lanes] * refs[1][x, rows, lanes]
            for j in range(1, pairs):
                total = total + refs[2 * j][x, rows, lanes] * refs[2 * j + 1][x, rows, lanes]
            out[x, rows, lanes] = total

    each_block(out, work)


def split_kernel(spot, courant, u, w, parts, inner, outer, swap, keep, slab_in, sides, sems):
    zs = parts.shape[0]
    _, tile_x, slab, _ = slab_in.shape
    planes = tile_x // QUAD
    me_shot, me_z, me_q = spot[0], spot[1], spot[2]
    rows = pl.ds(pl.multiple_of(me_shot * slab, SUB), slab)
    first = jnp.where(me_q % 2 == 0, tile_x - REACH, 0)
    loads = []
    for side in range(2):
        x0 = first if side == 0 else tile_x - REACH - first
        for k, field in enumerate((u, w)):
            loads.append(
                pltpu.make_async_copy(
                    field.at[pl.ds(x0, REACH)],
                    sides.at[side, pl.ds(k * REACH, REACH)],
                    sems.at[2 * side + k],
                )
            )
    loads.append(pltpu.make_async_copy(courant.at[:, :, rows, :], slab_in, sems.at[4]))
    for load in loads:
        load.start()
    stores = []
    for side, out in enumerate((inner, outer)):
        loads[2 * side].wait()
        loads[2 * side + 1].wait()
        stores.append(pltpu.make_async_copy(sides.at[side], out, sems.at[5 + side]))
        stores[-1].start()
    loads[4].wait()
    for z in range(zs):
        row = jnp.where(z <= me_z, 0, 1)
        stores.append(pltpu.make_async_copy(slab_in.at[row], parts.at[z], sems.at[7 + z]))
        stores[-1].start()
    for k, turn in enumerate((0, 2)):
        keep[k] = slab_in[1, pl.ds((me_q ^ turn) * planes, planes)]
        swap[k] = slab_in[1, pl.ds((me_q ^ turn ^ 1) * planes, planes)]
    for store in stores:
        store.wait()


def relay_kernel(keep, swapped, out):
    out[0] = keep[1]
    out[1] = swapped[1]


def gather_kernel(zs, table, line, keep, swapped, far, sent, sems):
    slots = sent.shape[0]
    me_z, me_q = table[table.shape[0] - 2], table[table.shape[0] - 1]

    def one(slot, carry):
        tile = table[slot // QUAD] + slot % QUAD
        place = ((me_z + tile // QUAD) % zs) * QUAD + tile % QUAD
        turn = me_q ^ (tile % QUAD)

        def send(source):
            pltpu.make_async_copy(source, sent.at[slot], sems.at[slot]).start()

        @pl.when(tile < zs * QUAD)
        def _():
            send(line.at[place])

        @pl.when(tile >= zs * QUAD)
        def _():
            @pl.when(turn == 0)
            def _():
                send(keep.at[0])

            @pl.when(turn == 1)
            def _():
                send(swapped.at[0])

            @pl.when(turn > 1)
            def _():
                send(far.at[turn - 2])

        return carry

    lax.fori_loop(0, slots, one, 0)

    def done(slot, carry):
        pltpu.make_async_copy(line.at[0], sent.at[slot], sems.at[slot]).wait()
        return carry

    lax.fori_loop(0, slots, done, 0)


def scatter_kernel(zs, table, got, line, keep, swap, held, sems):
    me_z, me_q = table[table.shape[0] - 2], table[table.shape[0] - 1]
    held[...] = jnp.zeros_like(held)

    def one(s, carry):
        place = pl.ds(table[s], QUAD)
        held[place] = held[place] + got[pl.ds(s * QUAD, QUAD)]
        return carry

    lax.fori_loop(0, got.shape[0] // QUAD, one, 0)
    copies = []
    for j in range(zs):
        to = ((me_z + j) % zs) * QUAD
        copies.append(
            pltpu.make_async_copy(
                held.at[pl.ds(j * QUAD, QUAD)], line.at[pl.ds(to, QUAD)], sems.at[j]
            )
        )
        copies[-1].start()
    for k, turn in enumerate((0, 2)):
        keep[k] = held[zs * QUAD + (me_q ^ turn)]
        swap[k] = held[zs * QUAD + (me_q ^ turn ^ 1)]
    for copy in copies:
        copy.wait()


def finish_kernel(zs, table, came, keep, swapped, far, out):
    planes = came.shape[1]
    me_z, me_q = table[table.shape[0] - 2], table[table.shape[0] - 1]
    extras = (keep[0], swapped[0], far[0], far[1])
    for turn in range(QUAD):
        q = me_q ^ turn
        low = came[q]
        high = extras[turn]
        for z in range(1, zs):
            value = came[z * QUAD + q]
            low = low + jnp.where(z <= me_z, value, 0.0)
            high = high + jnp.where(z <= me_z, 0.0, value)
        out[0, pl.ds(q * planes, planes)] = low
        out[1, pl.ds(q * planes, planes)] = high


def exchange(parts, axes):
    return lax.all_to_all(parts, axes, split_axis=0, concat_axis=0, tiled=True)


def swap_quads(value, turn):
    return lax.ppermute(value, "quad", [(q, q ^ turn) for q in range(QUAD)])


def quad_relay(keep, swap):
    swapped = swap_quads(swap, 1)
    (far,) = local_kernel(relay_kernel, [], [keep, swapped], [f32(*keep.shape)])
    return keep, swapped, swap_quads(far, 2)


def open_moves(courant, u, w, spot):
    rows, tile_x, ny, nz = courant.shape
    zs = lax.axis_size("zz")
    slab = ny // lax.axis_size("shot")
    planes = tile_x // QUAD
    hbm = pl.BlockSpec(memory_space=pltpu.HBM)
    vmem = pl.BlockSpec(memory_space=pltpu.VMEM)
    parts, inner, outer, swap, keep = pl.pallas_call(
        split_kernel,
        out_shape=[hbm32(zs, tile_x, slab, nz)]
        + [hbm32(2 * REACH, ny, nz)] * 2
        + [f32(2, planes, slab, nz)] * 2,
        in_specs=[pl.BlockSpec(memory_space=pltpu.SMEM), hbm, hbm, hbm],
        out_specs=[hbm, hbm, hbm, vmem, vmem],
        scratch_shapes=[
            pltpu.VMEM((rows, tile_x, slab, nz), jnp.float32),
            pltpu.VMEM((2, 2 * REACH, ny, nz), jnp.float32),
            pltpu.SemaphoreType.DMA((zs + 7,)),
        ],
        compiler_params=pltpu.CompilerParams(vmem_limit_bytes=VMEM_LIMIT),
        name="split",
    )(spot, in_hbm(courant), in_hbm(u), in_hbm(w))
    return parts.reshape(zs * QUAD, planes, slab, nz), inner, outer, keep, swap


def model_parts(line, extras, table):
    slots = lax.axis_size("shot") * QUAD
    smem = pl.BlockSpec(memory_space=pltpu.SMEM)
    anywhere = pl.BlockSpec(memory_space=pl.ANY)
    return pl.pallas_call(
        functools.partial(gather_kernel, lax.axis_size("zz")),
        out_shape=hbm32(slots, *line.shape[1:]),
        in_specs=[smem] + [anywhere] * 4,
        out_specs=pl.BlockSpec(memory_space=pltpu.HBM),
        scratch_shapes=[pltpu.SemaphoreType.DMA((slots,))],
        compiler_params=pltpu.CompilerParams(vmem_limit_bytes=1 << 20),
        name="gather",
    )(table, line, *extras)


def return_image(image, table):
    shots, tile_x, slab, nz = image.shape
    zs = lax.axis_size("zz")
    planes = tile_x // QUAD
    got = exchange(image.reshape(shots * QUAD, planes, slab, nz), PLANE)
    smem = pl.BlockSpec(memory_space=pltpu.SMEM)
    vmem = pl.BlockSpec(memory_space=pltpu.VMEM)
    line, keep, swap = pl.pallas_call(
        functools.partial(scatter_kernel, zs),
        out_shape=[hbm32(zs * QUAD, planes, slab, nz)] + [f32(2, planes, slab, nz)] * 2,
        in_specs=[smem, vmem],
        out_specs=[pl.BlockSpec(memory_space=pltpu.HBM), vmem, vmem],
        scratch_shapes=[
            pltpu.VMEM(((zs + 1) * QUAD, planes, slab, nz), jnp.float32),
            pltpu.SemaphoreType.DMA((zs,)),
        ],
        compiler_params=pltpu.CompilerParams(vmem_limit_bytes=VMEM_LIMIT),
        name="scatter",
    )(table, got)
    came = exchange(line, MP)
    extras = quad_relay(keep, swap)
    (out,) = local_kernel(
        functools.partial(finish_kernel, zs), [table], [came, *extras], [f32(2, tile_x, slab, nz)]
    )
    return out


def edges(n, scalars, now, back, drive, speed):
    _, ny, nz = now.shape
    hbm = pl.BlockSpec(memory_space=pltpu.HBM)
    vmem = pl.BlockSpec(memory_space=pltpu.VMEM)
    return pl.pallas_call(
        functools.partial(edges_kernel, n),
        out_shape=[f32(REACH, ny, nz)] * 2,
        in_specs=[pl.BlockSpec(memory_space=pltpu.SMEM), hbm, hbm, hbm, vmem],
        out_specs=[vmem] * 2,
        scratch_shapes=[
            pltpu.VMEM((3, 2, REACH, ny, nz), jnp.float32),
            pltpu.SemaphoreType.DMA((3, 2)),
        ],
        compiler_params=pltpu.CompilerParams(vmem_limit_bytes=VMEM_LIMIT),
    )(scalars, in_hbm(now), in_hbm(back), in_hbm(drive), speed)


def halos(inner, outer):
    count = lax.axis_size(MP)
    pairs = [(i, i + 1) for i in range(1, count - 1, 2)]
    far = lax.ppermute(outer, MP, pairs + [(j, i) for i, j in pairs])
    near = lax.ppermute(inner, MP, [(i, i ^ 1) for i in range(count)])
    return near, far


def window(
    courant,
    aperture_first,
    source_pos,
    wavelet,
    receiver_pos,
    residual,
    step_count,
    forward_prev,
    forward_now,
    adjoint_prev,
    adjoint_now,
):
    tile_x, ny, nz = forward_now.shape[1:]
    steps = wavelet.shape[1]
    receivers = receiver_pos.shape[1]
    spot = [lax.axis_index(name) for name in ("shot", "zz", "quad")]
    spot = jnp.stack(spot).astype(jnp.int32)
    u, w = forward_now[0], adjoint_now[0]
    parts, inner, outer, keep, swap = open_moves(courant, u, w, spot)
    sides = halos(inner, outer)
    line = exchange(parts, MP)
    extras = quad_relay(keep, swap)
    table = jnp.concatenate([all_first(aperture_first[0]), spot])
    me_index = lax.axis_index(MP)
    even = me_index % 2 == 0
    base = (me_index * tile_x).reshape(1).astype(jnp.int32)
    spots = receiver_pos[0]
    cells = (spots[:, 0] * ny + spots[:, 1]) * nz + spots[:, 2]
    scalars = jnp.concatenate(
        [
            step_count.astype(jnp.float32),
            base.astype(jnp.float32),
            even.reshape(1).astype(jnp.float32),
            source_pos[0].astype(jnp.float32),
            cells.astype(jnp.float32),
            wavelet[0],
            residual[0].reshape(-1),
        ]
    )
    field = f32(tile_x, ny, nz)
    edge = f32(REACH, ny, nz)
    padded = pltpu.VMEM((nz // LANES, tile_x, ny + 2 * SUB, LANES), jnp.float32)
    along = pltpu.VMEM((tile_x, ny, nz), jnp.float32)
    drives = []
    hbm = pl.BlockSpec(memory_space=pltpu.HBM)
    vmem = pl.BlockSpec(memory_space=pltpu.VMEM)
    smem = pl.BlockSpec(memory_space=pltpu.SMEM)
    drive, push = pl.pallas_call(
        functools.partial(first_kernel, steps, receivers),
        out_shape=[hbm32(tile_x, ny, nz)] * 2,
        in_specs=[smem] + [vmem] * 4,
        out_specs=[hbm, hbm],
        scratch_shapes=[along, along, padded, pltpu.SemaphoreType.DMA((2,))],
        compiler_params=pltpu.CompilerParams(vmem_limit_bytes=VMEM_LIMIT),
        name="first",
    )(scalars, u, w, *sides)
    sent = model_parts(line, extras, table)
    sent, drive, push = lax.optimization_barrier((sent, drive, push))
    owned = exchange(sent, PLANE).reshape(-1, tile_x, SUB, nz)
    drives.append(drive)
    u_sides = halos(*edges(0, scalars, u, forward_prev[0], drive, owned))
    w_sides = halos(*edges(steps - 1, scalars, w, adjoint_prev[0], push, owned))
    backs = []
    for n in range(1, steps):
        last = n == steps - 1
        state = [u, forward_prev[0], drive] if n == 1 else [u, vu]
        drive, *moved = local_kernel(
            functools.partial(forward_kernel, receivers, n, last),
            [scalars],
            [*state, owned, *u_sides],
            [field] if last else [field, field, field, edge, edge],
            [padded, along],
        )
        drives.append(drive)
        if not last:
            u, vu, inner, outer = moved
            u_sides = halos(inner, outer)
        if last:
            break
        state = [w, adjoint_prev[0], push] if n == 1 else [w, vw]
        outs = [field, field, edge, edge]
        if n == 1:
            outs = [field] + outs
        *opened, w, vw, inner, outer = local_kernel(
            functools.partial(adjoint_kernel, steps, receivers, steps - 1 - n),
            [scalars],
            [*state, owned, *w_sides],
            outs,
            [padded, along],
        )
        w_sides = halos(inner, outer)
        backs += [*opened, w]
    pairs = []
    for k in range(steps - 1):
        pairs += [backs[k], drives[steps - 1 - k]]
    (partial,) = local_kernel(functools.partial(products_kernel, steps - 1), [], pairs, [field])
    state = [w, vw, owned, partial, drives[0]]
    whole = f32(ny // SUB, tile_x, SUB, nz)
    image, open_sum = local_kernel(
        functools.partial(last_inner_kernel, steps, receivers),
        [scalars],
        state,
        [whole, f32(2 * REACH, ny, nz)],
        [padded, along],
    )
    (image,) = local_kernel(
        last_outer_kernel, [scalars], [*state, open_sum, *w_sides, image], [whole], aliases={9: 0}
    )
    return return_image(image, table)


def solution(mesh):
    shots, mp = mesh.devices.shape
    fine = Mesh(mesh.devices.reshape(shots, mp // QUAD, QUAD), ("shot", "zz", "quad"))
    return jax.shard_map(
        window,
        mesh=fine,
        in_specs=(
            P(None, MP, None, None),
            P("shot"),
            P("shot", None),
            P("shot", None),
            P("shot", None, None),
            P("shot", None, None),
            P("shot"),
            P("shot", MP, None, None),
            P("shot", MP, None, None),
            P("shot", MP, None, None),
            P("shot", MP, None, None),
        ),
        out_specs=P(None, MP, "shot", None),
        check_vma=False,
    )
```

```python
import functools

import jax
import jax.numpy as jnp
from jax import lax
from jax.experimental import pallas as pl
from jax.experimental.pallas import tpu as pltpu
from jax.sharding import Mesh, PartitionSpec as P


COEF = (-205.0 / 72.0, 1.6, -0.2, 8.0 / 315.0, -1.0 / 560.0)
WHOLE = (8064.0, -1008.0, 128.0, -9.0)
SCALE = 5040.0
QUAD = 4
MP = ("zz", "quad")
PLANE = ("shot", "quad")
LANES = 128
SUB = 8
REACH = 4
COUNT, BASE, EVEN, SOURCE, RECEIVERS = 0, 1, 2, 3, 6
NEAR = 12
VMEM_LIMIT = 16 << 20


def all_first(first):
    shots = lax.axis_size("shot")
    me = lax.axis_index("shot")
    known = jnp.where(jnp.arange(shots, dtype=jnp.int32) == me, first, 0)
    step = 1
    while step < shots:
        known = known + lax.ppermute(known, "shot", [(i, i ^ step) for i in range(shots)])
        step *= 2
    return known


def f32(*shape):
    return jax.ShapeDtypeStruct(shape, jnp.float32)


def hbm32(*shape):
    return pltpu.HBM(shape, jnp.float32)


def local_kernel(body, scalars, arrays, outs, scratch=(), aliases=None):
    vmem = pl.BlockSpec(memory_space=pltpu.VMEM)
    smem = pl.BlockSpec(memory_space=pltpu.SMEM)
    return pl.pallas_call(
        body,
        out_shape=outs,
        in_specs=[smem] * len(scalars) + [vmem] * len(arrays),
        out_specs=[vmem] * len(outs),
        scratch_shapes=list(scratch),
        input_output_aliases=aliases or {},
        compiler_params=pltpu.CompilerParams(vmem_limit_bytes=VMEM_LIMIT),
    )(*scalars, *arrays)


def in_hbm(value):
    return pltpu.with_memory_space_constraint(value, pltpu.HBM)


def band_matrix(nz):
    rows = lax.broadcasted_iota(jnp.int32, (nz, nz), 0)
    cols = lax.broadcasted_iota(jnp.int32, (nz, nz), 1)
    apart = jnp.abs(rows - cols)
    band = jnp.zeros((nz, nz), jnp.float32)
    for k in range(1, REACH + 1):
        band = jnp.where(apart == k, WHOLE[k - 1], band)
    return band.astype(jnp.bfloat16)


def prepare(field, padded, along_z):
    xs, ys, nz = field.shape
    band = band_matrix(nz)

    def times_band(part):
        return jnp.dot(part, band, preferred_element_type=jnp.float32)

    for x in range(0, xs, REACH):
        value = field[x : x + REACH].reshape(REACH * ys, nz)
        high = value.astype(jnp.bfloat16)
        rest = value - high.astype(jnp.float32)
        middle = rest.astype(jnp.bfloat16)
        low = (rest - middle.astype(jnp.float32)).astype(jnp.bfloat16)
        total = (times_band(low) + times_band(middle)) + times_band(high)
        total = total * (1.0 / SCALE) + (3.0 * COEF[0]) * value
        along_z[x : x + REACH] = total.reshape(REACH, ys, nz)
    edge = jnp.zeros((xs, SUB, LANES), jnp.float32)
    for h in range(nz // LANES):
        padded[h, :, 0:SUB, :] = edge
        padded[h, :, SUB + ys : SUB + ys + SUB, :] = edge
        padded[h, :, SUB : SUB + ys, :] = field[:, :, h * LANES : (h + 1) * LANES]


def add_point(target, x, y, z, amount):
    xs, _, nz = target.shape

    @pl.when((x >= 0) & (x < xs))
    def _():
        cells = lax.broadcasted_iota(jnp.int32, (1, 1, nz), 2)
        place = (pl.ds(x, 1), pl.ds(y, 1), slice(None))
        target[place] = target[place] + jnp.where(cells == z, amount, 0.0)


def whole(scalars, at):
    return scalars[at].astype(jnp.int32)


def is_even(scalars):
    return scalars[EVEN] > 0.5


def add_source(target, receivers, scalars, n):
    x = whole(scalars, SOURCE) - whole(scalars, BASE)
    amount = scalars[RECEIVERS + receivers + n]
    add_point(target, x, whole(scalars, SOURCE + 1), whole(scalars, SOURCE + 2), amount)


def add_receivers(target, scalars, steps, receivers, n):
    xs, ys, nz = target.shape
    base = whole(scalars, BASE)
    away = whole(scalars, SOURCE) - base
    amounts = RECEIVERS + receivers + steps + n * receivers
    z_bits = nz.bit_length() - 1
    x_bits = z_bits + ys.bit_length() - 1

    @pl.when((away + NEAR >= 0) & (away - NEAR < xs))
    def _():
        def one(j, carry):
            cell = whole(scalars, RECEIVERS + j)
            x, y = (cell >> x_bits) - base, (cell >> z_bits) & (ys - 1)
            add_point(target, x, y, cell & (nz - 1), scalars[amounts + j])
            return carry

        lax.fori_loop(0, receivers, one, 0)


def laplacian(padded, along_z, even, inner, outer, y0, h, plane=0):
    xs = along_z.shape[0]
    rows = pl.ds(y0, SUB)
    lanes = slice(h * LANES, (h + 1) * LANES)
    if inner is None:
        before = after = [None] * REACH
    else:
        near = [inner[plane + j, rows, lanes] for j in range(REACH)]
        far = [outer[plane + j, rows, lanes] for j in range(REACH)]
        before = [jnp.where(even, far[j], near[j]) for j in range(REACH)]
        after = [jnp.where(even, near[j], far[j]) for j in range(REACH)]
    column = before + [padded[h, x, pl.ds(y0 + SUB, SUB), :] for x in range(xs)] + after
    for x in range(xs):
        total = along_z[x, rows, lanes]
        for k in range(1, REACH + 1):
            pair = (
                padded[h, x, pl.ds(y0 + SUB + k, SUB), :]
                + padded[h, x, pl.ds(y0 + SUB - k, SUB), :]
            )
            for other in (column[x + REACH + k], column[x + REACH - k]):
                if other is not None:
                    pair = pair + other
            total = total + COEF[k] * pair
        yield x, column[x + REACH], total


def each_block(field, work):
    _, ys, nz = field.shape

    def step(i, carry):
        y0 = pl.multiple_of(i * SUB, SUB)
        for h in range(nz // LANES):
            work(i, y0, h, slice(h * LANES, (h + 1) * LANES))
        return carry

    lax.fori_loop(0, ys // SUB, step, 0)


def switch_on(scalars, n):
    return jnp.where(scalars[COUNT] > n + 0.5, 1.0, 0.0).astype(jnp.float32)


def first_kernel(steps, receivers, scalars, u, w, near, far, d, e, along_u, along_w, pad, sems):
    even = is_even(scalars)
    copies = []
    for k, (field, along, out) in enumerate(((u, along_u, d), (w, along_w, e))):
        prepare(field, pad, along)
        if k == 0:
            add_source(along, receivers, scalars, 0)
            live = switch_on(scalars, 0)
        else:
            add_receivers(along, scalars, steps, receivers, steps - 1)
            live = switch_on(scalars, steps - 1)

        def work(i, y0, h, lanes):
            rows = pl.ds(y0, SUB)
            for x, _, total in laplacian(pad, along, even, near, far, y0, h, k * REACH):
                along[x, rows, lanes] = live * total

        each_block(field, work)
        copy = pltpu.make_async_copy(along, out, sems.at[k])
        copy.start()
        copies.append(copy)
    for copy in copies:
        copy.wait()


def edge_out(even, field, inner, outer):
    xs = field.shape[0]

    @pl.when(even)
    def _():
        inner[...] = field[xs - REACH :]
        outer[...] = field[:REACH]

    @pl.when(jnp.logical_not(even))
    def _():
        inner[...] = field[:REACH]
        outer[...] = field[xs - REACH :]


def edges_kernel(n, scalars, now, back, drive, speed, inner, outer, held, sems):
    xs, ys, _ = now.shape
    even = is_even(scalars)
    live = switch_on(scalars, n)
    starts = (0, xs - REACH)
    copies = [
        pltpu.make_async_copy(source.at[pl.ds(x0, REACH)], held.at[k, side], sems.at[k, side])
        for side, x0 in enumerate(starts)
        for k, source in enumerate((now, back, drive))
    ]
    for copy in copies:
        copy.start()
    for side, x0 in enumerate(starts):
        for copy in copies[3 * side : 3 * side + 3]:
            copy.wait()
        ahead = even if side == 1 else jnp.logical_not(even)

        def update(out):
            def step(i, carry):
                rows = pl.ds(pl.multiple_of(i * SUB, SUB), SUB)
                for j in range(REACH):
                    here = held[0, side, j, rows, :]
                    more = (here - held[1, side, j, rows, :]) + speed[i, x0 + j] * held[
                        2, side, j, rows, :
                    ]
                    out[j, rows, :] = here + live * more
                return carry

            lax.fori_loop(0, ys // SUB, step, 0)

        @pl.when(ahead)
        def _():
            update(inner)

        @pl.when(jnp.logical_not(ahead))
        def _():
            update(outer)


def opening(scalars, n, now, back, drive, speed, new, gain):
    live = switch_on(scalars, n)

    def work(i, y0, h, lanes):
        rows = pl.ds(y0, SUB)
        for x in range(now.shape[0]):
            here = now[x, rows, lanes]
            more = (here - back[x, rows, lanes]) + speed[i, x, :, lanes] * drive[x, rows, lanes]
            gain[x, rows, lanes] = more
            new[x, rows, lanes] = here + live * more

    each_block(now, work)


def forward_kernel(receivers, n, last, scalars, *refs):
    if n == 1:
        u0, back, drive0, p, near, far, drive, new, gain, inner, outer, pad, along = refs
        opening(scalars, 0, u0, back, drive0, p, new, gain)
        u, vu = new, gain
    elif last:
        u, vu, p, near, far, drive, pad, along = refs
    else:
        u, vu, p, near, far, drive, new, gain, inner, outer, pad, along = refs
    prepare(u, pad, along)
    add_source(along, receivers, scalars, n)
    live = switch_on(scalars, n)
    even = is_even(scalars)

    def work(i, y0, h, lanes):
        rows = pl.ds(y0, SUB)
        for x, here, total in laplacian(pad, along, even, near, far, y0, h):
            total = live * total
            drive[x, rows, lanes] = total
            if last:
                continue
            more = vu[x, rows, lanes] + p[i, x, :, lanes] * total
            gain[x, rows, lanes] = more
            new[x, rows, lanes] = here + more

    each_block(u, work)
    if not last:
        edge_out(even, new, inner, outer)


def adjoint_kernel(steps, receivers, n, scalars, *refs):
    if n == steps - 2:
        w0, back, push, p, near, far, w, new, gain, inner, outer, pad, along = refs
        opening(scalars, steps - 1, w0, back, push, p, w, gain)
        vw = gain
    else:
        w, vw, p, near, far, new, gain, inner, outer, pad, along = refs
    prepare(w, pad, along)
    add_receivers(along, scalars, steps, receivers, n)
    live = switch_on(scalars, n)
    even = is_even(scalars)

    def work(i, y0, h, lanes):
        rows = pl.ds(y0, SUB)
        for x, here, total in laplacian(pad, along, even, near, far, y0, h):
            more = vw[x, rows, lanes] + (live * p[i, x, :, lanes]) * total
            gain[x, rows, lanes] = more
            new[x, rows, lanes] = here + live * more

    each_block(w, work)
    edge_out(even, new, inner, outer)


def last_inner_kernel(steps, receivers, scalars, w, vw, p, partial, drive, image, open_sum, pad, along):
    xs = w.shape[0]
    prepare(w, pad, along)
    add_receivers(along, scalars, steps, receivers, 0)
    live = switch_on(scalars, 0)

    def work(i, y0, h, lanes):
        rows = pl.ds(y0, SUB)
        for x, here, total in laplacian(pad, along, None, None, None, y0, h):
            if x < REACH or x >= xs - REACH:
                open_sum[x if x < REACH else x + 2 * REACH - xs, rows, lanes] = total
                continue
            more = vw[x, rows, lanes] + (live * p[i, x, :, lanes]) * total
            here = here + live * more
            image[i, x, :, lanes] = partial[x, rows, lanes] + here * drive[x, rows, lanes]

    each_block(w, work)


def last_outer_kernel(scalars, w, vw, p, partial, drive, open_sum, near, far, inside, image):
    del inside
    xs = w.shape[0]
    live = switch_on(scalars, 0)
    even = is_even(scalars)

    def work(i, y0, h, lanes):
        rows = pl.ds(y0, SUB)
        a = [near[j, rows, lanes] for j in range(REACH)]
        b = [far[j, rows, lanes] for j in range(REACH)]
        before = [jnp.where(even, b[j], a[j]) for j in range(REACH)]
        after = [jnp.where(even, a[j], b[j]) for j in range(REACH)]
        for side in range(2 * REACH):
            x = side if side < REACH else side + xs - 2 * REACH
            total = open_sum[side, rows, lanes]
            for k in range(1, REACH + 1):
                if x - k < 0:
                    total = total + COEF[k] * before[REACH + x - k]
                if x + k >= xs:
                    total = total + COEF[k] * after[x + k - xs]
            more = vw[x, rows, lanes] + (live * p[i, x, :, lanes]) * total
            here = w[x, rows, lanes] + live * more
            image[i, x, :, lanes] = partial[x, rows, lanes] + here * drive[x, rows, lanes]

    each_block(w, work)


def products_kernel(pairs, *refs):
    out = refs[-1]

    def work(i, y0, h, lanes):
        rows = pl.ds(y0, SUB)
        for x in range(out.shape[0]):
            total = refs[0][x, rows, lanes] * refs[1][x, rows, lanes]
            for j in range(1, pairs):
                total = total + refs[2 * j][x, rows, lanes] * refs[2 * j + 1][x, rows, lanes]
            out[x, rows, lanes] = total

    each_block(out, work)


def split_kernel(spot, courant, u, w, parts, inner, outer, swap, keep, slab_in, sides, sems):
    zs = parts.shape[0]
    _, tile_x, slab, _ = slab_in.shape
    planes = tile_x // QUAD
    me_shot, me_z, me_q = spot[0], spot[1], spot[2]
    rows = pl.ds(pl.multiple_of(me_shot * slab, SUB), slab)
    first = jnp.where(me_q % 2 == 0, tile_x - REACH, 0)
    loads = []
    for side in range(2):
        x0 = first if side == 0 else tile_x - REACH - first
        for k, field in enumerate((u, w)):
            loads.append(
                pltpu.make_async_copy(
                    field.at[pl.ds(x0, REACH)],
                    sides.at[side, pl.ds(k * REACH, REACH)],
                    sems.at[2 * side + k],
                )
            )
    loads.append(pltpu.make_async_copy(courant.at[:, :, rows, :], slab_in, sems.at[4]))
    for load in loads:
        load.start()
    stores = []
    for side, out in enumerate((inner, outer)):
        loads[2 * side].wait()
        loads[2 * side + 1].wait()
        stores.append(pltpu.make_async_copy(sides.at[side], out, sems.at[5 + side]))
        stores[-1].start()
    loads[4].wait()
    for z in range(zs):
        row = jnp.where(z <= me_z, 0, 1)
        stores.append(pltpu.make_async_copy(slab_in.at[row], parts.at[z], sems.at[7 + z]))
        stores[-1].start()
    for k, turn in enumerate((0, 2)):
        keep[k] = slab_in[1, pl.ds((me_q ^ turn) * planes, planes)]
        swap[k] = slab_in[1, pl.ds((me_q ^ turn ^ 1) * planes, planes)]
    for store in stores:
        store.wait()


def relay_kernel(keep, swapped, out):
    out[0] = keep[1]
    out[1] = swapped[1]


def gather_kernel(zs, table, line, keep, swapped, far, sent, sems):
    shots = sent.shape[0] // QUAD
    tiles = zs * QUAD
    me_z, me_q = table[table.shape[0] - 2], table[table.shape[0] - 1]

    def one(s, carry):
        first = table[s]
        start = (me_z * QUAD + first) % tiles
        together = (first + QUAD <= tiles) & (start + QUAD <= tiles)

        @pl.when(together)
        def _():
            pltpu.make_async_copy(
                line.at[pl.ds(start, QUAD)], sent.at[pl.ds(s * QUAD, QUAD)], sems.at[s]
            ).start()

        @pl.when(jnp.logical_not(together))
        def _():
            for k in range(QUAD):
                tile = first + k
                turn = me_q ^ (tile % QUAD)

                def send(source):
                    pltpu.make_async_copy(source, sent.at[s * QUAD + k], sems.at[s]).start()

                @pl.when(tile < tiles)
                def _():
                    send(line.at[(start + k) % tiles])

                @pl.when((tile >= tiles) & (turn == 0))
                def _():
                    send(keep.at[0])

                @pl.when((tile >= tiles) & (turn == 1))
                def _():
                    send(swapped.at[0])

                @pl.when((tile >= tiles) & (turn > 1))
                def _():
                    send(far.at[turn - 2])

        return carry

    lax.fori_loop(0, shots, one, 0)

    def done(s, carry):
        pltpu.make_async_copy(
            line.at[pl.ds(0, QUAD)], sent.at[pl.ds(s * QUAD, QUAD)], sems.at[s]
        ).wait()
        return carry

    lax.fori_loop(0, shots, done, 0)


def scatter_kernel(zs, table, got, line, keep, swap, held, sems):
    me_z, me_q = table[table.shape[0] - 2], table[table.shape[0] - 1]
    held[...] = jnp.zeros_like(held)

    def one(s, carry):
        place = pl.ds(table[s], QUAD)
        held[place] = held[place] + got[pl.ds(s * QUAD, QUAD)]
        return carry

    lax.fori_loop(0, got.shape[0] // QUAD, one, 0)
    copies = []
    for j in range(zs):
        to = ((me_z + j) % zs) * QUAD
        copies.append(
            pltpu.make_async_copy(
                held.at[pl.ds(j * QUAD, QUAD)], line.at[pl.ds(to, QUAD)], sems.at[j]
            )
        )
        copies[-1].start()
    for k, turn in enumerate((0, 2)):
        keep[k] = held[zs * QUAD + (me_q ^ turn)]
        swap[k] = held[zs * QUAD + (me_q ^ turn ^ 1)]
    for copy in copies:
        copy.wait()


def finish_kernel(zs, table, came, keep, swapped, far, out):
    planes = came.shape[1]
    me_z, me_q = table[table.shape[0] - 2], table[table.shape[0] - 1]
    extras = (keep[0], swapped[0], far[0], far[1])
    for turn in range(QUAD):
        q = me_q ^ turn
        low = came[q]
        high = extras[turn]
        for z in range(1, zs):
            value = came[z * QUAD + q]
            low = low + jnp.where(z <= me_z, value, 0.0)
            high = high + jnp.where(z <= me_z, 0.0, value)
        out[0, pl.ds(q * planes, planes)] = low
        out[1, pl.ds(q * planes, planes)] = high


def exchange(parts, axes):
    return lax.all_to_all(parts, axes, split_axis=0, concat_axis=0, tiled=True)


def swap_quads(value, turn):
    return lax.ppermute(value, "quad", [(q, q ^ turn) for q in range(QUAD)])


def quad_relay(keep, swap):
    swapped = swap_quads(swap, 1)
    (far,) = local_kernel(relay_kernel, [], [keep, swapped], [f32(*keep.shape)])
    return keep, swapped, swap_quads(far, 2)


def open_moves(courant, u, w, spot):
    rows, tile_x, ny, nz = courant.shape
    zs = lax.axis_size("zz")
    slab = ny // lax.axis_size("shot")
    planes = tile_x // QUAD
    hbm = pl.BlockSpec(memory_space=pltpu.HBM)
    vmem = pl.BlockSpec(memory_space=pltpu.VMEM)
    parts, inner, outer, swap, keep = pl.pallas_call(
        split_kernel,
        out_shape=[hbm32(zs, tile_x, slab, nz)]
        + [hbm32(2 * REACH, ny, nz)] * 2
        + [f32(2, planes, slab, nz)] * 2,
        in_specs=[pl.BlockSpec(memory_space=pltpu.SMEM), hbm, hbm, hbm],
        out_specs=[hbm, hbm, hbm, vmem, vmem],
        scratch_shapes=[
            pltpu.VMEM((rows, tile_x, slab, nz), jnp.float32),
            pltpu.VMEM((2, 2 * REACH, ny, nz), jnp.float32),
            pltpu.SemaphoreType.DMA((zs + 7,)),
        ],
        compiler_params=pltpu.CompilerParams(vmem_limit_bytes=VMEM_LIMIT),
        name="split",
    )(spot, in_hbm(courant), in_hbm(u), in_hbm(w))
    return parts.reshape(zs * QUAD, planes, slab, nz), inner, outer, keep, swap


def model_parts(line, extras, table):
    slots = lax.axis_size("shot") * QUAD
    smem = pl.BlockSpec(memory_space=pltpu.SMEM)
    anywhere = pl.BlockSpec(memory_space=pl.ANY)
    return pl.pallas_call(
        functools.partial(gather_kernel, lax.axis_size("zz")),
        out_shape=hbm32(slots, *line.shape[1:]),
        in_specs=[smem] + [anywhere] * 4,
        out_specs=pl.BlockSpec(memory_space=pltpu.HBM),
        scratch_shapes=[pltpu.SemaphoreType.DMA((slots // QUAD,))],
        compiler_params=pltpu.CompilerParams(vmem_limit_bytes=1 << 20),
        name="gather",
    )(table, line, *extras)


def return_image(image, table):
    shots, tile_x, slab, nz = image.shape
    zs = lax.axis_size("zz")
    planes = tile_x // QUAD
    got = exchange(image.reshape(shots * QUAD, planes, slab, nz), PLANE)
    smem = pl.BlockSpec(memory_space=pltpu.SMEM)
    vmem = pl.BlockSpec(memory_space=pltpu.VMEM)
    line, keep, swap = pl.pallas_call(
        functools.partial(scatter_kernel, zs),
        out_shape=[hbm32(zs * QUAD, planes, slab, nz)] + [f32(2, planes, slab, nz)] * 2,
        in_specs=[smem, vmem],
        out_specs=[pl.BlockSpec(memory_space=pltpu.HBM), vmem, vmem],
        scratch_shapes=[
            pltpu.VMEM(((zs + 1) * QUAD, planes, slab, nz), jnp.float32),
            pltpu.SemaphoreType.DMA((zs,)),
        ],
        compiler_params=pltpu.CompilerParams(vmem_limit_bytes=VMEM_LIMIT),
        name="scatter",
    )(table, got)
    came = exchange(line, MP)
    extras = quad_relay(keep, swap)
    (out,) = local_kernel(
        functools.partial(finish_kernel, zs), [table], [came, *extras], [f32(2, tile_x, slab, nz)]
    )
    return out


def edges(n, scalars, now, back, drive, speed):
    _, ny, nz = now.shape
    hbm = pl.BlockSpec(memory_space=pltpu.HBM)
    vmem = pl.BlockSpec(memory_space=pltpu.VMEM)
    return pl.pallas_call(
        functools.partial(edges_kernel, n),
        out_shape=[f32(REACH, ny, nz)] * 2,
        in_specs=[pl.BlockSpec(memory_space=pltpu.SMEM), hbm, hbm, hbm, vmem],
        out_specs=[vmem] * 2,
        scratch_shapes=[
            pltpu.VMEM((3, 2, REACH, ny, nz), jnp.float32),
            pltpu.SemaphoreType.DMA((3, 2)),
        ],
        compiler_params=pltpu.CompilerParams(vmem_limit_bytes=VMEM_LIMIT),
    )(scalars, in_hbm(now), in_hbm(back), in_hbm(drive), speed)


def halos(inner, outer):
    count = lax.axis_size(MP)
    pairs = [(i, i + 1) for i in range(1, count - 1, 2)]
    far = lax.ppermute(outer, MP, pairs + [(j, i) for i, j in pairs])
    near = lax.ppermute(inner, MP, [(i, i ^ 1) for i in range(count)])
    return near, far


def window(
    courant,
    aperture_first,
    source_pos,
    wavelet,
    receiver_pos,
    residual,
    step_count,
    forward_prev,
    forward_now,
    adjoint_prev,
    adjoint_now,
):
    tile_x, ny, nz = forward_now.shape[1:]
    steps = wavelet.shape[1]
    receivers = receiver_pos.shape[1]
    spot = [lax.axis_index(name) for name in ("shot", "zz", "quad")]
    spot = jnp.stack(spot).astype(jnp.int32)
    u, w = forward_now[0], adjoint_now[0]
    parts, inner, outer, keep, swap = open_moves(courant, u, w, spot)
    sides = halos(inner, outer)
    line = exchange(parts, MP)
    extras = quad_relay(keep, swap)
    table = jnp.concatenate([all_first(aperture_first[0]), spot])
    me_index = lax.axis_index(MP)
    even = me_index % 2 == 0
    base = (me_index * tile_x).reshape(1).astype(jnp.int32)
    spots = receiver_pos[0]
    cells = (spots[:, 0] * ny + spots[:, 1]) * nz + spots[:, 2]
    scalars = jnp.concatenate(
        [
            step_count.astype(jnp.float32),
            base.astype(jnp.float32),
            even.reshape(1).astype(jnp.float32),
            source_pos[0].astype(jnp.float32),
            cells.astype(jnp.float32),
            wavelet[0],
            residual[0].reshape(-1),
        ]
    )
    field = f32(tile_x, ny, nz)
    edge = f32(REACH, ny, nz)
    padded = pltpu.VMEM((nz // LANES, tile_x, ny + 2 * SUB, LANES), jnp.float32)
    along = pltpu.VMEM((tile_x, ny, nz), jnp.float32)
    drives = []
    hbm = pl.BlockSpec(memory_space=pltpu.HBM)
    vmem = pl.BlockSpec(memory_space=pltpu.VMEM)
    smem = pl.BlockSpec(memory_space=pltpu.SMEM)
    drive, push = pl.pallas_call(
        functools.partial(first_kernel, steps, receivers),
        out_shape=[hbm32(tile_x, ny, nz)] * 2,
        in_specs=[smem] + [vmem] * 4,
        out_specs=[hbm, hbm],
        scratch_shapes=[along, along, padded, pltpu.SemaphoreType.DMA((2,))],
        compiler_params=pltpu.CompilerParams(vmem_limit_bytes=VMEM_LIMIT),
        name="first",
    )(scalars, u, w, *sides)
    sent = model_parts(line, extras, table)
    sent, drive, push = lax.optimization_barrier((sent, drive, push))
    owned = exchange(sent, PLANE).reshape(-1, tile_x, SUB, nz)
    drives.append(drive)
    u_sides = halos(*edges(0, scalars, u, forward_prev[0], drive, owned))
    w_sides = halos(*edges(steps - 1, scalars, w, adjoint_prev[0], push, owned))
    backs = []
    for n in range(1, steps):
        last = n == steps - 1
        state = [u, forward_prev[0], drive] if n == 1 else [u, vu]
        drive, *moved = local_kernel(
            functools.partial(forward_kernel, receivers, n, last),
            [scalars],
            [*state, owned, *u_sides],
            [field] if last else [field, field, field, edge, edge],
            [padded, along],
        )
        drives.append(drive)
        if not last:
            u, vu, inner, outer = moved
            u_sides = halos(inner, outer)
        if last:
            break
        state = [w, adjoint_prev[0], push] if n == 1 else [w, vw]
        outs = [field, field, edge, edge]
        if n == 1:
            outs = [field] + outs
        *opened, w, vw, inner, outer = local_kernel(
            functools.partial(adjoint_kernel, steps, receivers, steps - 1 - n),
            [scalars],
            [*state, owned, *w_sides],
            outs,
            [padded, along],
        )
        w_sides = halos(inner, outer)
        backs += [*opened, w]
    pairs = []
    for k in range(steps - 1):
        pairs += [backs[k], drives[steps - 1 - k]]
    (partial,) = local_kernel(functools.partial(products_kernel, steps - 1), [], pairs, [field])
    state = [w, vw, owned, partial, drives[0]]
    whole = f32(ny // SUB, tile_x, SUB, nz)
    image, open_sum = local_kernel(
        functools.partial(last_inner_kernel, steps, receivers),
        [scalars],
        state,
        [whole, f32(2 * REACH, ny, nz)],
        [padded, along],
    )
    (image,) = local_kernel(
        last_outer_kernel, [scalars], [*state, open_sum, *w_sides, image], [whole], aliases={9: 0}
    )
    return return_image(image, table)


def solution(mesh):
    shots, mp = mesh.devices.shape
    fine = Mesh(mesh.devices.reshape(shots, mp // QUAD, QUAD), ("shot", "zz", "quad"))
    return jax.shard_map(
        window,
        mesh=fine,
        in_specs=(
            P(None, MP, None, None),
            P("shot"),
            P("shot", None),
            P("shot", None),
            P("shot", None, None),
            P("shot", None, None),
            P("shot"),
            P("shot", MP, None, None),
            P("shot", MP, None, None),
            P("shot", MP, None, None),
            P("shot", MP, None, None),
        ),
        out_specs=P(None, MP, "shot", None),
        check_vma=False,
    )
```

```python
import functools

import jax
import jax.numpy as jnp
from jax import lax
from jax.experimental import pallas as pl
from jax.experimental.pallas import tpu as pltpu
from jax.sharding import Mesh, PartitionSpec as P


COEF = (-205.0 / 72.0, 1.6, -0.2, 8.0 / 315.0, -1.0 / 560.0)
WHOLE = (8064.0, -1008.0, 128.0, -9.0)
SCALE = 5040.0
QUAD = 4
MP = ("zz", "quad")
PLANE = ("shot", "quad")
LANES = 128
SUB = 8
REACH = 4
COUNT, BASE, EVEN, SOURCE, RECEIVERS = 0, 1, 2, 3, 6
NEAR = 12
VMEM_LIMIT = 16 << 20


def all_first(first):
    shots = lax.axis_size("shot")
    me = lax.axis_index("shot")
    known = jnp.where(jnp.arange(shots, dtype=jnp.int32) == me, first, 0)
    step = 1
    while step < shots:
        known = known + lax.ppermute(known, "shot", [(i, i ^ step) for i in range(shots)])
        step *= 2
    return known


def f32(*shape):
    return jax.ShapeDtypeStruct(shape, jnp.float32)


def hbm32(*shape):
    return pltpu.HBM(shape, jnp.float32)


def local_kernel(body, scalars, arrays, outs, scratch=(), aliases=None):
    vmem = pl.BlockSpec(memory_space=pltpu.VMEM)
    smem = pl.BlockSpec(memory_space=pltpu.SMEM)
    return pl.pallas_call(
        body,
        out_shape=outs,
        in_specs=[smem] * len(scalars) + [vmem] * len(arrays),
        out_specs=[vmem] * len(outs),
        scratch_shapes=list(scratch),
        input_output_aliases=aliases or {},
        compiler_params=pltpu.CompilerParams(vmem_limit_bytes=VMEM_LIMIT),
    )(*scalars, *arrays)


def in_hbm(value):
    return pltpu.with_memory_space_constraint(value, pltpu.HBM)


def band_matrix(nz):
    rows = lax.broadcasted_iota(jnp.int32, (nz, nz), 0)
    cols = lax.broadcasted_iota(jnp.int32, (nz, nz), 1)
    apart = jnp.abs(rows - cols)
    band = jnp.zeros((nz, nz), jnp.float32)
    for k in range(1, REACH + 1):
        band = jnp.where(apart == k, WHOLE[k - 1], band)
    return band.astype(jnp.bfloat16)


def prepare(field, padded, along_z):
    xs, ys, nz = field.shape
    band = band_matrix(nz)

    def times_band(part):
        return jnp.dot(part, band, preferred_element_type=jnp.float32)

    for x in range(0, xs, REACH):
        value = field[x : x + REACH].reshape(REACH * ys, nz)
        high = value.astype(jnp.bfloat16)
        rest = value - high.astype(jnp.float32)
        middle = rest.astype(jnp.bfloat16)
        low = (rest - middle.astype(jnp.float32)).astype(jnp.bfloat16)
        total = (times_band(low) + times_band(middle)) + times_band(high)
        total = total * (1.0 / SCALE) + (3.0 * COEF[0]) * value
        along_z[x : x + REACH] = total.reshape(REACH, ys, nz)
    edge = jnp.zeros((xs, SUB, LANES), jnp.float32)
    for h in range(nz // LANES):
        padded[h, :, 0:SUB, :] = edge
        padded[h, :, SUB + ys : SUB + ys + SUB, :] = edge
        padded[h, :, SUB : SUB + ys, :] = field[:, :, h * LANES : (h + 1) * LANES]


def add_point(target, x, y, z, amount):
    xs, _, nz = target.shape

    @pl.when((x >= 0) & (x < xs))
    def _():
        cells = lax.broadcasted_iota(jnp.int32, (1, 1, nz), 2)
        place = (pl.ds(x, 1), pl.ds(y, 1), slice(None))
        target[place] = target[place] + jnp.where(cells == z, amount, 0.0)


def whole(scalars, at):
    return scalars[at].astype(jnp.int32)


def is_even(scalars):
    return scalars[EVEN] > 0.5


def add_source(target, receivers, scalars, n):
    x = whole(scalars, SOURCE) - whole(scalars, BASE)
    amount = scalars[RECEIVERS + receivers + n]
    add_point(target, x, whole(scalars, SOURCE + 1), whole(scalars, SOURCE + 2), amount)


def add_receivers(target, scalars, steps, receivers, n):
    xs, ys, nz = target.shape
    base = whole(scalars, BASE)
    away = whole(scalars, SOURCE) - base
    amounts = RECEIVERS + receivers + steps + n * receivers
    z_bits = nz.bit_length() - 1
    x_bits = z_bits + ys.bit_length() - 1

    @pl.when((away + NEAR >= 0) & (away - NEAR < xs))
    def _():
        def one(j, carry):
            cell = whole(scalars, RECEIVERS + j)
            x, y = (cell >> x_bits) - base, (cell >> z_bits) & (ys - 1)
            add_point(target, x, y, cell & (nz - 1), scalars[amounts + j])
            return carry

        lax.fori_loop(0, receivers, one, 0)


def laplacian(padded, along_z, even, inner, outer, y0, h, plane=0):
    xs = along_z.shape[0]
    rows = pl.ds(y0, SUB)
    lanes = slice(h * LANES, (h + 1) * LANES)
    if inner is None:
        before = after = [None] * REACH
    else:
        near = [inner[plane + j, rows, lanes] for j in range(REACH)]
        far = [outer[plane + j, rows, lanes] for j in range(REACH)]
        before = [jnp.where(even, far[j], near[j]) for j in range(REACH)]
        after = [jnp.where(even, near[j], far[j]) for j in range(REACH)]
    column = before + [padded[h, x, pl.ds(y0 + SUB, SUB), :] for x in range(xs)] + after
    for x in range(xs):
        total = along_z[x, rows, lanes]
        for k in range(1, REACH + 1):
            pair = (
                padded[h, x, pl.ds(y0 + SUB + k, SUB), :]
                + padded[h, x, pl.ds(y0 + SUB - k, SUB), :]
            )
            for other in (column[x + REACH + k], column[x + REACH - k]):
                if other is not None:
                    pair = pair + other
            total = total + COEF[k] * pair
        yield x, column[x + REACH], total


def each_block(field, work):
    _, ys, nz = field.shape

    def step(i, carry):
        y0 = pl.multiple_of(i * SUB, SUB)
        for h in range(nz // LANES):
            work(i, y0, h, slice(h * LANES, (h + 1) * LANES))
        return carry

    lax.fori_loop(0, ys // SUB, step, 0)


def switch_on(scalars, n):
    return jnp.where(scalars[COUNT] > n + 0.5, 1.0, 0.0).astype(jnp.float32)


def first_kernel(steps, receivers, scalars, u, w, near, far, d, e, along_u, along_w, pad, sems):
    even = is_even(scalars)
    copies = []
    for k, (field, along, out) in enumerate(((u, along_u, d), (w, along_w, e))):
        prepare(field, pad, along)
        if k == 0:
            add_source(along, receivers, scalars, 0)
            live = switch_on(scalars, 0)
        else:
            add_receivers(along, scalars, steps, receivers, steps - 1)
            live = switch_on(scalars, steps - 1)

        def work(i, y0, h, lanes):
            rows = pl.ds(y0, SUB)
            for x, _, total in laplacian(pad, along, even, near, far, y0, h, k * REACH):
                along[x, rows, lanes] = live * total

        each_block(field, work)
        copy = pltpu.make_async_copy(along, out, sems.at[k])
        copy.start()
        copies.append(copy)
    for copy in copies:
        copy.wait()


def edge_out(even, field, inner, outer):
    xs = field.shape[0]

    @pl.when(even)
    def _():
        inner[...] = field[xs - REACH :]
        outer[...] = field[:REACH]

    @pl.when(jnp.logical_not(even))
    def _():
        inner[...] = field[:REACH]
        outer[...] = field[xs - REACH :]


def edges_kernel(n, scalars, now, back, drive, speed, inner, outer, held, sems):
    xs, ys, _ = now.shape
    even = is_even(scalars)
    live = switch_on(scalars, n)
    starts = (0, xs - REACH)
    copies = [
        pltpu.make_async_copy(source.at[pl.ds(x0, REACH)], held.at[k, side], sems.at[k, side])
        for side, x0 in enumerate(starts)
        for k, source in enumerate((now, back, drive))
    ]
    for copy in copies:
        copy.start()
    for side, x0 in enumerate(starts):
        for copy in copies[3 * side : 3 * side + 3]:
            copy.wait()
        ahead = even if side == 1 else jnp.logical_not(even)

        def update(out):
            def step(i, carry):
                rows = pl.ds(pl.multiple_of(i * SUB, SUB), SUB)
                for j in range(REACH):
                    here = held[0, side, j, rows, :]
                    more = (here - held[1, side, j, rows, :]) + speed[i, x0 + j] * held[
                        2, side, j, rows, :
                    ]
                    out[j, rows, :] = here + live * more
                return carry

            lax.fori_loop(0, ys // SUB, step, 0)

        @pl.when(ahead)
        def _():
            update(inner)

        @pl.when(jnp.logical_not(ahead))
        def _():
            update(outer)


def opening(scalars, n, now, back, drive, speed, new, gain):
    live = switch_on(scalars, n)

    def work(i, y0, h, lanes):
        rows = pl.ds(y0, SUB)
        for x in range(now.shape[0]):
            here = now[x, rows, lanes]
            more = (here - back[x, rows, lanes]) + speed[i, x, :, lanes] * drive[x, rows, lanes]
            gain[x, rows, lanes] = more
            new[x, rows, lanes] = here + live * more

    each_block(now, work)


def forward_kernel(receivers, n, last, scalars, *refs):
    if n == 1:
        u0, back, drive0, p, near, far, drive, new, gain, inner, outer, pad, along = refs
        opening(scalars, 0, u0, back, drive0, p, new, gain)
        u, vu = new, gain
    elif last:
        u, vu, p, near, far, drive, pad, along = refs
    else:
        u, vu, p, near, far, drive, new, gain, inner, outer, pad, along = refs
    prepare(u, pad, along)
    add_source(along, receivers, scalars, n)
    live = switch_on(scalars, n)
    even = is_even(scalars)

    def work(i, y0, h, lanes):
        rows = pl.ds(y0, SUB)
        for x, here, total in laplacian(pad, along, even, near, far, y0, h):
            total = live * total
            drive[x, rows, lanes] = total
            if last:
                continue
            more = vu[x, rows, lanes] + p[i, x, :, lanes] * total
            gain[x, rows, lanes] = more
            new[x, rows, lanes] = here + more

    each_block(u, work)
    if not last:
        edge_out(even, new, inner, outer)


def adjoint_kernel(steps, receivers, n, scalars, *refs):
    if n == steps - 2:
        w0, back, push, p, near, far, w, new, gain, inner, outer, pad, along = refs
        opening(scalars, steps - 1, w0, back, push, p, w, gain)
        vw = gain
    else:
        w, vw, p, near, far, new, gain, inner, outer, pad, along = refs
    prepare(w, pad, along)
    add_receivers(along, scalars, steps, receivers, n)
    live = switch_on(scalars, n)
    even = is_even(scalars)

    def work(i, y0, h, lanes):
        rows = pl.ds(y0, SUB)
        for x, here, total in laplacian(pad, along, even, near, far, y0, h):
            more = vw[x, rows, lanes] + (live * p[i, x, :, lanes]) * total
            gain[x, rows, lanes] = more
            new[x, rows, lanes] = here + live * more

    each_block(w, work)
    edge_out(even, new, inner, outer)


def last_inner_kernel(steps, receivers, scalars, w, vw, p, partial, drive, image, open_sum, pad, along):
    xs = w.shape[0]
    prepare(w, pad, along)
    add_receivers(along, scalars, steps, receivers, 0)
    live = switch_on(scalars, 0)

    def work(i, y0, h, lanes):
        rows = pl.ds(y0, SUB)
        for x, here, total in laplacian(pad, along, None, None, None, y0, h):
            if x < REACH or x >= xs - REACH:
                open_sum[x if x < REACH else x + 2 * REACH - xs, rows, lanes] = total
                continue
            more = vw[x, rows, lanes] + (live * p[i, x, :, lanes]) * total
            here = here + live * more
            image[i, x, :, lanes] = partial[x, rows, lanes] + here * drive[x, rows, lanes]

    each_block(w, work)


def last_outer_kernel(scalars, w, vw, p, partial, drive, open_sum, near, far, inside, image):
    del inside
    xs = w.shape[0]
    live = switch_on(scalars, 0)
    even = is_even(scalars)

    def work(i, y0, h, lanes):
        rows = pl.ds(y0, SUB)
        a = [near[j, rows, lanes] for j in range(REACH)]
        b = [far[j, rows, lanes] for j in range(REACH)]
        before = [jnp.where(even, b[j], a[j]) for j in range(REACH)]
        after = [jnp.where(even, a[j], b[j]) for j in range(REACH)]
        for side in range(2 * REACH):
            x = side if side < REACH else side + xs - 2 * REACH
            total = open_sum[side, rows, lanes]
            for k in range(1, REACH + 1):
                if x - k < 0:
                    total = total + COEF[k] * before[REACH + x - k]
                if x + k >= xs:
                    total = total + COEF[k] * after[x + k - xs]
            more = vw[x, rows, lanes] + (live * p[i, x, :, lanes]) * total
            here = w[x, rows, lanes] + live * more
            image[i, x, :, lanes] = partial[x, rows, lanes] + here * drive[x, rows, lanes]

    each_block(w, work)


def products_kernel(pairs, *refs):
    out = refs[-1]

    def work(i, y0, h, lanes):
        rows = pl.ds(y0, SUB)
        for x in range(out.shape[0]):
            total = refs[0][x, rows, lanes] * refs[1][x, rows, lanes]
            for j in range(1, pairs):
                total = total + refs[2 * j][x, rows, lanes] * refs[2 * j + 1][x, rows, lanes]
            out[x, rows, lanes] = total

    each_block(out, work)


def split_kernel(spot, courant, u, w, parts, inner, outer, swap, keep, slab_in, sides, sems):
    zs = parts.shape[0]
    _, tile_x, slab, _ = slab_in.shape
    planes = tile_x // QUAD
    me_shot, me_z, me_q = spot[0], spot[1], spot[2]
    rows = pl.ds(pl.multiple_of(me_shot * slab, SUB), slab)
    first = jnp.where(me_q % 2 == 0, tile_x - REACH, 0)
    load = pltpu.make_async_copy(courant.at[:, :, rows, :], slab_in, sems.at[4])
    load.start()
    loads = []
    for side in range(2):
        x0 = first if side == 0 else tile_x - REACH - first
        for k, field in enumerate((u, w)):
            loads.append(
                pltpu.make_async_copy(
                    field.at[pl.ds(x0, REACH)],
                    sides.at[side, pl.ds(k * REACH, REACH)],
                    sems.at[2 * side + k],
                )
            )
            loads[-1].start()
    load.wait()
    stores = []
    for z in range(zs):
        row = jnp.where(z <= me_z, 0, 1)
        stores.append(pltpu.make_async_copy(slab_in.at[row], parts.at[z], sems.at[7 + z]))
        stores[-1].start()
    for side, out in enumerate((inner, outer)):
        loads[2 * side].wait()
        loads[2 * side + 1].wait()
        stores.append(pltpu.make_async_copy(sides.at[side], out, sems.at[5 + side]))
        stores[-1].start()
    for k, turn in enumerate((0, 2)):
        keep[k] = slab_in[1, pl.ds((me_q ^ turn) * planes, planes)]
        swap[k] = slab_in[1, pl.ds((me_q ^ turn ^ 1) * planes, planes)]
    for store in stores:
        store.wait()


def relay_kernel(keep, swapped, out):
    out[0] = keep[1]
    out[1] = swapped[1]


def gather_kernel(zs, table, line, keep, swapped, far, sent, sems):
    shots = sent.shape[0] // QUAD
    tiles = zs * QUAD
    me_z, me_q = table[table.shape[0] - 2], table[table.shape[0] - 1]

    def one(s, carry):
        first = table[s]
        start = (me_z * QUAD + first) % tiles
        together = (first + QUAD <= tiles) & (start + QUAD <= tiles)

        @pl.when(together)
        def _():
            pltpu.make_async_copy(
                line.at[pl.ds(start, QUAD)], sent.at[pl.ds(s * QUAD, QUAD)], sems.at[s]
            ).start()

        @pl.when(jnp.logical_not(together))
        def _():
            for k in range(QUAD):
                tile = first + k
                turn = me_q ^ (tile % QUAD)

                def send(source):
                    pltpu.make_async_copy(source, sent.at[s * QUAD + k], sems.at[s]).start()

                @pl.when(tile < tiles)
                def _():
                    send(line.at[(start + k) % tiles])

                @pl.when((tile >= tiles) & (turn == 0))
                def _():
                    send(keep.at[0])

                @pl.when((tile >= tiles) & (turn == 1))
                def _():
                    send(swapped.at[0])

                @pl.when((tile >= tiles) & (turn > 1))
                def _():
                    send(far.at[turn - 2])

        return carry

    lax.fori_loop(0, shots, one, 0)

    def done(s, carry):
        pltpu.make_async_copy(
            line.at[pl.ds(0, QUAD)], sent.at[pl.ds(s * QUAD, QUAD)], sems.at[s]
        ).wait()
        return carry

    lax.fori_loop(0, shots, done, 0)


def scatter_kernel(zs, table, got, line, keep, swap, held, sems):
    me_z, me_q = table[table.shape[0] - 2], table[table.shape[0] - 1]
    held[...] = jnp.zeros_like(held)

    def one(s, carry):
        place = pl.ds(table[s], QUAD)
        held[place] = held[place] + got[pl.ds(s * QUAD, QUAD)]
        return carry

    lax.fori_loop(0, got.shape[0] // QUAD, one, 0)
    copies = []
    for j in range(zs):
        to = ((me_z + j) % zs) * QUAD
        copies.append(
            pltpu.make_async_copy(
                held.at[pl.ds(j * QUAD, QUAD)], line.at[pl.ds(to, QUAD)], sems.at[j]
            )
        )
        copies[-1].start()
    for k, turn in enumerate((0, 2)):
        keep[k] = held[zs * QUAD + (me_q ^ turn)]
        swap[k] = held[zs * QUAD + (me_q ^ turn ^ 1)]
    for copy in copies:
        copy.wait()


def finish_kernel(zs, table, came, keep, swapped, far, out):
    planes = came.shape[1]
    me_z, me_q = table[table.shape[0] - 2], table[table.shape[0] - 1]
    extras = (keep[0], swapped[0], far[0], far[1])
    for turn in range(QUAD):
        q = me_q ^ turn
        low = came[q]
        high = extras[turn]
        for z in range(1, zs):
            value = came[z * QUAD + q]
            low = low + jnp.where(z <= me_z, value, 0.0)
            high = high + jnp.where(z <= me_z, 0.0, value)
        out[0, pl.ds(q * planes, planes)] = low
        out[1, pl.ds(q * planes, planes)] = high


def exchange(parts, axes):
    return lax.all_to_all(parts, axes, split_axis=0, concat_axis=0, tiled=True)


def swap_quads(value, turn):
    return lax.ppermute(value, "quad", [(q, q ^ turn) for q in range(QUAD)])


def quad_relay(keep, swap):
    swapped = swap_quads(swap, 1)
    (far,) = local_kernel(relay_kernel, [], [keep, swapped], [f32(*keep.shape)])
    return keep, swapped, swap_quads(far, 2)


def open_moves(courant, u, w, spot):
    rows, tile_x, ny, nz = courant.shape
    zs = lax.axis_size("zz")
    slab = ny // lax.axis_size("shot")
    planes = tile_x // QUAD
    hbm = pl.BlockSpec(memory_space=pltpu.HBM)
    vmem = pl.BlockSpec(memory_space=pltpu.VMEM)
    parts, inner, outer, swap, keep = pl.pallas_call(
        split_kernel,
        out_shape=[hbm32(zs, tile_x, slab, nz)]
        + [hbm32(2 * REACH, ny, nz)] * 2
        + [f32(2, planes, slab, nz)] * 2,
        in_specs=[pl.BlockSpec(memory_space=pltpu.SMEM), hbm, hbm, hbm],
        out_specs=[hbm, hbm, hbm, vmem, vmem],
        scratch_shapes=[
            pltpu.VMEM((rows, tile_x, slab, nz), jnp.float32),
            pltpu.VMEM((2, 2 * REACH, ny, nz), jnp.float32),
            pltpu.SemaphoreType.DMA((zs + 7,)),
        ],
        compiler_params=pltpu.CompilerParams(vmem_limit_bytes=VMEM_LIMIT),
        name="split",
    )(spot, in_hbm(courant), in_hbm(u), in_hbm(w))
    return parts.reshape(zs * QUAD, planes, slab, nz), inner, outer, keep, swap


def model_parts(line, extras, table):
    slots = lax.axis_size("shot") * QUAD
    smem = pl.BlockSpec(memory_space=pltpu.SMEM)
    anywhere = pl.BlockSpec(memory_space=pl.ANY)
    return pl.pallas_call(
        functools.partial(gather_kernel, lax.axis_size("zz")),
        out_shape=hbm32(slots, *line.shape[1:]),
        in_specs=[smem] + [anywhere] * 4,
        out_specs=pl.BlockSpec(memory_space=pltpu.HBM),
        scratch_shapes=[pltpu.SemaphoreType.DMA((slots // QUAD,))],
        compiler_params=pltpu.CompilerParams(vmem_limit_bytes=1 << 20),
        name="gather",
    )(table, line, *extras)


def return_image(image, table):
    shots, tile_x, slab, nz = image.shape
    zs = lax.axis_size("zz")
    planes = tile_x // QUAD
    got = exchange(image.reshape(shots * QUAD, planes, slab, nz), PLANE)
    smem = pl.BlockSpec(memory_space=pltpu.SMEM)
    vmem = pl.BlockSpec(memory_space=pltpu.VMEM)
    line, keep, swap = pl.pallas_call(
        functools.partial(scatter_kernel, zs),
        out_shape=[hbm32(zs * QUAD, planes, slab, nz)] + [f32(2, planes, slab, nz)] * 2,
        in_specs=[smem, vmem],
        out_specs=[pl.BlockSpec(memory_space=pltpu.HBM), vmem, vmem],
        scratch_shapes=[
            pltpu.VMEM(((zs + 1) * QUAD, planes, slab, nz), jnp.float32),
            pltpu.SemaphoreType.DMA((zs,)),
        ],
        compiler_params=pltpu.CompilerParams(vmem_limit_bytes=VMEM_LIMIT),
        name="scatter",
    )(table, got)
    came = exchange(line, MP)
    extras = quad_relay(keep, swap)
    (out,) = local_kernel(
        functools.partial(finish_kernel, zs), [table], [came, *extras], [f32(2, tile_x, slab, nz)]
    )
    return out


def edges(n, scalars, now, back, drive, speed):
    _, ny, nz = now.shape
    hbm = pl.BlockSpec(memory_space=pltpu.HBM)
    vmem = pl.BlockSpec(memory_space=pltpu.VMEM)
    return pl.pallas_call(
        functools.partial(edges_kernel, n),
        out_shape=[f32(REACH, ny, nz)] * 2,
        in_specs=[pl.BlockSpec(memory_space=pltpu.SMEM), hbm, hbm, hbm, vmem],
        out_specs=[vmem] * 2,
        scratch_shapes=[
            pltpu.VMEM((3, 2, REACH, ny, nz), jnp.float32),
            pltpu.SemaphoreType.DMA((3, 2)),
        ],
        compiler_params=pltpu.CompilerParams(vmem_limit_bytes=VMEM_LIMIT),
    )(scalars, in_hbm(now), in_hbm(back), in_hbm(drive), speed)


def halos(inner, outer):
    count = lax.axis_size(MP)
    pairs = [(i, i + 1) for i in range(1, count - 1, 2)]
    far = lax.ppermute(outer, MP, pairs + [(j, i) for i, j in pairs])
    near = lax.ppermute(inner, MP, [(i, i ^ 1) for i in range(count)])
    return near, far


def window(
    courant,
    aperture_first,
    source_pos,
    wavelet,
    receiver_pos,
    residual,
    step_count,
    forward_prev,
    forward_now,
    adjoint_prev,
    adjoint_now,
):
    tile_x, ny, nz = forward_now.shape[1:]
    steps = wavelet.shape[1]
    receivers = receiver_pos.shape[1]
    spot = [lax.axis_index(name) for name in ("shot", "zz", "quad")]
    spot = jnp.stack(spot).astype(jnp.int32)
    u, w = forward_now[0], adjoint_now[0]
    parts, inner, outer, keep, swap = open_moves(courant, u, w, spot)
    sides = halos(inner, outer)
    line = exchange(parts, MP)
    extras = quad_relay(keep, swap)
    table = jnp.concatenate([all_first(aperture_first[0]), spot])
    me_index = lax.axis_index(MP)
    even = me_index % 2 == 0
    base = (me_index * tile_x).reshape(1).astype(jnp.int32)
    spots = receiver_pos[0]
    cells = (spots[:, 0] * ny + spots[:, 1]) * nz + spots[:, 2]
    scalars = jnp.concatenate(
        [
            step_count.astype(jnp.float32),
            base.astype(jnp.float32),
            even.reshape(1).astype(jnp.float32),
            source_pos[0].astype(jnp.float32),
            cells.astype(jnp.float32),
            wavelet[0],
            residual[0].reshape(-1),
        ]
    )
    field = f32(tile_x, ny, nz)
    edge = f32(REACH, ny, nz)
    padded = pltpu.VMEM((nz // LANES, tile_x, ny + 2 * SUB, LANES), jnp.float32)
    along = pltpu.VMEM((tile_x, ny, nz), jnp.float32)
    drives = []
    hbm = pl.BlockSpec(memory_space=pltpu.HBM)
    vmem = pl.BlockSpec(memory_space=pltpu.VMEM)
    smem = pl.BlockSpec(memory_space=pltpu.SMEM)
    drive, push = pl.pallas_call(
        functools.partial(first_kernel, steps, receivers),
        out_shape=[hbm32(tile_x, ny, nz)] * 2,
        in_specs=[smem] + [vmem] * 4,
        out_specs=[hbm, hbm],
        scratch_shapes=[along, along, padded, pltpu.SemaphoreType.DMA((2,))],
        compiler_params=pltpu.CompilerParams(vmem_limit_bytes=VMEM_LIMIT),
        name="first",
    )(scalars, u, w, *sides)
    sent = model_parts(line, extras, table)
    sent, drive, push = lax.optimization_barrier((sent, drive, push))
    owned = exchange(sent, PLANE).reshape(-1, tile_x, SUB, nz)
    drives.append(drive)
    u_sides = halos(*edges(0, scalars, u, forward_prev[0], drive, owned))
    w_sides = halos(*edges(steps - 1, scalars, w, adjoint_prev[0], push, owned))
    backs = []
    for n in range(1, steps):
        last = n == steps - 1
        state = [u, forward_prev[0], drive] if n == 1 else [u, vu]
        drive, *moved = local_kernel(
            functools.partial(forward_kernel, receivers, n, last),
            [scalars],
            [*state, owned, *u_sides],
            [field] if last else [field, field, field, edge, edge],
            [padded, along],
        )
        drives.append(drive)
        if not last:
            u, vu, inner, outer = moved
            u_sides = halos(inner, outer)
        if last:
            break
        state = [w, adjoint_prev[0], push] if n == 1 else [w, vw]
        outs = [field, field, edge, edge]
        if n == 1:
            outs = [field] + outs
        *opened, w, vw, inner, outer = local_kernel(
            functools.partial(adjoint_kernel, steps, receivers, steps - 1 - n),
            [scalars],
            [*state, owned, *w_sides],
            outs,
            [padded, along],
        )
        w_sides = halos(inner, outer)
        backs += [*opened, w]
    pairs = []
    for k in range(steps - 1):
        pairs += [backs[k], drives[steps - 1 - k]]
    (partial,) = local_kernel(functools.partial(products_kernel, steps - 1), [], pairs, [field])
    state = [w, vw, owned, partial, drives[0]]
    whole = f32(ny // SUB, tile_x, SUB, nz)
    image, open_sum = local_kernel(
        functools.partial(last_inner_kernel, steps, receivers),
        [scalars],
        state,
        [whole, f32(2 * REACH, ny, nz)],
        [padded, along],
    )
    (image,) = local_kernel(
        last_outer_kernel, [scalars], [*state, open_sum, *w_sides, image], [whole], aliases={9: 0}
    )
    return return_image(image, table)


def solution(mesh):
    shots, mp = mesh.devices.shape
    fine = Mesh(mesh.devices.reshape(shots, mp // QUAD, QUAD), ("shot", "zz", "quad"))
    return jax.shard_map(
        window,
        mesh=fine,
        in_specs=(
            P(None, MP, None, None),
            P("shot"),
            P("shot", None),
            P("shot", None),
            P("shot", None, None),
            P("shot", None, None),
            P("shot"),
            P("shot", MP, None, None),
            P("shot", MP, None, None),
            P("shot", MP, None, None),
            P("shot", MP, None, None),
        ),
        out_specs=P(None, MP, "shot", None),
        check_vma=False,
    )
```
